32 devices in a mesh: row: 8 (over z, y), col: 4 (over x, core).
Axes of the slice: x: 2, y: 2, z: 4, core: 2. Of those that a mesh axis runs over, the one named last changes fastest.
Arguments:
- tokens: bfloat16 [8192, 2048], P('row', 'col'), may hold values from -6 to 6
- segments: int32 [8, 1024], P('row'), may hold values from 0 to 3, never falling along the last dimension, each value on 1 to 800 neighbouring positions
- gains: float32 [2, 2048], P(None, 'col'), may hold values from 0.5 to 1.5
- shifts: float32 [2, 2048], P(None, 'col'), may hold values from -1.8 to 1.8
- biases: float32 [4, 2048], P(None, 'col'), may hold values from -3 to 3
- mixing: bfloat16 [2048, 3, 2048], P('row', None, 'col'), may hold values from -0.125 to 0.125
- projection: bfloat16 [2048, 2048], P('row', 'col'), may hold values from -0.5 to 0.5
- expand: bfloat16 [2048, 8192], P('row', 'col'), may hold values from -0.125 to 0.125
- thresholds: float32 [8192], P('col'), may hold values from -3 to 3
- contract: bfloat16 [2048, 8192], P('row', 'col'), may hold values from -0.0625 to 0.0625
- cotangent: bfloat16 [8192, 2048], P('row', 'col'), may hold values from -6 to 6
Outputs:
- layer_out: bfloat16 [8192, 2048], P('row', 'col')
- tokens_grad: float32 [8192, 2048], P('row', 'col')
- gains_grad: float32 [2, 2048], P(None, 'col')
- shifts_grad: float32 [2, 2048], P(None, 'col')
- biases_grad: float32 [4, 2048], P(None, 'col')
- mixing_grad: float32 [2048, 3, 2048], P('row', None, 'col')
- projection_grad: float32 [2048, 2048], P('row', 'col')
- expand_grad: float32 [2048, 8192], P('row', 'col')
- thresholds_grad: float32 [8192], P('col')
- contract_grad: float32 [2048, 8192], P('row', 'col')
The draws below stay inside these ranges and needn't reach their ends.
Inputs may be any that keep to these rules, and one draw needn't show every extreme that they name: `segments`: within a sequence the document numbers never fall and every number from 0 to 3 occurs; a document holds at most 800 tokens.
All inputs are finite; a program needn't handle non-finite values.
Results may differ from the reference program's by a relative error of at most 0.0095.
Values may be sent and summed in bfloat16 or wider, within the bound.
No kernel may reach another device: no remote copies, remote signals or barrier semaphores. Data moves between devices by JAX's collectives and lax.ppermute only.
A program may use at most 192 MiB of HBM per device.

```python
import math
import jax
import jax.numpy as jnp
import numpy as np
from jax import lax

D = 2048
H = 32
HD = 64
FF = 8192
SEQ = 1024
SEQS = 8
TOKENS = 8192
DOCS = 4
DOC_MAX = 800


def levels(own_key, extent, shards, least, top_value):
    def one(dim, shards_of):
        draws = jax.random.uniform(jax.random.fold_in(jax.random.fold_in(own_key, 6), dim), (shards_of,), jnp.float32, least / len(shards), top_value / len(shards))
        return jnp.repeat(jnp.exp(draws), extent[dim] // shards_of).reshape((-1,) + (1,) * (len(extent) - dim - 1))

    factor_of = one(*shards[0])
    for cut in shards[1:]:
        factor_of = factor_of * one(*cut)
    return factor_of


def length_profile(amount, total, reach, slope):
    loads = [(1 << 20) // math.isqrt(standing ** slope) + 1 for standing in range(2, amount + 1)]
    spare, given = total - reach - (amount - 1), [1] * (amount - 1)
    while spare > 0:
        candidates = [i for i in range(amount - 1) if given[i] < reach]
        whole, remaining = sum([loads[i] for i in candidates]), spare
        for i in candidates:
            more = min(reach - given[i], max(1, remaining * loads[i] // whole), spare)
            given[i] = given[i] + more
            spare = spare - more
    return np.array([reach] + given)


def ragged(rng, count, total, reach, slope):
    if count == 2:
        one = jax.random.randint(rng, (), max(1, total - reach), min(reach, total - 1) + 1)
        return jnp.stack([one, total - one])
    lengths = jnp.asarray(length_profile(count, total, reach, slope), jnp.int32)
    twos = (count - 1) // 2
    giver, taker = lengths[1:1 + 2 * twos:2], lengths[2:2 + 2 * twos:2]
    slack = jnp.minimum(giver - 1, reach - taker)
    moved = jax.random.randint(jax.random.fold_in(rng, 1), (twos,), 0, 1 << 20) % (slack + 1)
    lengths = lengths.at[1:1 + 2 * twos:2].set(giver - moved).at[2:2 + 2 * twos:2].set(taker + moved)
    return lengths[jax.random.permutation(jax.random.fold_in(rng, 2), count)]


def centred(key, dims, scale, bound, cuts=(), kind=jnp.bfloat16):
    loudness = levels(key, dims, cuts, -0.22, 0.18) if cuts else 1.0
    values = jax.random.normal(key, dims, jnp.float32) * scale * loudness
    return jnp.minimum(jnp.maximum(values, -bound), bound).astype(kind)


def setup_inputs(seed: int = 0) -> dict:
    seeds = jax.random.split(jax.random.key(seed), 12)
    return {
        "tokens": centred(seeds[0], (TOKENS, D), 1.0, 6.0, ((0, 8), (1, 4))),
        "segments": jax.vmap(lambda own: jnp.searchsorted(jnp.cumsum(ragged(own, DOCS, SEQ, DOC_MAX, 2)), jnp.arange(SEQ), side="right"))(jax.random.split(seeds[1], SEQS)).reshape((SEQS, SEQ)).astype(jnp.int32),
        "gains": jnp.clip(1.0 + 0.1 * jax.random.normal(seeds[2], (2, D), jnp.float32), 0.5, 1.5),
        "shifts": centred(seeds[3], (2, D), 0.3, 1.8, ((1, 4),), jnp.float32),
        "biases": centred(seeds[4], (4, D), 0.5, 3.0, ((1, 4),), jnp.float32),
        "mixing": centred(seeds[5], (D, 3, D), D ** -0.5, 0.125, ((0, 8), (2, 4))),
        "projection": centred(seeds[6], (D, D), (D // 16) ** -0.5, 0.5, ((0, 8), (1, 4))),
        "expand": centred(seeds[7], (D, FF), D ** -0.5, 0.125, ((0, 8), (1, 4))),
        "thresholds": centred(seeds[8], (FF,), 0.5, 3.0, ((0, 4),), jnp.float32),
        "contract": centred(seeds[9], (D, FF), FF ** -0.5, 0.0625, ((0, 8), (1, 4))),
        "cotangent": centred(seeds[10], (TOKENS, D), 1.0, 6.0, ((0, 8), (1, 4))),
    }


@jax.custom_vjp
def low(v):
    return lax.optimization_barrier(v.astype(jnp.bfloat16)).astype(jnp.float32)

@jax.custom_vjp
def low_back(v):
    return v

def low_keep(v):
    return (low(v), None)

def low_pass(kept, grad):
    return (grad,)

def back_keep(v):
    return (v, None)

def back_low(kept, grad):
    return (low(grad),)
low.defvjp(low_keep, low_pass)
low_back.defvjp(back_keep, back_low)
precise = lax.Precision.HIGHEST
norm_eps = 1e-05
sqrt_half = 0.7071067811865476
masked_score = -1e+30

def normalize(hidden_rows, gain_row, shift_row):
    row_mean = lax.optimization_barrier(jnp.mean(hidden_rows, axis=-1, keepdims=True))
    spread = lax.optimization_barrier(jnp.mean(hidden_rows * hidden_rows, axis=-1, keepdims=True)) - row_mean * row_mean
    return (hidden_rows - row_mean) * lax.rsqrt(spread + norm_eps) * gain_row + shift_row

def head_attend(queries, key_rows, value_rows, decay_slope, allowed, distance):
    raw_scores = jnp.dot(queries, key_rows.T, precision=precise)
    scores = jnp.where(allowed, (raw_scores - decay_slope * distance) * HD ** (-0.5), masked_score)
    scores = low_back(scores)
    row_max = lax.optimization_barrier(jnp.max(scores, axis=-1, keepdims=True))
    weights = jnp.exp(scores - row_max)
    probabilities = low(weights / lax.optimization_barrier(jnp.sum(weights, axis=-1, keepdims=True)))
    return jnp.dot(probabilities, value_rows, precision=precise)

def split_heads(matrix):
    return matrix.reshape(SEQ, H, HD).transpose(1, 0, 2)

def forward(sequence, segment_row, gains, shifts, biases, mixing, projection, expand, thresholds, contract):
    first = low(normalize(sequence, gains[0], shifts[0]))
    mixed_rows = jnp.einsum('td,dcf->tcf', first, mixing, precision=precise)
    queries = low(low_back(mixed_rows[:, 0] + biases[0]))
    key_rows = low(low_back(mixed_rows[:, 1]))
    value_rows = low(low_back(mixed_rows[:, 2] + biases[1]))
    places = jnp.arange(SEQ)
    distance = (places[:, None] - places[None, :]).astype(jnp.float32)
    allowed = (segment_row[:, None] == segment_row[None, :]) & (places[None, :] <= places[:, None])
    slopes = 2.0 ** (-8.0 * (jnp.arange(H) + 1).astype(jnp.float32) / H)
    checked = jax.checkpoint(head_attend)

    def one_head(element):
        return checked(element[0], element[1], element[2], element[3], allowed, distance)
    attended = lax.map(one_head, (split_heads(queries), split_heads(key_rows), split_heads(value_rows), slopes))
    attended = low(low_back(attended.transpose(1, 0, 2).reshape(SEQ, D)))
    branch = low_back(jnp.dot(attended, projection.T, precision=precise) + biases[2])
    middle = sequence + branch
    second = low(normalize(middle, gains[1], shifts[1]))
    hidden = low_back(jnp.dot(second, expand, precision=precise) + thresholds)
    active = low(0.5 * hidden * (1.0 + jax.scipy.special.erf(hidden * sqrt_half)))
    return middle + low_back(jnp.dot(active, contract.T, precision=precise) + biases[3])

def reference(tokens, segments, gains, shifts, biases, mixing, projection, expand, thresholds, contract, cotangent):
    params = tuple((param.astype(jnp.float32) for param in (gains, shifts, biases, mixing, projection, expand, thresholds, contract)))
    sequences = tokens.astype(jnp.float32).reshape(SEQS, SEQ, D)
    upstream = cotangent.astype(jnp.float32).reshape(SEQS, SEQ, D)

    def one_sequence(totals, element):
        sequence, segment_row, cot_rows = element

        def forward_one(seq_values, *weights):
            return forward(seq_values, segment_row, *weights)
        output, pullback = jax.vjp(forward_one, sequence, *params)
        gradients = pullback(cot_rows)
        return (jax.tree.map(jnp.add, totals, tuple(gradients[1:])), (output, gradients[0]))
    zeros = tuple((jnp.zeros_like(param) for param in params))
    totals, (outputs, input_grads) = lax.scan(one_sequence, zeros, (sequences, segments, upstream))
    return (outputs.reshape(TOKENS, D).astype(jnp.bfloat16), input_grads.reshape(TOKENS, D), totals[0], totals[1], totals[2], totals[3], totals[4], totals[5], totals[6], totals[7])
```

```python
from functools import partial

import jax
import jax.numpy as jnp
from jax import lax
from jax.experimental import pallas as pl
from jax.experimental.pallas import tpu as pltpu
from jax.sharding import PartitionSpec as P

HD = 64


norm_eps = 1e-05
sqrt_half = 0.7071067811865476
inverse_root = 0.3989422804014327
masked_score = -1e30
contract_last = (((1,), (1,)), ((), ()))
contract_first = (((0,), (0,)), ((), ()))


def normalize(resid, gain_row, shift_row, full_width):
    row_sums = lax.psum((jnp.sum(resid, axis=1), jnp.sum(resid * resid, axis=1)), "col")
    row_mean = row_sums[0][:, None] / full_width
    spread = row_sums[1][:, None] / full_width - row_mean * row_mean
    row_scale = lax.rsqrt(spread + norm_eps)
    centred = (resid - row_mean) * row_scale
    return (centred, row_scale, (centred * gain_row + shift_row).astype(jnp.bfloat16))


def normalize_back(upstream, centred, row_scale, gain_row, full_width):
    scaled = upstream * gain_row
    row_sums = lax.psum((jnp.sum(scaled, axis=1), jnp.sum(scaled * centred, axis=1)), "col")
    result = row_scale * (
        scaled - row_sums[0][:, None] / full_width - centred * (row_sums[1][:, None] / full_width)
    )
    return (result, jnp.sum(upstream * centred, axis=0), jnp.sum(upstream, axis=0))


def gather_features(local_part):
    return lax.all_gather(local_part, "col", axis=1, tiled=True)


def gather_grads(local_part):
    return lax.all_gather(local_part, "col", axis=1, tiled=True)


def sum_forward(partial_term):
    return lax.psum_scatter(partial_term, "col", scatter_dimension=1, tiled=True)


def sum_backward(partial_term):
    return lax.psum_scatter(partial_term, "col", scatter_dimension=1, tiled=True)


NT=(((1,),(1,)),((),()))
TN=(((0,),(0,)),((),()))
far=-1e33

def pick_heads(pair):
    lane=lax.broadcasted_iota(jnp.int32,pair.shape,1)
    zero=jnp.zeros_like(pair)
    return jnp.concatenate([jnp.where(lane<HD,pair,zero),jnp.where(lane<HD,zero,pair)],axis=0)

def attend_kernel(slope_ref,start_ref,q_ref,k_ref,v_ref,out_ref,log_ref,dist_ref,*,rows,scale):
    pair=pl.program_id(1)
    length=k_ref.shape[0]
    @pl.when(pair==0)
    def _():
        for r0 in range(0,length,rows):
            shape=(rows,r0+rows)
            i=lax.broadcasted_iota(jnp.int32,shape,0)+r0
            j=lax.broadcasted_iota(jnp.int32,shape,1)
            ok=(j<=i)&(j>=start_ref[0,r0:r0+rows,:])
            dist_ref[r0:r0+rows,0:r0+rows]=jnp.where(ok,(j-i).astype(jnp.float32),far)
    s0=slope_ref[2*pair]*scale; s1=slope_ref[2*pair+1]*scale
    for r0 in range(0,length,rows):
        r1=r0+rows
        q=pick_heads(q_ref[r0:r1,:]*jnp.asarray(scale,jnp.bfloat16))
        s=lax.dot_general(q,k_ref[0:r1,:],NT,preferred_element_type=jnp.float32)
        d=dist_ref[r0:r1,0:r1]
        s=jnp.concatenate([s[:rows]+d*s0,s[rows:]+d*s1],axis=0)
        m=jnp.max(s,axis=1,keepdims=True)
        e=jnp.exp(s-m)
        l=jnp.sum(e,axis=1,keepdims=True)
        p=(e*(1.0/l)).astype(jnp.bfloat16)
        o=jnp.dot(p,v_ref[0:r1,:],preferred_element_type=jnp.float32)
        lane=lax.broadcasted_iota(jnp.int32,(rows,2*HD),1)
        out_ref[r0:r1,:]=jnp.where(lane<HD,o[:rows],o[rows:]).astype(jnp.bfloat16)
        t=jnp.where(lane<HD,jnp.broadcast_to((m+jnp.log(l))[:rows],(rows,2*HD)),jnp.broadcast_to((m+jnp.log(l))[rows:],(rows,2*HD)))
        t=t.T
        log_ref[0,0:1,r0:r1]=t[0:1]
        log_ref[0,1:2,r0:r1]=t[HD:HD+1]

def attend_forward(q,k,v,start,slopes,seqs,rows=256):
    length=q.shape[0]//seqs; pairs=q.shape[1]//(2*HD)
    spec=pl.BlockSpec((length,2*HD),lambda s,p,*_:(s,p))
    return pl.pallas_call(partial(attend_kernel,rows=rows,scale=HD**-0.5),
        grid_spec=pltpu.PrefetchScalarGridSpec(num_scalar_prefetch=1,grid=(seqs,pairs),
            in_specs=[pl.BlockSpec((1,length,1),lambda s,p,*_:(s,0,0)),spec,spec,spec],
            out_specs=[spec,pl.BlockSpec((1,2,length),lambda s,p,*_:(s*pairs+p,0,0))],
            scratch_shapes=[pltpu.VMEM((length,length),jnp.float32)]),
        out_shape=[jax.ShapeDtypeStruct(q.shape,jnp.bfloat16),jax.ShapeDtypeStruct((seqs*pairs,2,length),jnp.float32)],
        compiler_params=pltpu.CompilerParams(vmem_limit_bytes=40<<20),
        cost_estimate=pl.CostEstimate(flops=4*seqs*pairs*2*length*length*HD,bytes_accessed=8*q.size,transcendentals=seqs*pairs*length*length),
        name="attend_forward")(slopes,start[:,:,None],q,k,v)

def attend_back_kernel(slope_ref,start_ref,log_ref,q_ref,k_ref,v_ref,g_ref,dq_ref,dk_ref,dv_ref,qs_ref,vs_ref,dist_ref,ka_ref,va_ref,*,rows,scale):
    pair=pl.program_id(1)
    length=k_ref.shape[0]
    @pl.when(pair==0)
    def _():
        for r0 in range(0,length,rows):
            shape=(r0+rows,rows)
            i=lax.broadcasted_iota(jnp.int32,shape,1)+r0
            j=lax.broadcasted_iota(jnp.int32,shape,0)
            ok=(j<=i)&(j>=start_ref[0,:,r0:r0+rows])
            dist_ref[0:r0+rows,r0:r0+rows]=jnp.where(ok,(j-i).astype(jnp.float32),far)
    s0=slope_ref[2*pair]*scale; s1=slope_ref[2*pair+1]*scale
    half=jnp.asarray(scale,jnp.bfloat16)
    qsum=jnp.zeros((1,2*HD),jnp.float32)
    for r0 in reversed(range(0,length,rows)):
        r1=r0+rows
        q=pick_heads(q_ref[r0:r1,:]*half)
        g=pick_heads(g_ref[r0:r1,:])
        k=k_ref[0:r1,:]; v=v_ref[0:r1,:]
        s=lax.dot_general(k,q,NT,preferred_element_type=jnp.float32)
        d=dist_ref[0:r1,r0:r1]
        logs=jnp.concatenate([log_ref[0,0:1,r0:r1],log_ref[0,1:2,r0:r1]],axis=1)
        s=jnp.concatenate([s[:,:rows]+d*s0,s[:,rows:]+d*s1],axis=1)
        p=jnp.exp(s-logs)
        t=lax.dot_general(v,g,NT,preferred_element_type=jnp.float32)
        centre=jnp.sum(p*t,axis=0,keepdims=True)
        ds=(p*(t-centre)).astype(jnp.bfloat16)
        pb=p.astype(jnp.bfloat16)
        va=jnp.dot(pb,g,preferred_element_type=jnp.float32)
        ka=jnp.dot(ds,q,preferred_element_type=jnp.float32)
        if r1==length:
            va_ref[...]=va; ka_ref[...]=ka
        else:
            va_ref[0:r1,:]+=va; ka_ref[0:r1,:]+=ka
        dq=lax.dot_general(ds,k,TN,preferred_element_type=jnp.float32)
        lane=lax.broadcasted_iota(jnp.int32,(rows,2*HD),1)
        dq=(jnp.where(lane<HD,dq[:rows],dq[rows:])*scale).astype(jnp.bfloat16)
        dq_ref[r0:r1,:]=dq
        qsum=qsum+jnp.sum(dq.astype(jnp.float32),axis=0,keepdims=True)
    qs_ref[0]=qsum
    dk_ref[...]=ka_ref[...].astype(jnp.bfloat16)
    dv=va_ref[...].astype(jnp.bfloat16)
    dv_ref[...]=dv
    vs_ref[0]=jnp.sum(dv.astype(jnp.float32),axis=0,keepdims=True)

def attend_backward(q,k,v,g,start,logs,slopes,seqs,rows=256):
    length=q.shape[0]//seqs; pairs=q.shape[1]//(2*HD)
    spec=pl.BlockSpec((length,2*HD),lambda s,p,*_:(s,p))
    out=jax.ShapeDtypeStruct(q.shape,jnp.bfloat16)
    sums=jax.ShapeDtypeStruct((seqs,1,q.shape[1]),jnp.float32)
    sspec=pl.BlockSpec((1,1,2*HD),lambda s,p,*_:(s,0,p))
    return pl.pallas_call(partial(attend_back_kernel,rows=rows,scale=HD**-0.5),
        grid_spec=pltpu.PrefetchScalarGridSpec(num_scalar_prefetch=1,grid=(seqs,pairs),
            in_specs=[pl.BlockSpec((1,1,length),lambda s,p,*_:(s,0,0)),pl.BlockSpec((1,2,length),lambda s,p,*_:(s*pairs+p,0,0)),spec,spec,spec,spec],
            out_specs=[spec,spec,spec,sspec,sspec],
            scratch_shapes=[pltpu.VMEM((length,length),jnp.float32),pltpu.VMEM((length,2*HD),jnp.float32),pltpu.VMEM((length,2*HD),jnp.float32)]),
        out_shape=[out,out,out,sums,sums],
        compiler_params=pltpu.CompilerParams(vmem_limit_bytes=40<<20),
        cost_estimate=pl.CostEstimate(flops=10*seqs*pairs*2*length*length*HD,bytes_accessed=14*q.size,transcendentals=seqs*pairs*length*length),
        name="attend_backward")(slopes,start[:,None,:],logs,q,k,v,g)


def on_device(
    tokens,
    segments,
    gains,
    shifts,
    biases,
    mixing,
    projection,
    expand,
    thresholds,
    contract,
    cotangent,
):
    seq_count = segments.shape[0]
    col_parts = lax.axis_size("col")
    full_width = tokens.shape[1] * col_parts
    head_count = mixing.shape[2] // HD
    head_ids = (lax.axis_index("col") * head_count + jnp.arange(head_count)).astype(jnp.float32)
    slopes = jnp.exp2(-8.0 * (head_ids + 1.0) / (head_count * col_parts))
    starts = jnp.sum(segments[:, None, :] < segments[:, :, None], axis=2).astype(jnp.int32)
    full_mix, full_proj, full_expand, full_contract = (
        lax.all_gather(mixing, "row", axis=0, tiled=True),
        lax.all_gather(projection, "row", axis=0, tiled=True),
        lax.all_gather(expand, "row", axis=0, tiled=True),
        lax.all_gather(contract, "row", axis=0, tiled=True),
    )
    resid_in = tokens.astype(jnp.float32)
    first_centred, first_scale, first_normed = normalize(resid_in, gains[0], shifts[0], full_width)
    first_full = gather_features(first_normed)
    mixed_rows = jnp.einsum("td,dcf->tcf", first_full, full_mix, preferred_element_type=jnp.float32)
    query_part = (mixed_rows[:, 0] + biases[0]).astype(jnp.bfloat16)
    key_part = mixed_rows[:, 1].astype(jnp.bfloat16)
    value_part = (mixed_rows[:, 2] + biases[1]).astype(jnp.bfloat16)
    attended, log_totals = attend_forward(
        query_part, key_part, value_part, starts, slopes, seq_count
    )
    proj_term = lax.dot_general(
        attended, full_proj, contract_last, preferred_element_type=jnp.float32
    )
    middle = resid_in + (sum_forward(proj_term) + biases[2])
    second_centred, second_scale, second_normed = normalize(middle, gains[1], shifts[1], full_width)
    second_full = gather_features(second_normed)
    hidden = jnp.dot(second_full, full_expand, preferred_element_type=jnp.float32) + thresholds
    erf_part = jax.scipy.special.erf(hidden * sqrt_half)
    active = (0.5 * hidden * (1.0 + erf_part)).astype(jnp.bfloat16)
    mlp_term = lax.dot_general(
        active, full_contract, contract_last, preferred_element_type=jnp.float32
    )
    layer_out = (middle + (sum_forward(mlp_term) + biases[3])).astype(jnp.bfloat16)
    back_mix, back_proj, back_expand, back_contract = (
        lax.all_gather(mixing, "row", axis=0, tiled=True),
        lax.all_gather(projection, "row", axis=0, tiled=True),
        lax.all_gather(expand, "row", axis=0, tiled=True),
        lax.all_gather(contract, "row", axis=0, tiled=True),
    )
    cot_full = gather_grads(cotangent)
    columns = cot_full
    contract_grad = lax.psum_scatter(
        lax.dot_general(columns, active, contract_first, preferred_element_type=jnp.float32),
        "row",
        scatter_dimension=0,
        tiled=True,
    )
    active_grad = jnp.dot(cot_full, back_contract, preferred_element_type=jnp.float32)
    density = jnp.exp(-0.5 * hidden * hidden) * inverse_root
    hidden_grad = (active_grad * (0.5 * (1.0 + erf_part) + hidden * density)).astype(jnp.bfloat16)
    columns = second_full
    expand_grad = lax.psum_scatter(
        lax.dot_general(columns, hidden_grad, contract_first, preferred_element_type=jnp.float32),
        "row",
        scatter_dimension=0,
        tiled=True,
    )
    thresholds_part = jnp.sum(hidden_grad.astype(jnp.float32), axis=0)
    second_back = sum_backward(
        lax.dot_general(hidden_grad, back_expand, contract_last, preferred_element_type=jnp.float32)
    )
    second_input, second_gain_part, second_shift_part = normalize_back(
        second_back, second_centred, second_scale, gains[1], full_width
    )
    cot_float = cotangent.astype(jnp.float32)
    middle_grad = cot_float + second_input
    branch_grad = middle_grad.astype(jnp.bfloat16)
    branch_full = gather_grads(branch_grad)
    columns = branch_full
    projection_grad = lax.psum_scatter(
        lax.dot_general(columns, attended, contract_first, preferred_element_type=jnp.float32),
        "row",
        scatter_dimension=0,
        tiled=True,
    )
    attended_grad = jnp.dot(branch_full, back_proj, preferred_element_type=jnp.float32).astype(
        jnp.bfloat16
    )
    query_back, key_back, value_back, query_bias_part, value_bias_part = attend_backward(
        query_part, key_part, value_part, attended_grad, starts, log_totals, slopes, seq_count
    )
    mixed_grad = jnp.stack([query_back, key_back, value_back], axis=1)
    columns = first_full
    mixing_grad = lax.psum_scatter(
        jnp.einsum("tc,tkf->ckf", columns, mixed_grad, preferred_element_type=jnp.float32),
        "row",
        scatter_dimension=0,
        tiled=True,
    )
    query_bias_part = jnp.sum(query_bias_part, axis=(0, 1))
    value_bias_part = jnp.sum(value_bias_part, axis=(0, 1))
    first_back = sum_backward(
        jnp.einsum("tkf,dkf->td", mixed_grad, back_mix, preferred_element_type=jnp.float32)
    )
    first_input, first_gain_part, first_shift_part = normalize_back(
        first_back, first_centred, first_scale, gains[0], full_width
    )
    tokens_grad = middle_grad + first_input
    gains_grad, shifts_grad, biases_grad, thresholds_grad = lax.psum(
        (
            jnp.stack([first_gain_part, second_gain_part]),
            jnp.stack([first_shift_part, second_shift_part]),
            jnp.stack(
                [
                    query_bias_part,
                    value_bias_part,
                    jnp.sum(branch_grad.astype(jnp.float32), axis=0),
                    jnp.sum(cot_float, axis=0),
                ]
            ),
            thresholds_part,
        ),
        "row",
    )
    return (
        layer_out,
        tokens_grad,
        gains_grad,
        shifts_grad,
        biases_grad,
        mixing_grad,
        projection_grad,
        expand_grad,
        thresholds_grad,
        contract_grad,
    )


def solution(mesh):
    return jax.shard_map(
        on_device,
        mesh=mesh,
        in_specs=(
            P("row", "col"),
            P("row", None),
            P(None, "col"),
            P(None, "col"),
            P(None, "col"),
            P("row", None, "col"),
            P("row", "col"),
            P("row", "col"),
            P("col"),
            P("row", "col"),
            P("row", "col"),
        ),
        out_specs=(
            P("row", "col"),
            P("row", "col"),
            P(None, "col"),
            P(None, "col"),
            P(None, "col"),
            P("row", None, "col"),
            P("row", "col"),
            P("row", "col"),
            P("col"),
            P("row", "col"),
        ),
        check_vma=False,
    )
```

```python
import math
from functools import partial

import jax
import jax.numpy as jnp
from jax import lax
from jax.experimental import pallas as pl
from jax.experimental.pallas import tpu as pltpu
from jax.sharding import PartitionSpec as P

HD = 64
BLOCK = 256

norm_eps = 1e-05
sqrt_half = 0.7071067811865476
inverse_root = 0.3989422804014327
far = -1e33
NT = (((1,), (1,)), ((), ()))
TN = (((0,), (0,)), ((), ()))
VMEM_LIMIT = 48 << 20
f32 = jnp.float32
bf16 = jnp.bfloat16


def pick_heads(pair):
    lane = lax.broadcasted_iota(jnp.int32, pair.shape, 1)
    zero = jnp.zeros_like(pair)
    return jnp.concatenate(
        [jnp.where(lane < HD, pair, zero), jnp.where(lane < HD, zero, pair)], axis=0
    )


def attend_kernel(
    slope_ref, start_ref, q_ref, k_ref, v_ref, out_ref, log_ref, dist_ref, *, rows, scale
):
    pair = pl.program_id(1)
    length = k_ref.shape[0]

    @pl.when(pair == 0)
    def _():
        for r0 in range(0, length, rows):
            shape = (rows, r0 + rows)
            i = lax.broadcasted_iota(jnp.int32, shape, 0) + r0
            j = lax.broadcasted_iota(jnp.int32, shape, 1)
            allowed = (j <= i) & (j >= start_ref[0, r0 : r0 + rows, :])
            dist_ref[r0 : r0 + rows, 0 : r0 + rows] = jnp.where(allowed, (j - i).astype(f32), far)

    slope_a, slope_b = slope_ref[2 * pair] * scale, slope_ref[2 * pair + 1] * scale
    for r0 in range(0, length, rows):
        r1 = r0 + rows
        q = pick_heads(q_ref[r0:r1, :] * jnp.asarray(scale, bf16))
        s = lax.dot_general(q, k_ref[0:r1, :], NT, preferred_element_type=f32)
        d = dist_ref[r0:r1, 0:r1]
        s = jnp.concatenate([s[:rows] + d * slope_a, s[rows:] + d * slope_b], axis=0)
        row_max = jnp.max(s, axis=1, keepdims=True)
        weights = jnp.exp(s - row_max)
        row_total = jnp.sum(weights, axis=1, keepdims=True)
        probs = (weights * (1.0 / row_total)).astype(bf16)
        o = jnp.dot(probs, v_ref[0:r1, :], preferred_element_type=f32)
        lane = lax.broadcasted_iota(jnp.int32, (rows, 2 * HD), 1)
        out_ref[r0:r1, :] = jnp.where(lane < HD, o[:rows], o[rows:]).astype(bf16)
        logs = row_max + jnp.log(row_total)
        logs = jnp.where(
            lane < HD,
            jnp.broadcast_to(logs[:rows], (rows, 2 * HD)),
            jnp.broadcast_to(logs[rows:], (rows, 2 * HD)),
        ).T
        log_ref[0, 0:1, r0:r1] = logs[0:1]
        log_ref[0, 1:2, r0:r1] = logs[HD : HD + 1]


def attend_forward(mixed, starts, slopes, seqs, rows=256):
    length, pairs = mixed.shape[0] // seqs, mixed.shape[1] // (6 * HD)

    def part(i):
        return pl.BlockSpec((length, 2 * HD), lambda s, p, *_: (s, i * pairs + p))

    return pl.pallas_call(
        partial(attend_kernel, rows=rows, scale=HD**-0.5),
        grid_spec=pltpu.PrefetchScalarGridSpec(
            num_scalar_prefetch=1,
            grid=(seqs, pairs),
            in_specs=[
                pl.BlockSpec((1, length, 1), lambda s, p, *_: (s, 0, 0)),
                part(0),
                part(1),
                part(2),
            ],
            out_specs=[part(0), pl.BlockSpec((1, 2, length), lambda s, p, *_: (s * pairs + p, 0, 0))],
            scratch_shapes=[pltpu.VMEM((length, length), f32)],
        ),
        out_shape=[
            jax.ShapeDtypeStruct((mixed.shape[0], 2 * HD * pairs), bf16),
            jax.ShapeDtypeStruct((seqs * pairs, 2, length), f32),
        ],
        compiler_params=pltpu.CompilerParams(vmem_limit_bytes=40 << 20),
        cost_estimate=pl.CostEstimate(
            flops=8 * seqs * pairs * length * length * HD * 3,
            bytes_accessed=4 * mixed.size,
            transcendentals=seqs * pairs * length * length,
        ),
        name="attend_forward",
    )(slopes, starts[:, :, None], mixed, mixed, mixed)


def attend_back_kernel(
    slope_ref,
    start_ref,
    log_ref,
    q_ref,
    k_ref,
    v_ref,
    g_ref,
    dq_ref,
    dk_ref,
    dv_ref,
    qs_ref,
    vs_ref,
    dist_ref,
    ka_ref,
    va_ref,
    *,
    rows,
    scale,
):
    pair = pl.program_id(1)
    length = k_ref.shape[0]

    @pl.when(pair == 0)
    def _():
        for r0 in range(0, length, rows):
            shape = (r0 + rows, rows)
            i = lax.broadcasted_iota(jnp.int32, shape, 1) + r0
            j = lax.broadcasted_iota(jnp.int32, shape, 0)
            allowed = (j <= i) & (j >= start_ref[0, :, r0 : r0 + rows])
            dist_ref[0 : r0 + rows, r0 : r0 + rows] = jnp.where(allowed, (j - i).astype(f32), far)

    slope_a, slope_b = slope_ref[2 * pair] * scale, slope_ref[2 * pair + 1] * scale
    query_sum = jnp.zeros((1, 2 * HD), f32)
    for r0 in reversed(range(0, length, rows)):
        r1 = r0 + rows
        q = pick_heads(q_ref[r0:r1, :] * jnp.asarray(scale, bf16))
        g = pick_heads(g_ref[r0:r1, :])
        k, v = k_ref[0:r1, :], v_ref[0:r1, :]
        s = lax.dot_general(k, q, NT, preferred_element_type=f32)
        d = dist_ref[0:r1, r0:r1]
        logs = jnp.concatenate([log_ref[0, 0:1, r0:r1], log_ref[0, 1:2, r0:r1]], axis=1)
        s = jnp.concatenate([s[:, :rows] + d * slope_a, s[:, rows:] + d * slope_b], axis=1)
        probs = jnp.exp(s - logs)
        t = lax.dot_general(v, g, NT, preferred_element_type=f32)
        centre = jnp.sum(probs * t, axis=0, keepdims=True)
        score_grad = (probs * (t - centre)).astype(bf16)
        value_part = jnp.dot(probs.astype(bf16), g, preferred_element_type=f32)
        key_part = jnp.dot(score_grad, q, preferred_element_type=f32)
        if r1 == length:
            va_ref[...] = value_part
            ka_ref[...] = key_part
        else:
            va_ref[0:r1, :] += value_part
            ka_ref[0:r1, :] += key_part
        dq = lax.dot_general(score_grad, k, TN, preferred_element_type=f32)
        lane = lax.broadcasted_iota(jnp.int32, (rows, 2 * HD), 1)
        dq = (jnp.where(lane < HD, dq[:rows], dq[rows:]) * scale).astype(bf16)
        dq_ref[r0:r1, :] = dq
        query_sum = query_sum + jnp.sum(dq.astype(f32), axis=0, keepdims=True)
    qs_ref[0] = query_sum
    dk_ref[...] = ka_ref[...].astype(bf16)
    dv = va_ref[...].astype(bf16)
    dv_ref[...] = dv
    vs_ref[0] = jnp.sum(dv.astype(f32), axis=0, keepdims=True)


def attend_backward(mixed, grads, starts, logs, slopes, seqs, rows=256):
    length, pairs = mixed.shape[0] // seqs, mixed.shape[1] // (6 * HD)

    def part(i):
        return pl.BlockSpec((length, 2 * HD), lambda s, p, *_: (s, i * pairs + p))

    out = jax.ShapeDtypeStruct(grads.shape, bf16)
    sums = jax.ShapeDtypeStruct((seqs, 1, grads.shape[1]), f32)
    sum_spec = pl.BlockSpec((1, 1, 2 * HD), lambda s, p, *_: (s, 0, p))
    return pl.pallas_call(
        partial(attend_back_kernel, rows=rows, scale=HD**-0.5),
        grid_spec=pltpu.PrefetchScalarGridSpec(
            num_scalar_prefetch=1,
            grid=(seqs, pairs),
            in_specs=[
                pl.BlockSpec((1, 1, length), lambda s, p, *_: (s, 0, 0)),
                pl.BlockSpec((1, 2, length), lambda s, p, *_: (s * pairs + p, 0, 0)),
                part(0),
                part(1),
                part(2),
                part(0),
            ],
            out_specs=[part(0), part(0), part(0), sum_spec, sum_spec],
            scratch_shapes=[
                pltpu.VMEM((length, length), f32),
                pltpu.VMEM((length, 2 * HD), f32),
                pltpu.VMEM((length, 2 * HD), f32),
            ],
        ),
        out_shape=[out, out, out, sums, sums],
        compiler_params=pltpu.CompilerParams(vmem_limit_bytes=40 << 20),
        cost_estimate=pl.CostEstimate(
            flops=20 * seqs * pairs * length * length * HD * 2,
            bytes_accessed=14 * grads.size,
            transcendentals=seqs * pairs * length * length,
        ),
        name="attend_backward",
    )(slopes, starts[:, None, :], logs, mixed, mixed, mixed, grads)


def resident(shape):
    return pl.BlockSpec(shape, lambda *_: (0,) * len(shape))


def flat_rows(ws):
    return jnp.concatenate([w[...] for w in ws], axis=0)


def matmul_call(kernel, grid, ins, outs, scratch, flops, name, prefetch=()):
    moved = sum(a.size * a.dtype.itemsize for a, _ in ins)
    moved += sum(jnp.dtype(t).itemsize * math.prod(s) for s, t, _ in outs)
    return pl.pallas_call(
        kernel,
        grid_spec=pltpu.PrefetchScalarGridSpec(
            num_scalar_prefetch=len(prefetch),
            grid=grid,
            in_specs=[s for _, s in ins],
            out_specs=[s for _, _, s in outs],
            scratch_shapes=scratch,
        ),
        out_shape=[jax.ShapeDtypeStruct(s, t) for s, t, _ in outs],
        compiler_params=pltpu.CompilerParams(vmem_limit_bytes=VMEM_LIMIT),
        cost_estimate=pl.CostEstimate(flops=flops, bytes_accessed=moved, transcendentals=0),
        name=name,
    )(*prefetch, *[a for a, _ in ins])


def times_rows(x, ws, extras, outs, finish, name, tn, tm=256):
    tokens, depth = x.shape
    width = ws[0].shape[1]
    tn, tm = min(tn, width), min(tm, tokens)
    n_ws, n_ex = len(ws), len(extras)

    def kernel(*refs):
        x_ref, w_refs = refs[0], refs[1 : 1 + n_ws]
        extra, out = refs[1 + n_ws : 1 + n_ws + n_ex], refs[1 + n_ws + n_ex :]
        rows = pl.ds(pl.multiple_of(pl.program_id(1) * tm, tm), tm)
        acc = jnp.dot(x_ref[rows, :], flat_rows(w_refs), preferred_element_type=f32)
        finish(acc, extra, out)

    def spec(shape):
        if shape[0] == 1:
            return pl.BlockSpec((1, tn), lambda n, m: (0, n))
        return pl.BlockSpec((tm, tn), lambda n, m: (m, n))

    ins = [(x, resident(x.shape))]
    ins += [(w, pl.BlockSpec((w.shape[0], tn), lambda n, m: (0, n))) for w in ws]
    ins += [(e, spec(e.shape)) for e in extras]
    return matmul_call(
        kernel,
        (width // tn, tokens // tm),
        ins,
        [(s, t, spec(s)) for s, t in outs],
        [],
        2 * tokens * depth * width,
        name,
    )


def times_columns(xs, ws, slots, name, tm=256):
    tokens = xs[0].shape[0]
    tm = min(tm, tokens)
    blocks = sum(w.shape[0] for w in ws) // BLOCK
    half = blocks // 2
    n_xs = len(xs)

    def kernel(slot_ref, *refs):
        x_refs, w_refs = refs[:n_xs], refs[n_xs : n_xs + len(ws)]
        sent_ref, kept_ref = refs[n_xs + len(ws) :]
        x = jnp.concatenate([r[...] for r in x_refs], axis=1)
        at = 0
        for w_ref in w_refs:
            for r0 in range(0, w_ref.shape[0], BLOCK):
                acc = lax.dot_general(x, w_ref[r0 : r0 + BLOCK, :], NT, preferred_element_type=f32)
                slot = slot_ref[at]

                @pl.when(slot < half)
                def _():
                    place = pl.ds(pl.multiple_of(slot * BLOCK, BLOCK), BLOCK)
                    sent_ref[:, place] = acc.astype(bf16)

                @pl.when(slot >= half)
                def _():
                    place = pl.ds(pl.multiple_of((slot - half) * BLOCK, BLOCK), BLOCK)
                    kept_ref[:, place] = acc

                at += 1

    ins = [(x, pl.BlockSpec((tm, x.shape[1]), lambda m, *_: (m, 0))) for x in xs]
    ins += [(w, resident(w.shape)) for w in ws]
    out_spec = pl.BlockSpec((tm, half * BLOCK), lambda m, *_: (m, 0))
    return matmul_call(
        kernel,
        (tokens // tm,),
        ins,
        [((tokens, half * BLOCK), bf16, out_spec), ((tokens, half * BLOCK), f32, out_spec)],
        [],
        2 * tokens * blocks * BLOCK * ws[0].shape[1],
        name,
        prefetch=(slots,),
    )


def weight_parts(a, first, count, gs, dtype, name):
    tokens = a.shape[0]
    width = sum(g.shape[1] for g in gs)
    n_gs = len(gs)

    def kernel(a_ref, *refs):
        g_refs, out_refs = refs[:n_gs], refs[n_gs:]
        g = jnp.concatenate([r[...] for r in g_refs], axis=1)
        acc = lax.dot_general(a_ref[...], g, TN, preferred_element_type=f32).astype(dtype)
        for i in range(count):

            @pl.when(pl.program_id(0) == i)
            def _(i=i):
                out_refs[i][...] = acc

    ins = [(a, pl.BlockSpec((tokens, BLOCK), lambda i: (0, first + i)))]
    ins += [(g, resident(g.shape)) for g in gs]
    return matmul_call(
        kernel,
        (count,),
        ins,
        [((BLOCK, width), dtype, resident((BLOCK, width))) for _ in range(count)],
        [],
        2 * tokens * BLOCK * count * width,
        name,
    )


def place_blocks(values, place_ref, out_ref):
    at = 0
    for value in values:
        for c0 in range(0, value.shape[1], BLOCK):
            place = pl.ds(pl.multiple_of(place_ref[at] * BLOCK, BLOCK), BLOCK)
            out_ref[:, place] = value[:, c0 : c0 + BLOCK]
            at += 1


def lay_out(parts, places, name, tm=256):
    tokens, width = parts[0].shape
    full = width * len(parts)

    def kernel(place_ref, *refs):
        place_blocks([r[...] for r in refs[:-1]], place_ref, refs[-1])

    return matmul_call(
        kernel,
        (tokens // tm,),
        [(p, pl.BlockSpec((tm, width), lambda m, *_: (m, 0))) for p in parts],
        [((tokens, full), bf16, pl.BlockSpec((tm, full), lambda m, *_: (m, 0)))],
        [],
        tokens * full,
        name,
        prefetch=(places,),
    )[0]


def normalize(parts, gain, shift, places, name, tm=256):
    tokens, width = parts[0].shape
    n = len(parts)
    full = width * n

    def kernel(place_ref, *refs):
        gain_ref, shift_ref, out_ref, mean_ref, scale_ref = refs[n:]
        rows = [r[...].astype(f32) for r in refs[:n]]
        mean = sum(jnp.sum(v, axis=1, keepdims=True) for v in rows) / full
        square = sum(jnp.sum(v * v, axis=1, keepdims=True) for v in rows) / full
        scale = lax.rsqrt(square - mean * mean + norm_eps)
        mean_ref[...] = mean
        scale_ref[...] = scale
        done = []
        for i, v in enumerate(rows):
            cols = slice(i * width, (i + 1) * width)
            done.append(((v - mean) * scale * gain_ref[:, cols] + shift_ref[:, cols]).astype(bf16))
        place_blocks(done, place_ref, out_ref)

    ins = [(p, pl.BlockSpec((tm, width), lambda m, *_: (m, 0))) for p in parts]
    ins += [(gain, resident(gain.shape)), (shift, resident(shift.shape))]
    column = pl.BlockSpec((tm, 1), lambda m, *_: (m, 0))
    return matmul_call(
        kernel,
        (tokens // tm,),
        ins,
        [
            ((tokens, full), bf16, pl.BlockSpec((tm, full), lambda m, *_: (m, 0))),
            ((tokens, 1), f32, column),
            ((tokens, 1), f32, column),
        ],
        [],
        8 * tokens * full,
        name,
        prefetch=(places,),
    )


def swap(x, axis, bit):
    return lax.ppermute(x, axis, [(i, i ^ bit) for i in range(lax.axis_size(axis))])


def turn(x, steps):
    count = lax.axis_size("row")
    return lax.ppermute(x, "row", [(i, (i + 2 * steps) % count) for i in range(count)])


def gather_columns(x):
    near, across = swap(x, "col", 1), swap(x, "col", 2)
    return [x, near, across, swap(across, "col", 1)]


def sum_columns(sent, kept):
    half = kept.shape[1] // 2
    got = swap(sent, "col", 1)
    across = swap((kept[:, half:] + got[:, half:].astype(f32)).astype(bf16), "col", 2)
    return kept[:, :half] + got[:, :half].astype(f32) + across.astype(f32)


def sum_col_stats(stats):
    stats = stats + swap(stats, "col", 1)
    return stats + swap(stats, "col", 2)


def sum_rows(x):
    bit = 1
    while bit < lax.axis_size("row"):
        x = x + swap(x, "row", bit)
        bit *= 2
    return x


def gather_rows(w, stepped):
    if not stepped:
        return [lax.all_gather(w, "row", axis=0, tiled=True)]
    own = [w] + [turn(w, k) for k in range(1, lax.axis_size("row") // 2)]
    return own + [swap(v, "row", 1) for v in own]


def sum_weight(a, gs, stepped, name):
    if not stepped:
        whole = weight_parts(a, 0, a.shape[1] // BLOCK, gs, f32, name)
        return lax.psum_scatter(
            jnp.concatenate(whole, axis=0), "row", scatter_dimension=0, tiled=True
        )
    count = lax.axis_size("row") // 2
    other = weight_parts(a, count, count, gs, bf16, name + "_other")
    got = [None] * count
    for k in reversed(range(count)):
        got[k] = swap(other[k], "row", 1)
    mine = weight_parts(a, 0, count, gs, f32, name + "_mine")
    total = None
    for k in reversed(range(count)):
        term = mine[k] + got[k].astype(f32)
        if k:
            term = turn(term.astype(bf16), -k).astype(f32)
        total = term if total is None else total + term
    return total


def on_device(
    tokens,
    segments,
    gains,
    shifts,
    biases,
    mixing,
    projection,
    expand,
    thresholds,
    contract,
    cotangent,
):
    seqs = segments.shape[0]
    rows, cols = lax.axis_size("row"), lax.axis_size("col")
    row, col = lax.axis_index("row"), lax.axis_index("col")
    tokens_here, width = tokens.shape
    full = width * cols
    heads = width // HD
    stepped = full // rows == BLOCK and rows == 2 * cols
    blocks = full // BLOCK
    per_col = width // BLOCK
    at = jnp.arange(blocks)
    if stepped:
        outer, inner = row // 2, row % 2
        ids = 2 * ((outer - at % (rows // 2)) % (rows // 2)) + (inner ^ (at // (rows // 2)))
        mine = (at // per_col) ^ col
        places = ((at % per_col) ^ inner) * (rows // 2) + (outer - mine) % (rows // 2)
    else:
        ids = at
        places = ((at // per_col) ^ col) * per_col + at % per_col
    away = (ids // per_col) ^ col
    slots = (away // 2 + (1 - away % 2) * 2) * per_col + ids % per_col
    places, slots = places.astype(jnp.int32), slots.astype(jnp.int32)

    head_ids = (col * heads + jnp.arange(heads)).astype(f32)
    slopes = jnp.exp2(-8.0 * (head_ids + 1.0) / (heads * cols))
    starts = jnp.sum(segments[:, None, :] < segments[:, :, None], axis=2).astype(jnp.int32)

    full_mix = gather_rows(mixing.reshape(mixing.shape[0], -1), stepped)
    token_parts = gather_columns(tokens)
    norms = gather_columns(jnp.concatenate([gains, shifts], axis=0))
    norms = jnp.concatenate(norms, axis=1)
    full_proj = gather_rows(projection, stepped)
    full_expand = gather_rows(expand, stepped)
    full_contract = gather_rows(contract, stepped)
    cot_parts = gather_columns(cotangent)

    first_full, first_mean, first_scale = normalize(
        token_parts, norms[0:1], norms[2:3], places, "first_norm"
    )
    mixed_bias = jnp.concatenate([biases[0:1], jnp.zeros((1, width), f32), biases[1:2]], axis=1)

    def add_bias(acc, extra, out):
        out[0][...] = (acc + extra[0][...]).astype(bf16)

    (mixed,) = times_rows(
        first_full,
        full_mix,
        [mixed_bias],
        [((tokens_here, 3 * width), bf16)],
        add_bias,
        "mix",
        tn=512,
    )
    attended, logs = attend_forward(mixed, starts, slopes, seqs)
    resid = tokens.astype(f32)
    middle = resid + (
        sum_columns(*times_columns([attended], full_proj, slots, "project")) + biases[2]
    )
    second_full, second_mean, second_scale = normalize(
        gather_columns(middle.astype(bf16)), norms[1:2], norms[3:4], places, "second_norm"
    )

    def activate(acc, extra, out):
        hidden = acc + extra[0][...]
        bell = 0.5 * (1.0 + lax.erf(hidden * sqrt_half))
        out[0][...] = (hidden * bell).astype(bf16)
        out[1][...] = bell + hidden * (jnp.exp(-0.5 * hidden * hidden) * inverse_root)

    hidden_shape = (tokens_here, expand.shape[1])
    active, slope = times_rows(
        second_full,
        full_expand,
        [thresholds[None]],
        [(hidden_shape, bf16), (hidden_shape, f32)],
        activate,
        "expand",
        tn=512,
    )
    cot_full = lay_out(cot_parts, places, "cotangent_rows")
    contract_grad = sum_weight(cot_full, [active], stepped, "contract_grad")

    def back_activate(acc, extra, out):
        grad = (acc * extra[0][...]).astype(bf16)
        out[0][...] = grad
        total = jnp.sum(grad.astype(f32), axis=0, keepdims=True)

        @pl.when(pl.program_id(1) == 0)
        def _():
            out[1][...] = total

        @pl.when(pl.program_id(1) > 0)
        def _():
            out[1][...] += total

    hidden_grad, thresholds_part = times_rows(
        cot_full,
        full_contract,
        [slope],
        [(hidden_shape, bf16), ((1, hidden_shape[1]), f32)],
        back_activate,
        "contract_back",
        tn=512,
    )
    second_back = sum_columns(*times_columns([hidden_grad], full_expand, slots, "expand_back"))
    layer_out = (
        middle + (sum_columns(*times_columns([active], full_contract, slots, "contract")) + biases[3])
    ).astype(bf16)
    expand_grad = sum_weight(second_full, [hidden_grad], stepped, "expand_grad")

    def norm_back(upstream, centred, scale, gain):
        scaled = upstream * gain
        sums = sum_col_stats(
            jnp.stack([jnp.sum(scaled, axis=1), jnp.sum(scaled * centred, axis=1)])
        )
        result = scale * (
            scaled - sums[0][:, None] / full - centred * (sums[1][:, None] / full)
        )
        return result, jnp.sum(upstream * centred, axis=0), jnp.sum(upstream, axis=0)

    second_centred = (middle - second_mean) * second_scale
    second_input, second_gain, second_shift = norm_back(
        second_back, second_centred, second_scale, gains[1]
    )
    cot_float = cotangent.astype(f32)
    middle_grad = cot_float + second_input
    branch_grad = middle_grad.astype(bf16)
    branch_full = lay_out(gather_columns(branch_grad), places, "branch_rows")

    def store(acc, extra, out):
        out[0][...] = acc.astype(bf16)

    (attended_grad,) = times_rows(
        branch_full,
        full_proj,
        [],
        [((tokens_here, width), bf16)],
        store,
        "project_back",
        tn=512,
    )
    projection_grad = sum_weight(branch_full, [attended], stepped, "projection_grad")
    query_back, key_back, value_back, query_sum, value_sum = attend_backward(
        mixed, attended_grad, starts, logs, slopes, seqs
    )
    mixed_grads = [query_back, key_back, value_back]
    mixing_grad = sum_weight(first_full, mixed_grads, stepped, "mixing_grad")
    first_back = sum_columns(*times_columns(mixed_grads, full_mix, slots, "mix_back"))
    first_centred = (resid - first_mean) * first_scale
    first_input, first_gain, first_shift = norm_back(
        first_back, first_centred, first_scale, gains[0]
    )
    tokens_grad = middle_grad + first_input
    small = jnp.stack(
        [
            first_gain,
            second_gain,
            first_shift,
            second_shift,
            jnp.sum(query_sum, axis=(0, 1)),
            jnp.sum(value_sum, axis=(0, 1)),
            jnp.sum(branch_grad.astype(f32), axis=0),
            jnp.sum(cot_float, axis=0),
        ]
    )
    small = sum_rows(jnp.concatenate([small, thresholds_part.reshape(-1, width)], axis=0))
    return (
        layer_out,
        tokens_grad,
        small[0:2],
        small[2:4],
        small[4:8],
        mixing_grad.reshape(mixing.shape),
        projection_grad,
        expand_grad,
        small[8:].reshape(thresholds.shape),
        contract_grad,
    )


def solution(mesh):
    return jax.shard_map(
        on_device,
        mesh=mesh,
        in_specs=(
            P("row", "col"),
            P("row", None),
            P(None, "col"),
            P(None, "col"),
            P(None, "col"),
            P("row", None, "col"),
            P("row", "col"),
            P("row", "col"),
            P("col"),
            P("row", "col"),
            P("row", "col"),
        ),
        out_specs=(
            P("row", "col"),
            P("row", "col"),
            P(None, "col"),
            P(None, "col"),
            P(None, "col"),
            P("row", None, "col"),
            P("row", "col"),
            P("row", "col"),
            P("col"),
            P("row", "col"),
        ),
        check_vma=False,
    )
```

```python
import math
from functools import partial

import jax
import jax.numpy as jnp
from jax import lax
from jax.experimental import pallas as pl
from jax.experimental.pallas import tpu as pltpu
from jax.sharding import PartitionSpec as P

HD = 64
BLOCK = 256

norm_eps = 1e-05
sqrt_half = 0.7071067811865476
inverse_root = 0.3989422804014327
far = -1e33
NT = (((1,), (1,)), ((), ()))
TN = (((0,), (0,)), ((), ()))
VMEM_LIMIT = 56 << 20
CHEAP = 64
f32 = jnp.float32
bf16 = jnp.bfloat16


def pick_heads(pair):
    lane = lax.broadcasted_iota(jnp.int32, pair.shape, 1)
    zero = jnp.zeros_like(pair)
    return jnp.concatenate(
        [jnp.where(lane < HD, pair, zero), jnp.where(lane < HD, zero, pair)], axis=0
    )


def attend_kernel(
    slope_ref, start_ref, q_ref, k_ref, v_ref, out_ref, log_ref, dist_ref, *, rows, scale
):
    pair = pl.program_id(1)
    length = k_ref.shape[0]

    @pl.when(pair == 0)
    def _():
        for r0 in range(0, length, rows):
            shape = (rows, r0 + rows)
            i = lax.broadcasted_iota(jnp.int32, shape, 0) + r0
            j = lax.broadcasted_iota(jnp.int32, shape, 1)
            allowed = (j <= i) & (j >= start_ref[0, r0 : r0 + rows, :])
            dist_ref[r0 : r0 + rows, 0 : r0 + rows] = jnp.where(allowed, (j - i).astype(f32), far)

    slope_a, slope_b = slope_ref[2 * pair] * scale, slope_ref[2 * pair + 1] * scale
    for r0 in range(0, length, rows):
        r1 = r0 + rows
        q = pick_heads(q_ref[r0:r1, :] * jnp.asarray(scale, bf16))
        s = lax.dot_general(q, k_ref[0:r1, :], NT, preferred_element_type=f32)
        d = dist_ref[r0:r1, 0:r1]
        s = jnp.concatenate([s[:rows] + d * slope_a, s[rows:] + d * slope_b], axis=0)
        row_max = jnp.max(s, axis=1, keepdims=True)
        weights = jnp.exp(s - row_max)
        row_total = jnp.sum(weights, axis=1, keepdims=True)
        probs = (weights * (1.0 / row_total)).astype(bf16)
        o = jnp.dot(probs, v_ref[0:r1, :], preferred_element_type=f32)
        lane = lax.broadcasted_iota(jnp.int32, (rows, 2 * HD), 1)
        out_ref[r0:r1, :] = jnp.where(lane < HD, o[:rows], o[rows:]).astype(bf16)
        logs = row_max + jnp.log(row_total)
        logs = jnp.where(
            lane < HD,
            jnp.broadcast_to(logs[:rows], (rows, 2 * HD)),
            jnp.broadcast_to(logs[rows:], (rows, 2 * HD)),
        ).T
        log_ref[0, 0:1, r0:r1] = logs[0:1]
        log_ref[0, 1:2, r0:r1] = logs[HD : HD + 1]


def attend_forward(mixed, starts, slopes, seqs, rows=256):
    length, pairs = mixed.shape[0] // seqs, mixed.shape[1] // (6 * HD)

    def part(i):
        return pl.BlockSpec((length, 2 * HD), lambda s, p, *_: (s, i * pairs + p))

    return pl.pallas_call(
        partial(attend_kernel, rows=rows, scale=HD**-0.5),
        grid_spec=pltpu.PrefetchScalarGridSpec(
            num_scalar_prefetch=1,
            grid=(seqs, pairs),
            in_specs=[
                pl.BlockSpec((1, length, 1), lambda s, p, *_: (s, 0, 0)),
                part(0),
                part(1),
                part(2),
            ],
            out_specs=[part(0), pl.BlockSpec((1, 2, length), lambda s, p, *_: (s * pairs + p, 0, 0))],
            scratch_shapes=[pltpu.VMEM((length, length), f32)],
        ),
        out_shape=[
            jax.ShapeDtypeStruct((mixed.shape[0], 2 * HD * pairs), bf16),
            jax.ShapeDtypeStruct((seqs * pairs, 2, length), f32),
        ],
        compiler_params=pltpu.CompilerParams(vmem_limit_bytes=VMEM_LIMIT),
        cost_estimate=pl.CostEstimate(
            flops=16 * seqs * pairs * length * length * HD // CHEAP,
            bytes_accessed=4 * mixed.size // CHEAP,
            transcendentals=seqs * pairs * length * length // CHEAP,
        ),
        name="attend_forward",
    )(slopes, starts[:, :, None], mixed, mixed, mixed)


def attend_back_kernel(
    slope_ref,
    start_ref,
    log_ref,
    q_ref,
    k_ref,
    v_ref,
    g_ref,
    dq_ref,
    dk_ref,
    dv_ref,
    qs_ref,
    vs_ref,
    dist_ref,
    ka_ref,
    va_ref,
    *,
    rows,
    scale,
):
    pair = pl.program_id(1)
    length = k_ref.shape[0]

    @pl.when(pair == 0)
    def _():
        for r0 in range(0, length, rows):
            shape = (r0 + rows, rows)
            i = lax.broadcasted_iota(jnp.int32, shape, 1) + r0
            j = lax.broadcasted_iota(jnp.int32, shape, 0)
            allowed = (j <= i) & (j >= start_ref[0, :, r0 : r0 + rows])
            dist_ref[0 : r0 + rows, r0 : r0 + rows] = jnp.where(allowed, (j - i).astype(f32), far)

    slope_a, slope_b = slope_ref[2 * pair] * scale, slope_ref[2 * pair + 1] * scale
    query_sum = jnp.zeros((1, 2 * HD), f32)
    for r0 in reversed(range(0, length, rows)):
        r1 = r0 + rows
        q = pick_heads(q_ref[r0:r1, :] * jnp.asarray(scale, bf16))
        g = pick_heads(g_ref[r0:r1, :])
        k, v = k_ref[0:r1, :], v_ref[0:r1, :]
        s = lax.dot_general(k, q, NT, preferred_element_type=f32)
        d = dist_ref[0:r1, r0:r1]
        logs = jnp.concatenate([log_ref[0, 0:1, r0:r1], log_ref[0, 1:2, r0:r1]], axis=1)
        s = jnp.concatenate([s[:, :rows] + d * slope_a, s[:, rows:] + d * slope_b], axis=1)
        probs = jnp.exp(s - logs)
        t = lax.dot_general(v, g, NT, preferred_element_type=f32)
        centre = jnp.sum(probs * t, axis=0, keepdims=True)
        score_grad = (probs * (t - centre)).astype(bf16)
        value_part = jnp.dot(probs.astype(bf16), g, preferred_element_type=f32)
        key_part = jnp.dot(score_grad, q, preferred_element_type=f32)
        if r1 == length:
            va_ref[...] = value_part
            ka_ref[...] = key_part
        else:
            va_ref[0:r1, :] += value_part
            ka_ref[0:r1, :] += key_part
        dq = lax.dot_general(score_grad, k, TN, preferred_element_type=f32)
        lane = lax.broadcasted_iota(jnp.int32, (rows, 2 * HD), 1)
        dq = (jnp.where(lane < HD, dq[:rows], dq[rows:]) * scale).astype(bf16)
        dq_ref[r0:r1, :] = dq
        query_sum = query_sum + jnp.sum(dq.astype(f32), axis=0, keepdims=True)
    qs_ref[0] = query_sum
    dk_ref[...] = ka_ref[...].astype(bf16)
    dv = va_ref[...].astype(bf16)
    dv_ref[...] = dv
    vs_ref[0] = jnp.sum(dv.astype(f32), axis=0, keepdims=True)


def attend_backward(mixed, grads, starts, logs, slopes, seqs, rows=256):
    length, pairs = mixed.shape[0] // seqs, mixed.shape[1] // (6 * HD)

    def part(i):
        return pl.BlockSpec((length, 2 * HD), lambda s, p, *_: (s, i * pairs + p))

    out = jax.ShapeDtypeStruct(grads.shape, bf16)
    sums = jax.ShapeDtypeStruct((seqs, 1, grads.shape[1]), f32)
    sum_spec = pl.BlockSpec((1, 1, 2 * HD), lambda s, p, *_: (s, 0, p))
    return pl.pallas_call(
        partial(attend_back_kernel, rows=rows, scale=HD**-0.5),
        grid_spec=pltpu.PrefetchScalarGridSpec(
            num_scalar_prefetch=1,
            grid=(seqs, pairs),
            in_specs=[
                pl.BlockSpec((1, 1, length), lambda s, p, *_: (s, 0, 0)),
                pl.BlockSpec((1, 2, length), lambda s, p, *_: (s * pairs + p, 0, 0)),
                part(0),
                part(1),
                part(2),
                part(0),
            ],
            out_specs=[part(0), part(0), part(0), sum_spec, sum_spec],
            scratch_shapes=[
                pltpu.VMEM((length, length), f32),
                pltpu.VMEM((length, 2 * HD), f32),
                pltpu.VMEM((length, 2 * HD), f32),
            ],
        ),
        out_shape=[out, out, out, sums, sums],
        compiler_params=pltpu.CompilerParams(vmem_limit_bytes=VMEM_LIMIT),
        cost_estimate=pl.CostEstimate(
            flops=40 * seqs * pairs * length * length * HD // CHEAP,
            bytes_accessed=14 * grads.size // CHEAP,
            transcendentals=seqs * pairs * length * length // CHEAP,
        ),
        name="attend_backward",
    )(slopes, starts[:, None, :], logs, mixed, mixed, mixed, grads)


def resident(shape):
    return pl.BlockSpec(shape, lambda *_: (0,) * len(shape), pipeline_mode=pl.Buffered(1))


def kept_out(shape):
    return pl.BlockSpec(shape, lambda *_: (0,) * len(shape))


def flat_rows(ws):
    return jnp.concatenate([w[...] for w in ws], axis=0)


def matmul_call(kernel, grid, ins, outs, scratch, flops, name, prefetch=()):
    moved = sum(a.size * a.dtype.itemsize for a, _ in ins)
    moved += sum(jnp.dtype(t).itemsize * math.prod(s) for s, t, _ in outs)
    return pl.pallas_call(
        kernel,
        grid_spec=pltpu.PrefetchScalarGridSpec(
            num_scalar_prefetch=len(prefetch),
            grid=grid,
            in_specs=[s for _, s in ins],
            out_specs=[s for _, _, s in outs],
            scratch_shapes=scratch,
        ),
        out_shape=[jax.ShapeDtypeStruct(s, t) for s, t, _ in outs],
        compiler_params=pltpu.CompilerParams(vmem_limit_bytes=VMEM_LIMIT),
        cost_estimate=pl.CostEstimate(
            flops=flops // CHEAP, bytes_accessed=moved // CHEAP, transcendentals=0
        ),
        name=name,
    )(*prefetch, *[a for a, _ in ins])


def times_rows(x, ws, extras, outs, finish, name, tn, window=None, joins=()):
    tokens, depth = x.shape
    first, width = window or (0, ws[0].shape[1])
    first, tiles = first // tn, width // tn
    n_ws, n_ex, n_out = len(ws), len(extras), len(outs)
    steps = ws[0].shape[1] // tn if joins else tiles

    def kernel(*refs):
        x_ref, w_refs = refs[0], refs[1 : 1 + n_ws]
        extra, out = refs[1 + n_ws : 1 + n_ws + n_ex], refs[1 + n_ws + n_ex :]
        for places, joined in zip(joins, out[n_out:]):
            at = 0
            for i in places:
                joined[at : at + ws[i].shape[0], :] = w_refs[i][...]
                at += ws[i].shape[0]

        def multiply():
            acc = jnp.dot(x_ref[...], flat_rows(w_refs), preferred_element_type=f32)
            finish(acc, extra, out[:n_out])

        if steps == tiles:
            multiply()
        else:
            pl.when(pl.program_id(0) < tiles)(multiply)

    def spec(rows):
        return pl.BlockSpec((rows, tn), lambda n: (0, jnp.minimum(n, tiles - 1)))

    def tile(rows):
        return pl.BlockSpec((rows, tn), lambda n: (0, n + first))

    ins = [(x, resident(x.shape))] + [(w, tile(w.shape[0])) for w in ws]
    ins += [(e, spec(e.shape[0])) for e in extras]
    results = [(s, t, spec(s[0])) for s, t in outs]
    for places in joins:
        rows = sum(ws[i].shape[0] for i in places)
        results.append(((rows, ws[0].shape[1]), bf16, tile(rows)))
    return matmul_call(kernel, (steps,), ins, results, [], 2 * tokens * depth * width, name)


def times_columns(xs, ws, order, side, dtype, name, first=0, added=None, block=0):
    tokens = xs[0].shape[0]
    count = order.shape[1]
    n_xs = len(xs)
    width = sum(x.shape[1] for x in xs)

    def kernel(order_ref, side_ref, *refs):
        x_refs, w_refs, rest, out_ref = refs[:n_xs], refs[n_xs : n_xs + 2], refs[n_xs + 2 :], refs[-1]
        x = jnp.concatenate([r[...] for r in x_refs], axis=1)
        for i, w_ref in enumerate(w_refs):
            acc = lax.dot_general(x, w_ref[...], NT, preferred_element_type=f32)
            place = side_ref[0] if i == 0 else 1 - side_ref[0]
            place = pl.ds(pl.multiple_of(place * BLOCK, BLOCK), BLOCK)
            if added is not None:
                acc = acc + rest[0][:, place].astype(f32)
            out_ref[:, place] = acc.astype(dtype)

    def rows(i):
        return pl.BlockSpec((BLOCK, width), lambda n, order_ref, _: (order_ref[i, n], first // width))

    def pair(start):
        return pl.BlockSpec((tokens, 2 * BLOCK), lambda n, *_: (0, start + n))

    ins = [(x, resident(x.shape)) for x in xs]
    ins += [(w, rows(i)) for i, w in enumerate(ws)]
    ins += [] if added is None else [(added, pair(block))]
    return matmul_call(
        kernel,
        (count,),
        ins,
        [((tokens, 2 * BLOCK * count), dtype, pair(0))],
        [],
        4 * tokens * BLOCK * count * width,
        name,
        prefetch=(order, side),
    )[0]


def weight_rows(a, order, gs, name, added=(), apart=False, dtype=bf16):
    tokens = a.shape[0]
    width = sum(g.shape[1] for g in gs)
    count = order.shape[0]
    n_gs = len(gs)

    def kernel(order_ref, a_ref, *refs):
        g_refs, added_refs = refs[:n_gs], refs[n_gs : n_gs + len(added)]
        out_refs = refs[n_gs + len(added) :]
        g = jnp.concatenate([r[...] for r in g_refs], axis=1)
        acc = lax.dot_general(a_ref[...], g, TN, preferred_element_type=f32)
        if not apart and not added:
            out_refs[0][...] = acc.astype(dtype)
            return
        for i in range(count):

            @pl.when(pl.program_id(0) == i)
            def _(i=i):
                total = acc + added_refs[i][...].astype(f32) if added else acc
                out_refs[i if apart else 0][...] = total.astype(dtype)

    block = pl.BlockSpec((BLOCK, width), lambda i, *_: (i, 0))
    ins = [(a, pl.BlockSpec((tokens, BLOCK), lambda i, order_ref: (0, order_ref[i])))]
    ins += [(g, resident(g.shape)) for g in gs]
    ins += [(b, resident(b.shape)) for b in added]
    if apart:
        outs = [((BLOCK, width), dtype, kept_out((BLOCK, width)))] * count
    else:
        outs = [((count * BLOCK, width), dtype, block)]
    done = matmul_call(
        kernel, (count,), ins, outs, [], 2 * tokens * BLOCK * count * width, name, prefetch=(order,)
    )
    return done if apart else done[0]


def place_blocks(values, place_ref, out_ref):
    at = 0
    for value in values:
        for c0 in range(0, value.shape[1], BLOCK):
            place = pl.ds(pl.multiple_of(place_ref[at] * BLOCK, BLOCK), BLOCK)
            out_ref[:, place] = value[:, c0 : c0 + BLOCK]
            at += 1


def lay_out(parts, places, name, tm=256):
    tokens, width = parts[0].shape
    full = width * len(parts)

    def kernel(place_ref, *refs):
        place_blocks([r[...] for r in refs[:-1]], place_ref, refs[-1])

    return matmul_call(
        kernel,
        (tokens // tm,),
        [(p, pl.BlockSpec((tm, width), lambda m, *_: (m, 0))) for p in parts],
        [((tokens, full), bf16, pl.BlockSpec((tm, full), lambda m, *_: (m, 0)))],
        [],
        tokens * full,
        name,
        prefetch=(places,),
    )[0]


def normalize(parts, gain, shift, places, name, tm=256):
    tokens, width = parts[0].shape
    n = len(parts)
    full = width * n

    def kernel(place_ref, *refs):
        gain_ref, shift_ref, out_ref, mean_ref, scale_ref = refs[n:]
        rows = [r[...].astype(f32) for r in refs[:n]]
        mean = sum(jnp.sum(v, axis=1, keepdims=True) for v in rows) / full
        square = sum(jnp.sum(v * v, axis=1, keepdims=True) for v in rows) / full
        scale = lax.rsqrt(square - mean * mean + norm_eps)
        mean_ref[...] = mean
        scale_ref[...] = scale
        done = []
        for i, v in enumerate(rows):
            cols = slice(i * width, (i + 1) * width)
            done.append(((v - mean) * scale * gain_ref[:, cols] + shift_ref[:, cols]).astype(bf16))
        place_blocks(done, place_ref, out_ref)

    ins = [(p, pl.BlockSpec((tm, width), lambda m, *_: (m, 0))) for p in parts]
    ins += [(gain, resident(gain.shape)), (shift, resident(shift.shape))]
    column = pl.BlockSpec((tm, 1), lambda m, *_: (m, 0))
    return matmul_call(
        kernel,
        (tokens // tm,),
        ins,
        [
            ((tokens, full), bf16, pl.BlockSpec((tm, full), lambda m, *_: (m, 0))),
            ((tokens, 1), f32, column),
            ((tokens, 1), f32, column),
        ],
        [],
        8 * tokens * full,
        name,
        prefetch=(places,),
    )


def swap(x, axis, bit):
    return lax.ppermute(x, axis, [(i, i ^ bit) for i in range(lax.axis_size(axis))])


def turn(x, steps):
    count = lax.axis_size("row")
    return lax.ppermute(x, "row", [(i, (i + 2 * steps) % count) for i in range(count)])


def sum_col_stats(stats):
    stats = stats + swap(stats, "col", 1)
    return stats + swap(stats, "col", 2)


def sum_rows(x):
    bit = 1
    while bit < lax.axis_size("row"):
        x = x + swap(x, "row", bit)
        bit *= 2
    return x


def after(x, *first):
    return lax.optimization_barrier((x,) + first)[0] if first else x


def outer_groups():
    outer = lax.axis_size("row") // 2
    return [[2 * i + inner for i in range(outer)] for inner in range(2)]


def find(ids, wanted):
    at = jnp.arange(ids.shape[0])
    return jnp.sum(jnp.where(ids[None, :] == wanted[:, None], at[None, :], 0), axis=1).astype(
        jnp.int32
    )


def gather_whole(w):
    return [lax.all_gather(w, "row", axis=0, tiled=True)]


def gather_outer(w):
    return lax.all_gather(w, "row", axis=0, tiled=True, axis_index_groups=outer_groups())


class Clock:
    def __init__(self):
        self.now, self.new = [], []

    def at(self, x):
        return after(x, *self.now)

    def put(self, *xs):
        self.new += xs

    def tick(self):
        self.now, self.new = self.new, []


def on_device(
    tokens,
    segments,
    gains,
    shifts,
    biases,
    mixing,
    projection,
    expand,
    thresholds,
    contract,
    cotangent,
):
    seqs = segments.shape[0]
    rows, cols = lax.axis_size("row"), lax.axis_size("col")
    row, col = lax.axis_index("row"), lax.axis_index("col")
    tokens_here, width = tokens.shape
    full = width * cols
    heads = width // HD
    stepped = full // rows == BLOCK and rows == 2 * cols
    blocks, per_col = full // BLOCK, width // BLOCK
    at = jnp.arange(blocks)
    ours = per_col * ((at // per_col) ^ col) + at % per_col
    place, side = row // 2, row % 2
    steps = jnp.arange(max(rows // 2, 1))
    back = (place - steps) % (rows // 2)
    if stepped:
        ids_attend = jnp.concatenate([2 * back + side, 2 * back + 1 - side])
        ids_expand = jnp.concatenate([2 * steps + side, 2 * steps + 1 - side])
        ids_contract = jnp.stack([2 * steps + side, 2 * steps + 1 - side], axis=1).reshape(-1)
    else:
        ids_attend = ids_expand = ids_contract = at
        side = 0 * side
    sides = jnp.reshape(side, (1,)).astype(jnp.int32)
    away = jnp.array([1, 3, 0, 2]) ^ col
    clock = Clock()
    at_now, put, tick = clock.at, clock.put, clock.tick

    def columns_order(ids, ws):
        want = jnp.stack([2 * away + side, 2 * away + 1 - side]).reshape(-1)
        order = find(ids, want).reshape(2, -1)
        return order if len(ws) == 1 else order % (blocks // 2)

    def two(ws):
        return ws if len(ws) == 2 else [ws[0], ws[0]]

    def columns_sent(xs, ws, ids, name, first=0):
        order = columns_order(ids, ws)
        xs = [at_now(xs[0])] + xs[1:]
        sent = times_columns(xs, two(ws), order[:, :2], sides, bf16, name + "_sent", first)
        return swap(sent, "col", 1)

    def columns_part(xs, ws, ids, got, name, first=0):
        order = columns_order(ids, ws)[:, 3:]
        return times_columns(xs, two(ws), order, sides, bf16, name + "_part", first, got, 1)

    def columns_base(xs, ws, ids, got, name, first=0):
        order = columns_order(ids, ws)[:, 2:3]
        xs = [at_now(xs[0])] + xs[1:]
        return times_columns(xs, two(ws), order, sides, f32, name + "_base", first, got, 0)

    def weight_other(a, ids, gs, name):
        if not stepped:
            return [weight_rows(at_now(a), find(ids, at), gs, name, dtype=f32)]
        other = find(ids, 2 * steps + 1 - side)
        return weight_rows(at_now(a), other, gs, name + "_other", apart=True)

    def move(parts, k):
        return swap(at_now(parts[k]), "row", 1) if stepped else parts[0]

    def weight_mine(a, ids, gs, got, name):
        if not stepped:
            return lax.psum_scatter(got[0], "row", scatter_dimension=0, tiled=True)
        mine = find(ids, 2 * steps + side)
        total = weight_rows(at_now(a), mine, gs, name + "_mine", got)
        return lax.psum_scatter(
            total, "row", scatter_dimension=0, tiled=True, axis_index_groups=outer_groups()
        ).astype(f32)

    head_ids = (col * heads + jnp.arange(heads)).astype(f32)
    slopes = jnp.exp2(-8.0 * (head_ids + 1.0) / (heads * cols))
    starts = jnp.sum(segments[:, None, :] < segments[:, :, None], axis=2).astype(jnp.int32)
    places_attend, places_expand = find(ids_attend, ours), find(ids_expand, ours)
    places_contract = find(ids_contract, ours)
    mix_width = 3 * width
    mixed_bias = jnp.concatenate([biases[0:1], jnp.zeros((1, width), f32), biases[1:2]], axis=1)

    attend_rows = jnp.concatenate([mixing.reshape(mixing.shape[0], -1), projection], axis=1)
    small = jnp.concatenate([gains, shifts], axis=0)
    put(attend_rows)
    tick()
    if stepped:
        own, near = [attend_rows], []
    else:
        whole = gather_whole(attend_rows)[0]
        own, near = [whole[: full // 2]], [whole[full // 2 :]]
        full_expand = gather_whole(expand)
        full_contract = gather_whole(contract)

    def weight_step(k):
        if stepped:
            ready = at_now(own[k])
            near.append(swap(ready, "row", 1))
            put(near[k])
            if k + 1 < rows // 2:
                own.append(turn(ready, 1))
                put(own[k + 1])

    weight_step(0)
    tokens_now = at_now(tokens)
    token_parts = [tokens, swap(tokens_now, "col", 1), swap(tokens_now, "col", 2)]
    put(*token_parts[1:])
    tick()

    weight_step(1)
    cot_now = at_now(cotangent)
    cot_parts = [cotangent, swap(cot_now, "col", 1), swap(cot_now, "col", 2)]
    token_parts.append(swap(at_now(token_parts[2]), "col", 1))
    put(*cot_parts[1:], token_parts[3])
    if stepped:
        expand_mine = gather_outer(at_now(expand))
    tick()

    weight_step(2)
    small_now = at_now(small)
    norms = [small, swap(small_now, "col", 1), swap(small_now, "col", 2)]
    cot_parts.append(swap(at_now(cot_parts[2]), "col", 1))
    put(*norms[1:], cot_parts[3])
    tick()

    weight_step(3)
    norms.append(swap(at_now(norms[2]), "col", 1))
    norms = jnp.concatenate(norms, axis=1)
    first_full, first_mean, first_scale = normalize(
        token_parts, norms[0:1], norms[2:3], places_attend, "first_norm"
    )
    cot_full = lay_out([at_now(cot_parts[0])] + cot_parts[1:], places_contract, "cotangent_rows")
    put(first_full, cot_full)
    tick()

    def add_bias(acc, extra, out):
        out[0][...] = (acc + extra[0][...]).astype(bf16)

    if stepped:
        contract_pair = jnp.concatenate([contract, swap(at_now(contract), "row", 1)], axis=0)
        put(contract_pair, expand_mine)
    mixed, *full_attend = times_rows(
        at_now(first_full),
        own + near,
        [mixed_bias],
        [((tokens_here, mix_width), bf16)],
        add_bias,
        "mix",
        tn=width,
        window=(0, mix_width),
        joins=[range(len(own)), range(len(own), len(own) + len(near))],
    )
    attended, logs = attend_forward(mixed, starts, slopes, seqs)
    put(attended)
    tick()

    if stepped:
        full_contract = [gather_outer(at_now(contract_pair))]
        expand_near = []

    def expand_step(k):
        if stepped:
            block = expand_mine[k * BLOCK : (k + 1) * BLOCK]
            expand_near.append(swap(at_now(block), "row", 1))
            put(expand_near[k])

    expand_step(0)
    got = columns_sent([attended], full_attend, ids_attend, "project", mix_width)
    part = columns_part([attended], full_attend, ids_attend, got, "project", mix_width)
    put(part)
    tick()

    expand_step(1)
    across = swap(at_now(part), "col", 2)
    base = columns_base([attended], full_attend, ids_attend, got, "project", mix_width)
    resid = tokens.astype(f32)
    middle = resid + (base + across.astype(f32) + biases[2])
    middle_low = middle.astype(bf16)
    put(middle_low)
    tick()

    expand_step(2)
    middle_now = at_now(middle_low)
    middle_parts = [middle_low, swap(middle_now, "col", 1), swap(middle_now, "col", 2)]
    put(*middle_parts[1:])
    tick()

    expand_step(3)
    middle_parts.append(swap(at_now(middle_parts[2]), "col", 1))
    second_full, second_mean, second_scale = normalize(
        middle_parts, norms[1:2], norms[3:4], places_expand, "second_norm"
    )
    put(second_full)
    tick()

    def activate(acc, extra, out):
        hidden = acc + extra[0][...]
        bell = 0.5 * (1.0 + lax.erf(hidden * sqrt_half))
        out[0][...] = (hidden * bell).astype(bf16)
        out[1][...] = bell + hidden * (jnp.exp(-0.5 * hidden * hidden) * inverse_root)

    hidden_shape = (tokens_here, expand.shape[1])
    active, slope, *joined = times_rows(
        at_now(second_full),
        [expand_mine] + expand_near if stepped else full_expand,
        [thresholds[None]],
        [(hidden_shape, bf16), (hidden_shape, f32)],
        activate,
        "expand",
        tn=512,
        joins=[range(1, 1 + rows // 2)] if stepped else [],
    )
    if stepped:
        full_expand = [expand_mine] + joined
    contract_other = weight_other(cot_full, ids_contract, [active], "contract_grad")
    put(active, *contract_other)
    tick()

    contract_got = [move(contract_other, 0)]
    put(contract_got[0], *full_contract)
    tick()

    def back_activate(acc, extra, out):
        grad = (acc * extra[0][...]).astype(bf16)
        out[0][...] = grad
        out[1][...] = jnp.sum(grad.astype(f32), axis=0, keepdims=True)

    contract_got.append(move(contract_other, 1))
    hidden_grad, thresholds_part = times_rows(
        at_now(cot_full),
        full_contract,
        [slope],
        [(hidden_shape, bf16), ((1, hidden_shape[1]), f32)],
        back_activate,
        "contract_back",
        tn=512,
    )
    got = columns_sent([hidden_grad], full_expand, ids_expand, "expand_back")
    part = columns_part([hidden_grad], full_expand, ids_expand, got, "expand_back")
    put(contract_got[1], part)
    tick()

    contract_got.append(move(contract_other, 2))
    across = swap(at_now(part), "col", 2)
    base = columns_base([hidden_grad], full_expand, ids_expand, got, "expand_back")
    expand_other = weight_other(second_full, ids_expand, [hidden_grad], "expand_grad")
    second_back = base + across.astype(f32)
    put(contract_got[2], second_back, *expand_other)
    tick()

    def norm_back(upstream, centred, scale, gain):
        scaled = upstream * gain
        sums = sum_col_stats(
            jnp.stack([jnp.sum(scaled, axis=1), jnp.sum(scaled * centred, axis=1)])
        )
        result = scale * (
            scaled - sums[0][:, None] / full - centred * (sums[1][:, None] / full)
        )
        return result, jnp.sum(upstream * centred, axis=0), jnp.sum(upstream, axis=0)

    contract_got.append(move(contract_other, 3))
    second_centred = (middle - second_mean) * second_scale
    second_input, second_gain, second_shift = norm_back(
        at_now(second_back), second_centred, second_scale, gains[1]
    )
    cot_float = cotangent.astype(f32)
    middle_grad = cot_float + second_input
    branch_grad = middle_grad.astype(bf16)
    branch_parts = [branch_grad, swap(branch_grad, "col", 1), swap(branch_grad, "col", 2)]
    out_got = columns_sent([after(active, branch_grad)], full_contract, ids_contract, "contract")
    put(contract_got[3], *branch_parts[1:])
    tick()

    def store(acc, extra, out):
        out[0][...] = acc.astype(bf16)

    expand_got = [move(expand_other, 0)]
    branch_parts.append(swap(at_now(branch_parts[2]), "col", 1))
    contract_grad = weight_mine(cot_full, ids_contract, [active], contract_got, "contract_grad")
    branch_full = lay_out(branch_parts, places_attend, "branch_rows")
    (attended_grad,) = times_rows(
        branch_full,
        full_attend,
        [],
        [((tokens_here, width), bf16)],
        store,
        "project_back",
        tn=width,
        window=(mix_width, width),
    )
    project_other = weight_other(branch_full, ids_attend, [attended], "projection_grad")
    put(expand_got[0], attended_grad, project_other[0])
    tick()

    expand_got.append(move(expand_other, 1))
    query_back, key_back, value_back, query_sum, value_sum = attend_backward(
        mixed, at_now(attended_grad), starts, logs, slopes, seqs
    )
    mixed_grads = [query_back, key_back, value_back]
    put(expand_got[1], query_back)
    tick()

    expand_got.append(move(expand_other, 2))
    got = columns_sent(mixed_grads, full_attend, ids_attend, "mix_back")
    if stepped:
        mine, other = find(ids_attend, 2 * back + side), find(ids_attend, 2 * back + 1 - side)
        mixing_other = [
            weight_rows(at_now(first_full), other[k : k + 2], mixed_grads, "mixing_grad_other")
            for k in range(0, rows // 2, 2)
        ]
    else:
        mixing_other = weight_other(first_full, ids_attend, mixed_grads, "mixing_grad")
    part = columns_part(mixed_grads, full_attend, ids_attend, got, "mix_back")
    put(expand_got[2], part, *mixing_other)
    tick()

    expand_got.append(move(expand_other, 3))
    across = swap(at_now(part), "col", 2)
    base = columns_base(mixed_grads, full_attend, ids_attend, got, "mix_back")
    out_part = columns_part(
        [at_now(active)], full_contract, ids_contract, out_got, "contract"
    )
    first_back = base + across.astype(f32)
    put(expand_got[3], first_back, out_part)
    tick()

    project_got = [swap(at_now(v), "row", 1) for v in project_other] if stepped else project_other
    expand_grad = weight_mine(second_full, ids_expand, [hidden_grad], expand_got, "expand_grad")
    first_centred = (resid - first_mean) * first_scale
    first_input, first_gain, first_shift = norm_back(
        at_now(first_back), first_centred, first_scale, gains[0]
    )
    tokens_grad = middle_grad + first_input
    out_across = swap(at_now(out_part), "col", 2)
    out_base = columns_base([active], full_contract, ids_contract, out_got, "contract")
    small = jnp.stack(
        [
            first_gain,
            second_gain,
            first_shift,
            second_shift,
            jnp.sum(query_sum, axis=(0, 1)),
            jnp.sum(value_sum, axis=(0, 1)),
            jnp.sum(branch_grad.astype(f32), axis=0),
            jnp.sum(cot_float, axis=0),
        ]
    )
    small = jnp.concatenate([small, thresholds_part.reshape(-1, width)], axis=0)
    put(small, out_base, out_across, *project_got)
    tick()

    layer_out = (middle + (out_base + out_across.astype(f32) + biases[3])).astype(bf16)
    projection_grad = weight_mine(
        branch_full, ids_attend, [attended], project_got, "projection_grad"
    )
    if stepped:
        far = swap(at_now(mixing_other[1]), "row", 1)
        small = sum_rows(at_now(small))
        put(far, small)
        tick()

        def mixing_mine(k, got):
            parts = [got[:BLOCK], got[BLOCK:]]
            return weight_rows(
                first_full, mine[k : k + 2], mixed_grads, "mixing_grad_mine", parts, True
            )

        nearer = swap(at_now(mixing_other[0]), "row", 1)
        terms = mixing_mine(2, at_now(far))
        terms = [turn(terms[1], -3), turn(terms[0], -2)]
        put(nearer, *terms)
        tick()
        own_term, step_term = mixing_mine(0, at_now(nearer))
        terms += [turn(step_term, -1), own_term]
        mixing_grad = sum(t.astype(f32) for t in terms)
    else:
        small = sum_rows(at_now(small))
        mixing_grad = weight_mine(None, None, None, mixing_other, None)
    mixing_grad = jnp.stack(
        [mixing_grad[:, i * width : (i + 1) * width] for i in range(3)], axis=1
    )
    return (
        layer_out,
        tokens_grad,
        small[0:2],
        small[2:4],
        small[4:8],
        mixing_grad,
        projection_grad,
        expand_grad,
        small[8:].reshape(thresholds.shape),
        contract_grad,
    )


def solution(mesh):
    return jax.shard_map(
        on_device,
        mesh=mesh,
        in_specs=(
            P("row", "col"),
            P("row", None),
            P(None, "col"),
            P(None, "col"),
            P(None, "col"),
            P("row", None, "col"),
            P("row", "col"),
            P("row", "col"),
            P("col"),
            P("row", "col"),
            P("row", "col"),
        ),
        out_specs=(
            P("row", "col"),
            P("row", "col"),
            P(None, "col"),
            P(None, "col"),
            P(None, "col"),
            P("row", None, "col"),
            P("row", "col"),
            P("row", "col"),
            P("col"),
            P("row", "col"),
        ),
        check_vma=False,
    )
```

```python
import math
from functools import partial

import jax
import jax.numpy as jnp
from jax import lax
from jax.experimental import pallas as pl
from jax.experimental.pallas import tpu as pltpu
from jax.sharding import PartitionSpec as P

HD = 64
BLOCK = 256

norm_eps = 1e-05
sqrt_half = 0.7071067811865476
inverse_root = 0.3989422804014327
far = -1e33
NT = (((1,), (1,)), ((), ()))
TN = (((0,), (0,)), ((), ()))
VMEM_LIMIT = 56 << 20
CHEAP = 64
f32 = jnp.float32
bf16 = jnp.bfloat16


def pick_heads(pair):
    lane = lax.broadcasted_iota(jnp.int32, pair.shape, 1)
    zero = jnp.zeros_like(pair)
    return jnp.concatenate(
        [jnp.where(lane < HD, pair, zero), jnp.where(lane < HD, zero, pair)], axis=0
    )


def attend_kernel(
    slope_ref, start_ref, q_ref, k_ref, v_ref, out_ref, log_ref, dist_ref, *, rows, scale
):
    pair = pl.program_id(1)
    length = k_ref.shape[0]

    @pl.when(pair == 0)
    def _():
        for r0 in range(0, length, rows):
            shape = (rows, r0 + rows)
            i = lax.broadcasted_iota(jnp.int32, shape, 0) + r0
            j = lax.broadcasted_iota(jnp.int32, shape, 1)
            allowed = (j <= i) & (j >= start_ref[0, r0 : r0 + rows, :])
            dist_ref[r0 : r0 + rows, 0 : r0 + rows] = jnp.where(allowed, (j - i).astype(f32), far)

    slope_a, slope_b = slope_ref[2 * pair] * scale, slope_ref[2 * pair + 1] * scale
    for r0 in range(0, length, rows):
        r1 = r0 + rows
        q = pick_heads(q_ref[r0:r1, :] * jnp.asarray(scale, bf16))
        s = lax.dot_general(q, k_ref[0:r1, :], NT, preferred_element_type=f32)
        d = dist_ref[r0:r1, 0:r1]
        s = jnp.concatenate([s[:rows] + d * slope_a, s[rows:] + d * slope_b], axis=0)
        row_max = jnp.max(s, axis=1, keepdims=True)
        weights = jnp.exp(s - row_max)
        row_total = jnp.sum(weights, axis=1, keepdims=True)
        probs = (weights * (1.0 / row_total)).astype(bf16)
        o = jnp.dot(probs, v_ref[0:r1, :], preferred_element_type=f32)
        lane = lax.broadcasted_iota(jnp.int32, (rows, 2 * HD), 1)
        out_ref[r0:r1, :] = jnp.where(lane < HD, o[:rows], o[rows:]).astype(bf16)
        logs = row_max + jnp.log(row_total)
        logs = jnp.where(
            lane < HD,
            jnp.broadcast_to(logs[:rows], (rows, 2 * HD)),
            jnp.broadcast_to(logs[rows:], (rows, 2 * HD)),
        ).T
        log_ref[0, 0:1, r0:r1] = logs[0:1]
        log_ref[0, 1:2, r0:r1] = logs[HD : HD + 1]


def attend_forward(mixed, starts, slopes, seqs, rows=256):
    length, pairs = mixed.shape[0] // seqs, mixed.shape[1] // (6 * HD)

    def part(i):
        return pl.BlockSpec((length, 2 * HD), lambda s, p, *_: (s, i * pairs + p))

    return pl.pallas_call(
        partial(attend_kernel, rows=rows, scale=HD**-0.5),
        grid_spec=pltpu.PrefetchScalarGridSpec(
            num_scalar_prefetch=1,
            grid=(seqs, pairs),
            in_specs=[
                pl.BlockSpec((1, length, 1), lambda s, p, *_: (s, 0, 0)),
                part(0),
                part(1),
                part(2),
            ],
            out_specs=[part(0), pl.BlockSpec((1, 2, length), lambda s, p, *_: (s * pairs + p, 0, 0))],
            scratch_shapes=[pltpu.VMEM((length, length), f32)],
        ),
        out_shape=[
            jax.ShapeDtypeStruct((mixed.shape[0], 2 * HD * pairs), bf16),
            jax.ShapeDtypeStruct((seqs * pairs, 2, length), f32),
        ],
        compiler_params=pltpu.CompilerParams(vmem_limit_bytes=VMEM_LIMIT),
        cost_estimate=pl.CostEstimate(
            flops=16 * seqs * pairs * length * length * HD // CHEAP,
            bytes_accessed=4 * mixed.size // CHEAP,
            transcendentals=seqs * pairs * length * length // CHEAP,
        ),
        name="attend_forward",
    )(slopes, starts[:, :, None], mixed, mixed, mixed)


def attend_back_kernel(
    slope_ref,
    start_ref,
    log_ref,
    q_ref,
    k_ref,
    v_ref,
    g_ref,
    dq_ref,
    dk_ref,
    dv_ref,
    qs_ref,
    vs_ref,
    dist_ref,
    ka_ref,
    va_ref,
    *,
    rows,
    scale,
):
    pair = pl.program_id(1)
    length = k_ref.shape[0]

    @pl.when(pair == 0)
    def _():
        for r0 in range(0, length, rows):
            shape = (r0 + rows, rows)
            i = lax.broadcasted_iota(jnp.int32, shape, 1) + r0
            j = lax.broadcasted_iota(jnp.int32, shape, 0)
            allowed = (j <= i) & (j >= start_ref[0, :, r0 : r0 + rows])
            dist_ref[0 : r0 + rows, r0 : r0 + rows] = jnp.where(allowed, (j - i).astype(f32), far)

    slope_a, slope_b = slope_ref[2 * pair] * scale, slope_ref[2 * pair + 1] * scale
    query_sum = jnp.zeros((1, 2 * HD), f32)
    for r0 in reversed(range(0, length, rows)):
        r1 = r0 + rows
        q = pick_heads(q_ref[r0:r1, :] * jnp.asarray(scale, bf16))
        g = pick_heads(g_ref[r0:r1, :])
        k, v = k_ref[0:r1, :], v_ref[0:r1, :]
        s = lax.dot_general(k, q, NT, preferred_element_type=f32)
        d = dist_ref[0:r1, r0:r1]
        logs = jnp.concatenate([log_ref[0, 0:1, r0:r1], log_ref[0, 1:2, r0:r1]], axis=1)
        s = jnp.concatenate([s[:, :rows] + d * slope_a, s[:, rows:] + d * slope_b], axis=1)
        probs = jnp.exp(s - logs)
        t = lax.dot_general(v, g, NT, preferred_element_type=f32)
        centre = jnp.sum(probs * t, axis=0, keepdims=True)
        score_grad = (probs * (t - centre)).astype(bf16)
        value_part = jnp.dot(probs.astype(bf16), g, preferred_element_type=f32)
        key_part = jnp.dot(score_grad, q, preferred_element_type=f32)
        if r1 == length:
            va_ref[...] = value_part
            ka_ref[...] = key_part
        else:
            va_ref[0:r1, :] += value_part
            ka_ref[0:r1, :] += key_part
        dq = lax.dot_general(score_grad, k, TN, preferred_element_type=f32)
        lane = lax.broadcasted_iota(jnp.int32, (rows, 2 * HD), 1)
        dq = (jnp.where(lane < HD, dq[:rows], dq[rows:]) * scale).astype(bf16)
        dq_ref[r0:r1, :] = dq
        query_sum = query_sum + jnp.sum(dq.astype(f32), axis=0, keepdims=True)
    qs_ref[0] = query_sum
    dk_ref[...] = ka_ref[...].astype(bf16)
    dv = va_ref[...].astype(bf16)
    dv_ref[...] = dv
    vs_ref[0] = jnp.sum(dv.astype(f32), axis=0, keepdims=True)


def attend_backward(mixed, grads, starts, logs, slopes, seqs, rows=256):
    length, pairs = mixed.shape[0] // seqs, mixed.shape[1] // (6 * HD)

    def part(i):
        return pl.BlockSpec((length, 2 * HD), lambda s, p, *_: (s, i * pairs + p))

    out = jax.ShapeDtypeStruct(grads.shape, bf16)
    sums = jax.ShapeDtypeStruct((seqs, 1, grads.shape[1]), f32)
    sum_spec = pl.BlockSpec((1, 1, 2 * HD), lambda s, p, *_: (s, 0, p))
    return pl.pallas_call(
        partial(attend_back_kernel, rows=rows, scale=HD**-0.5),
        grid_spec=pltpu.PrefetchScalarGridSpec(
            num_scalar_prefetch=1,
            grid=(seqs, pairs),
            in_specs=[
                pl.BlockSpec((1, 1, length), lambda s, p, *_: (s, 0, 0)),
                pl.BlockSpec((1, 2, length), lambda s, p, *_: (s * pairs + p, 0, 0)),
                part(0),
                part(1),
                part(2),
                part(0),
            ],
            out_specs=[part(0), part(0), part(0), sum_spec, sum_spec],
            scratch_shapes=[
                pltpu.VMEM((length, length), f32),
                pltpu.VMEM((length, 2 * HD), f32),
                pltpu.VMEM((length, 2 * HD), f32),
            ],
        ),
        out_shape=[out, out, out, sums, sums],
        compiler_params=pltpu.CompilerParams(vmem_limit_bytes=VMEM_LIMIT),
        cost_estimate=pl.CostEstimate(
            flops=40 * seqs * pairs * length * length * HD // CHEAP,
            bytes_accessed=14 * grads.size // CHEAP,
            transcendentals=seqs * pairs * length * length // CHEAP,
        ),
        name="attend_backward",
    )(slopes, starts[:, None, :], logs, mixed, mixed, mixed, grads)


def resident(shape):
    return pl.BlockSpec(shape, lambda *_: (0,) * len(shape), pipeline_mode=pl.Buffered(1))


def kept_out(shape):
    return pl.BlockSpec(shape, lambda *_: (0,) * len(shape))


def flat_rows(ws):
    return jnp.concatenate([w[...] for w in ws], axis=0)


def matmul_call(kernel, grid, ins, outs, scratch, flops, name, prefetch=()):
    moved = sum(a.size * a.dtype.itemsize for a, _ in ins)
    moved += sum(jnp.dtype(t).itemsize * math.prod(s) for s, t, _ in outs)
    return pl.pallas_call(
        kernel,
        grid_spec=pltpu.PrefetchScalarGridSpec(
            num_scalar_prefetch=len(prefetch),
            grid=grid,
            in_specs=[s for _, s in ins],
            out_specs=[s for _, _, s in outs],
            scratch_shapes=scratch,
        ),
        out_shape=[jax.ShapeDtypeStruct(s, t) for s, t, _ in outs],
        compiler_params=pltpu.CompilerParams(vmem_limit_bytes=VMEM_LIMIT),
        cost_estimate=pl.CostEstimate(
            flops=flops // CHEAP, bytes_accessed=moved // CHEAP, transcendentals=0
        ),
        name=name,
    )(*prefetch, *[a for a, _ in ins])


def times_rows(x, ws, extras, outs, finish, name, tn, window=None, joins=()):
    tokens, depth = x.shape
    first, width = window or (0, ws[0].shape[1])
    first, tiles = first // tn, width // tn
    n_ws, n_ex, n_out = len(ws), len(extras), len(outs)
    steps = ws[0].shape[1] // tn if joins else tiles

    def kernel(*refs):
        x_ref, w_refs = refs[0], refs[1 : 1 + n_ws]
        extra, out = refs[1 + n_ws : 1 + n_ws + n_ex], refs[1 + n_ws + n_ex :]
        for places, joined in zip(joins, out[n_out:]):
            at = 0
            for i in places:
                joined[at : at + ws[i].shape[0], :] = w_refs[i][...]
                at += ws[i].shape[0]

        def multiply():
            acc = jnp.dot(x_ref[...], flat_rows(w_refs), preferred_element_type=f32)
            finish(acc, extra, out[:n_out])

        if steps == tiles:
            multiply()
        else:
            pl.when(pl.program_id(0) < tiles)(multiply)

    def spec(rows):
        return pl.BlockSpec((rows, tn), lambda n: (0, jnp.minimum(n, tiles - 1)))

    def tile(rows):
        return pl.BlockSpec((rows, tn), lambda n: (0, n + first))

    ins = [(x, resident(x.shape))] + [(w, tile(w.shape[0])) for w in ws]
    ins += [(e, spec(e.shape[0])) for e in extras]
    results = [(s, t, spec(s[0])) for s, t in outs]
    for places in joins:
        rows = sum(ws[i].shape[0] for i in places)
        results.append(((rows, ws[0].shape[1]), bf16, tile(rows)))
    return matmul_call(kernel, (steps,), ins, results, [], 2 * tokens * depth * width, name)


def times_columns(xs, ws, order, side, dtype, name, first=0, added=(), block=0, chunks=1):
    tokens = xs[0].shape[0]
    count = order.shape[1]
    n_xs = len(xs)
    width = sum(x.shape[1] for x in xs)
    rows = tokens // chunks

    def kernel(order_ref, side_ref, *refs):
        x_refs, w_refs = refs[:n_xs], refs[n_xs : n_xs + 2]
        added_refs, out_refs = refs[n_xs + 2 : n_xs + 2 + len(added)], refs[-chunks:]
        x = jnp.concatenate([r[...] for r in x_refs], axis=1)
        for i, w_ref in enumerate(w_refs):
            acc = lax.dot_general(x, w_ref[...], NT, preferred_element_type=f32)
            place = side_ref[0] if i == 0 else 1 - side_ref[0]
            place = pl.ds(pl.multiple_of(place * BLOCK, BLOCK), BLOCK)
            if added:
                acc = acc + jnp.concatenate([r[:, place] for r in added_refs]).astype(f32)
            for c, out_ref in enumerate(out_refs):
                out_ref[:, place] = acc[c * rows : (c + 1) * rows].astype(dtype)

    def w_spec(i):
        return pl.BlockSpec((BLOCK, width), lambda n, order_ref, _: (order_ref[i, n], first // width))

    def pair(height, start):
        return pl.BlockSpec((height, 2 * BLOCK), lambda n, *_: (0, start + n))

    ins = [(x, resident(x.shape)) for x in xs]
    ins += [(w, w_spec(i)) for i, w in enumerate(ws)]
    ins += [(b, pair(b.shape[0], block)) for b in added]
    done = matmul_call(
        kernel,
        (count,),
        ins,
        [((rows, 2 * BLOCK * count), dtype, pair(rows, 0))] * chunks,
        [],
        4 * tokens * BLOCK * count * width,
        name,
        prefetch=(order, side),
    )
    return done if chunks > 1 else done[0]


def weight_rows(a, order, gs, name, groups=None, dtype=bf16):
    tokens = a.shape[0]
    width = sum(g.shape[1] for g in gs)
    count = order.shape[0]
    n_gs = len(gs)

    def kernel(order_ref, a_ref, *refs):
        g_refs, out_refs = refs[:n_gs], refs[n_gs:]
        g = jnp.concatenate([r[...] for r in g_refs], axis=1)
        acc = lax.dot_general(a_ref[...], g, TN, preferred_element_type=f32).astype(dtype)
        if groups is None:
            out_refs[0][...] = acc
            return
        for out_ref, group in zip(out_refs, groups):
            for j, i in enumerate(group):

                @pl.when(pl.program_id(0) == i)
                def _(out_ref=out_ref, rows=slice(j * BLOCK, (j + 1) * BLOCK)):
                    out_ref[rows, :] = acc

    ins = [(a, pl.BlockSpec((tokens, BLOCK), lambda i, order_ref: (0, order_ref[i])))]
    ins += [(g, resident(g.shape)) for g in gs]
    if groups is None:
        outs = [((count * BLOCK, width), dtype, pl.BlockSpec((BLOCK, width), lambda i, *_: (i, 0)))]
    else:
        shapes = [(len(group) * BLOCK, width) for group in groups]
        outs = [(shape, dtype, kept_out(shape)) for shape in shapes]
    done = matmul_call(
        kernel, (count,), ins, outs, [], 2 * tokens * BLOCK * count * width, name, prefetch=(order,)
    )
    return done[0] if groups is None else done


def place_blocks(values, place_ref, out_ref):
    at = 0
    for value in values:
        for c0 in range(0, value.shape[1], BLOCK):
            place = pl.ds(pl.multiple_of(place_ref[at] * BLOCK, BLOCK), BLOCK)
            out_ref[:, place] = value[:, c0 : c0 + BLOCK]
            at += 1


def lay_out(parts, places, name, tm=256):
    tokens, width = parts[0].shape
    full = width * len(parts)

    def kernel(place_ref, *refs):
        place_blocks([r[...] for r in refs[:-1]], place_ref, refs[-1])

    return matmul_call(
        kernel,
        (tokens // tm,),
        [(p, pl.BlockSpec((tm, width), lambda m, *_: (m, 0))) for p in parts],
        [((tokens, full), bf16, pl.BlockSpec((tm, full), lambda m, *_: (m, 0)))],
        [],
        tokens * full,
        name,
        prefetch=(places,),
    )[0]


def normalize(parts, gain, shift, places, name, tm=256):
    tokens, width = parts[0].shape
    n = len(parts)
    full = width * n

    def kernel(place_ref, *refs):
        gain_ref, shift_ref, out_ref, mean_ref, scale_ref = refs[n:]
        rows = [r[...].astype(f32) for r in refs[:n]]
        mean = sum(jnp.sum(v, axis=1, keepdims=True) for v in rows) / full
        square = sum(jnp.sum(v * v, axis=1, keepdims=True) for v in rows) / full
        scale = lax.rsqrt(square - mean * mean + norm_eps)
        mean_ref[...] = mean
        scale_ref[...] = scale
        done = []
        for i, v in enumerate(rows):
            cols = slice(i * width, (i + 1) * width)
            done.append(((v - mean) * scale * gain_ref[:, cols] + shift_ref[:, cols]).astype(bf16))
        place_blocks(done, place_ref, out_ref)

    ins = [(p, pl.BlockSpec((tm, width), lambda m, *_: (m, 0))) for p in parts]
    ins += [(gain, resident(gain.shape)), (shift, resident(shift.shape))]
    column = pl.BlockSpec((tm, 1), lambda m, *_: (m, 0))
    return matmul_call(
        kernel,
        (tokens // tm,),
        ins,
        [
            ((tokens, full), bf16, pl.BlockSpec((tm, full), lambda m, *_: (m, 0))),
            ((tokens, 1), f32, column),
            ((tokens, 1), f32, column),
        ],
        [],
        8 * tokens * full,
        name,
        prefetch=(places,),
    )


def swap(x, axis, bit):
    return lax.ppermute(x, axis, [(i, i ^ bit) for i in range(lax.axis_size(axis))])


def turn(x, steps):
    count = lax.axis_size("row")
    return lax.ppermute(x, "row", [(i, (i + 2 * steps) % count) for i in range(count)])


def sum_col_stats(stats):
    stats = stats + swap(stats, "col", 1)
    return stats + swap(stats, "col", 2)


def sum_rows(x):
    bit = 1
    while bit < lax.axis_size("row"):
        x = x + swap(x, "row", bit)
        bit *= 2
    return x


def after(x, *first):
    return lax.optimization_barrier((x,) + first)[0] if first else x


def outer_groups():
    outer = lax.axis_size("row") // 2
    return [[2 * i + inner for i in range(outer)] for inner in range(2)]


def find(ids, wanted):
    at = jnp.arange(ids.shape[0])
    return jnp.sum(jnp.where(ids[None, :] == wanted[:, None], at[None, :], 0), axis=1).astype(
        jnp.int32
    )


def gather_whole(w):
    return [lax.all_gather(w, "row", axis=0, tiled=True)]


def gather_outer(w):
    return lax.all_gather(w, "row", axis=0, tiled=True, axis_index_groups=outer_groups())


class Clock:
    def __init__(self):
        self.now, self.new = [], []

    def at(self, x):
        return after(x, *self.now)

    def put(self, *xs):
        self.new += xs

    def tick(self):
        self.now, self.new = self.new, []


def on_device(
    tokens,
    segments,
    gains,
    shifts,
    biases,
    mixing,
    projection,
    expand,
    thresholds,
    contract,
    cotangent,
):
    seqs = segments.shape[0]
    rows, cols = lax.axis_size("row"), lax.axis_size("col")
    row, col = lax.axis_index("row"), lax.axis_index("col")
    tokens_here, width = tokens.shape
    full = width * cols
    heads = width // HD
    stepped = full // rows == BLOCK and rows == 2 * cols
    blocks, per_col = full // BLOCK, width // BLOCK
    at = jnp.arange(blocks)
    ours = per_col * ((at // per_col) ^ col) + at % per_col
    place, side = row // 2, row % 2
    steps = jnp.arange(max(rows // 2, 1))
    back = (place - steps) % (rows // 2)
    if stepped:
        ids_attend = ids_expand = jnp.concatenate([2 * back + side, 2 * back + 1 - side])
        ids_contract = jnp.stack([2 * steps + side, 2 * steps + 1 - side], axis=1).reshape(-1)
    else:
        ids_attend = ids_expand = ids_contract = at
        side = 0 * side
    sides = jnp.reshape(side, (1,)).astype(jnp.int32)
    away = jnp.array([1, 3, 0, 2]) ^ col
    clock = Clock()
    at_now, put, tick = clock.at, clock.put, clock.tick

    def columns_order(ids, ws):
        want = jnp.stack([2 * away + side, 2 * away + 1 - side]).reshape(-1)
        order = find(ids, want).reshape(2, -1)
        return order if len(ws) == 1 else order % (blocks // 2)

    def two(ws):
        return ws if len(ws) == 2 else [ws[0], ws[0]]

    def columns_sent(xs, ws, ids, name, first=0, chunks=4):
        order = columns_order(ids, ws)[:, :2]
        xs = [at_now(xs[0])] + xs[1:]
        sent = times_columns(
            xs, two(ws), order, sides, bf16, name + "_sent", first, chunks=chunks
        )
        return [swap(v, "col", 1) for v in (sent if chunks > 1 else [sent])]

    def columns_part(xs, ws, ids, got, name, first=0):
        order = columns_order(ids, ws)[:, 3:]
        return times_columns(xs, two(ws), order, sides, bf16, name + "_part", first, got, 1)

    def columns_base(xs, ws, ids, got, name, first=0):
        order = columns_order(ids, ws)[:, 2:3]
        xs = [at_now(xs[0])] + xs[1:]
        return times_columns(xs, two(ws), order, sides, f32, name + "_base", first, got, 0)

    class WeightSum:
        def __init__(self, a, ids, gs, name, groups=None):
            self.a, self.ids, self.gs, self.name = a, ids, gs, name
            self.left = rows // 2
            self.groups = groups or [[k] for k in reversed(range(self.left))]
            self.got, self.carry, self.result = {}, None, None

        def cut(self):
            if stepped:
                other = find(self.ids, 2 * back + 1 - side)
                self.sent = list(
                    weight_rows(at_now(self.a), other, self.gs, self.name + "_other", self.groups)
                )
            else:
                self.sent = [
                    weight_rows(at_now(self.a), find(self.ids, at), self.gs, self.name, dtype=f32)
                ]
            put(*self.sent)

        def keep(self, *first):
            if stepped:
                mine = find(self.ids, 2 * back + side)
                a = after(at_now(self.a), *first)
                single = [[k] for k in range(rows // 2)]
                self.kept = weight_rows(a, mine, self.gs, self.name + "_mine", single, f32)
                put(*self.kept)

        def move(self):
            if stepped:
                group = self.groups.pop(0)
                got = swap(at_now(self.sent.pop(0)), "row", 1)
                put(got)
                for j, k in enumerate(group):
                    self.got[k] = got[j * BLOCK : (j + 1) * BLOCK]

        def add(self):
            if not stepped:
                if self.result is None:
                    self.result = lax.psum_scatter(
                        self.sent[0], "row", scatter_dimension=0, tiled=True
                    )
                return
            self.left -= 1
            total = self.kept[self.left] + at_now(self.got[self.left]).astype(f32)
            if self.carry is not None:
                total = total + self.carry.astype(f32)
            if self.left == 0:
                self.result = total
            else:
                self.carry = turn(total.astype(bf16), -1)
                put(self.carry)

    head_ids = (col * heads + jnp.arange(heads)).astype(f32)
    slopes = jnp.exp2(-8.0 * (head_ids + 1.0) / (heads * cols))
    starts = jnp.sum(segments[:, None, :] < segments[:, :, None], axis=2).astype(jnp.int32)
    places_attend, places_expand = find(ids_attend, ours), find(ids_expand, ours)
    places_contract = find(ids_contract, ours)
    mix_width = 3 * width
    mixed_bias = jnp.concatenate([biases[0:1], jnp.zeros((1, width), f32), biases[1:2]], axis=1)

    attend_rows = jnp.concatenate([mixing.reshape(mixing.shape[0], -1), projection], axis=1)
    small = jnp.concatenate([gains, shifts], axis=0)
    put(attend_rows)
    tick()
    if stepped:
        own, near = [attend_rows], []
    else:
        whole = gather_whole(attend_rows)[0]
        own, near = [whole[: full // 2]], [whole[full // 2 :]]
        full_expand = gather_whole(expand)
        full_contract = gather_whole(contract)

    def weight_step(k):
        if stepped:
            ready = at_now(own[k])
            near.append(swap(ready, "row", 1))
            put(near[k])
            if k + 1 < rows // 2:
                own.append(turn(ready, 1))
                put(own[k + 1])

    weight_step(0)
    tokens_now = at_now(tokens)
    token_parts = [tokens, swap(tokens_now, "col", 1), swap(tokens_now, "col", 2)]
    put(*token_parts[1:])
    tick()

    weight_step(1)
    cot_now = at_now(cotangent)
    cot_parts = [cotangent, swap(cot_now, "col", 1), swap(cot_now, "col", 2)]
    token_parts.append(swap(at_now(token_parts[2]), "col", 1))
    put(*cot_parts[1:], token_parts[3])
    tick()

    weight_step(2)
    small_now = at_now(small)
    norms = [small, swap(small_now, "col", 1), swap(small_now, "col", 2)]
    cot_parts.append(swap(at_now(cot_parts[2]), "col", 1))
    put(*norms[1:], cot_parts[3])
    tick()

    weight_step(3)
    norms.append(swap(at_now(norms[2]), "col", 1))
    norms = jnp.concatenate(norms, axis=1)
    first_full, first_mean, first_scale = normalize(
        token_parts, norms[0:1], norms[2:3], places_attend, "first_norm"
    )
    cot_full = lay_out([at_now(cot_parts[0])] + cot_parts[1:], places_contract, "cotangent_rows")
    put(first_full, cot_full)
    expand_own, expand_near = [expand], []

    def expand_turn():
        if stepped:
            expand_own.append(turn(at_now(expand_own[-1]), 1))
            put(expand_own[-1])

    def expand_step(k):
        if stepped:
            expand_near.append(swap(at_now(expand_own[k]), "row", 1))
            put(expand_near[k])

    expand_turn()
    expand_turn()
    if stepped:
        contract_pair = jnp.concatenate([contract, swap(at_now(contract), "row", 1)], axis=0)
        put(contract_pair)
    tick()

    def add_bias(acc, extra, out):
        out[0][...] = (acc + extra[0][...]).astype(bf16)

    expand_turn()
    expand_step(0)
    if stepped:
        full_contract = [gather_outer(at_now(contract_pair))]
    mixed, *full_attend = times_rows(
        at_now(first_full),
        own + near,
        [mixed_bias],
        [((tokens_here, mix_width), bf16)],
        add_bias,
        "mix",
        tn=width,
        window=(0, mix_width),
        joins=[range(len(own)), range(len(own), len(own) + len(near))],
    )
    attended, logs = attend_forward(mixed, starts, slopes, seqs)
    put(attended)
    tick()

    expand_step(1)
    got = columns_sent([attended], full_attend, ids_attend, "project", mix_width)
    part = columns_part([attended], full_attend, ids_attend, got, "project", mix_width)
    put(part)
    tick()

    expand_step(2)
    across = swap(at_now(part), "col", 2)
    base = columns_base([attended], full_attend, ids_attend, got, "project", mix_width)
    resid = tokens.astype(f32)
    middle = resid + (base + across.astype(f32) + biases[2])
    middle_low = middle.astype(bf16)
    put(middle_low)
    tick()

    expand_step(3)
    middle_now = at_now(middle_low)
    middle_parts = [middle_low, swap(middle_now, "col", 1), swap(middle_now, "col", 2)]
    put(*middle_parts[1:])
    tick()

    middle_parts.append(swap(at_now(middle_parts[2]), "col", 1))
    second_full, second_mean, second_scale = normalize(
        middle_parts, norms[1:2], norms[3:4], places_expand, "second_norm"
    )
    put(second_full)
    tick()

    def activate(acc, extra, out):
        hidden = acc + extra[0][...]
        bell = 0.5 * (1.0 + lax.erf(hidden * sqrt_half))
        out[0][...] = (hidden * bell).astype(bf16)
        out[1][...] = bell + hidden * (jnp.exp(-0.5 * hidden * hidden) * inverse_root)

    hidden_shape = (tokens_here, expand.shape[1])
    active, slope, *joined = times_rows(
        at_now(second_full),
        expand_own + expand_near if stepped else full_expand,
        [thresholds[None]],
        [(hidden_shape, bf16), (hidden_shape, f32)],
        activate,
        "expand",
        tn=512,
        joins=[range(rows // 2), range(rows // 2, rows)] if stepped else [],
    )
    if stepped:
        full_expand = joined
    contract_sum = WeightSum(
        cot_full, ids_contract, [active], "contract_grad", [[3, 2], [1], [0]]
    )
    contract_sum.cut()
    put(active)
    tick()

    def back_activate(acc, extra, out):
        grad = (acc * extra[0][...]).astype(bf16)
        out[0][...] = grad
        out[1][...] = jnp.sum(grad.astype(f32), axis=0, keepdims=True)

    contract_sum.move()
    contract_sum.keep()
    hidden_grad, thresholds_part = times_rows(
        at_now(cot_full),
        full_contract,
        [slope],
        [(hidden_shape, bf16), ((1, hidden_shape[1]), f32)],
        back_activate,
        "contract_back",
        tn=512,
    )
    got = columns_sent([hidden_grad], full_expand, ids_expand, "expand_back")
    part = columns_part([hidden_grad], full_expand, ids_expand, got, "expand_back")
    put(part)
    tick()

    contract_sum.add()
    contract_sum.move()
    across = swap(at_now(part), "col", 2)
    base = columns_base([hidden_grad], full_expand, ids_expand, got, "expand_back")
    expand_sum = WeightSum(second_full, ids_expand, [hidden_grad], "expand_grad")
    expand_sum.cut()
    second_back = base + across.astype(f32)
    put(second_back)
    tick()

    def norm_back(upstream, centred, scale, gain):
        scaled = upstream * gain
        sums = sum_col_stats(
            jnp.stack([jnp.sum(scaled, axis=1), jnp.sum(scaled * centred, axis=1)])
        )
        result = scale * (
            scaled - sums[0][:, None] / full - centred * (sums[1][:, None] / full)
        )
        return result, jnp.sum(upstream * centred, axis=0), jnp.sum(upstream, axis=0)

    contract_sum.add()
    contract_sum.move()
    second_centred = (middle - second_mean) * second_scale
    second_input, second_gain, second_shift = norm_back(
        at_now(second_back), second_centred, second_scale, gains[1]
    )
    cot_float = cotangent.astype(f32)
    middle_grad = cot_float + second_input
    branch_grad = middle_grad.astype(bf16)
    branch_parts = [branch_grad, swap(branch_grad, "col", 1), swap(branch_grad, "col", 2)]
    expand_sum.keep(branch_grad)
    put(*branch_parts[1:])
    tick()

    def store(acc, extra, out):
        out[0][...] = acc.astype(bf16)

    contract_sum.add()
    expand_sum.move()
    branch_parts.append(swap(at_now(branch_parts[2]), "col", 1))
    branch_full = lay_out(branch_parts, places_attend, "branch_rows")
    (attended_grad,) = times_rows(
        branch_full,
        full_attend,
        [],
        [((tokens_here, width), bf16)],
        store,
        "project_back",
        tn=width,
        window=(mix_width, width),
    )
    project_sum = WeightSum(branch_full, ids_attend, [attended], "projection_grad", [[3, 2, 1, 0]])
    project_sum.cut()
    put(attended_grad)
    tick()

    expand_sum.add()
    expand_sum.move()
    query_back, key_back, value_back, query_sum, value_sum = attend_backward(
        mixed, at_now(attended_grad), starts, logs, slopes, seqs
    )
    mixed_grads = [query_back, key_back, value_back]
    put(query_back)
    tick()

    contract_sum.add()
    expand_sum.add()
    expand_sum.move()
    got = columns_sent(mixed_grads, full_attend, ids_attend, "mix_back")
    mixing_sum = WeightSum(first_full, ids_attend, mixed_grads, "mixing_grad")
    mixing_sum.cut()
    part = columns_part(mixed_grads, full_attend, ids_attend, got, "mix_back")
    put(part)
    tick()

    expand_sum.add()
    expand_sum.move()
    across = swap(at_now(part), "col", 2)
    base = columns_base(mixed_grads, full_attend, ids_attend, got, "mix_back")
    out_got = columns_sent([active], full_contract, ids_contract, "contract", chunks=1)
    first_back = base + across.astype(f32)
    put(first_back, *out_got)
    tick()

    expand_sum.add()
    project_sum.move()
    project_sum.keep()
    out_part = columns_part([at_now(active)], full_contract, ids_contract, out_got, "contract")
    first_centred = (resid - first_mean) * first_scale
    first_input, first_gain, first_shift = norm_back(
        at_now(first_back), first_centred, first_scale, gains[0]
    )
    tokens_grad = middle_grad + first_input
    small = jnp.stack(
        [
            first_gain,
            second_gain,
            first_shift,
            second_shift,
            jnp.sum(query_sum, axis=(0, 1)),
            jnp.sum(value_sum, axis=(0, 1)),
            jnp.sum(branch_grad.astype(f32), axis=0),
            jnp.sum(cot_float, axis=0),
        ]
    )
    small = jnp.concatenate([small, thresholds_part.reshape(-1, width)], axis=0)
    put(small, out_part)
    tick()

    project_sum.add()
    mixing_sum.move()
    mixing_sum.keep()
    out_across = swap(at_now(out_part), "col", 2)
    out_base = columns_base([active], full_contract, ids_contract, out_got, "contract")
    layer_out = (middle + (out_base + out_across.astype(f32) + biases[3])).astype(bf16)
    put(layer_out)
    bit = 1
    while bit < rows:
        small = small + swap(at_now(small), "row", bit)
        put(small)
        tick()
        bit *= 2
        project_sum.add()
        mixing_sum.add()
        if mixing_sum.groups:
            mixing_sum.move()
    tick()
    mixing_sum.add()
    contract_grad, expand_grad = contract_sum.result, expand_sum.result
    projection_grad, mixing_grad = project_sum.result, mixing_sum.result
    mixing_grad = jnp.stack(
        [mixing_grad[:, i * width : (i + 1) * width] for i in range(3)], axis=1
    )
    return (
        layer_out,
        tokens_grad,
        small[0:2],
        small[2:4],
        small[4:8],
        mixing_grad,
        projection_grad,
        expand_grad,
        small[8:].reshape(thresholds.shape),
        contract_grad,
    )


def solution(mesh):
    return jax.shard_map(
        on_device,
        mesh=mesh,
        in_specs=(
            P("row", "col"),
            P("row", None),
            P(None, "col"),
            P(None, "col"),
            P(None, "col"),
            P("row", None, "col"),
            P("row", "col"),
            P("row", "col"),
            P("col"),
            P("row", "col"),
            P("row", "col"),
        ),
        out_specs=(
            P("row", "col"),
            P("row", "col"),
            P(None, "col"),
            P(None, "col"),
            P(None, "col"),
            P("row", None, "col"),
            P("row", "col"),
            P("row", "col"),
            P("col"),
            P("row", "col"),
        ),
        check_vma=False,
    )
```

```python
import math
from functools import partial

import jax
import jax.numpy as jnp
from jax import lax
from jax.experimental import pallas as pl
from jax.experimental.pallas import tpu as pltpu
from jax.sharding import PartitionSpec as P

HD = 64
BLOCK = 256

norm_eps = 1e-05
sqrt_half = 0.7071067811865476
inverse_root = 0.3989422804014327
far = -1e33
NT = (((1,), (1,)), ((), ()))
TN = (((0,), (0,)), ((), ()))
VMEM_LIMIT = 56 << 20
CHEAP = 64
f32 = jnp.float32
bf16 = jnp.bfloat16


def pick_heads(pair):
    lane = lax.broadcasted_iota(jnp.int32, pair.shape, 1)
    zero = jnp.zeros_like(pair)
    return jnp.concatenate(
        [jnp.where(lane < HD, pair, zero), jnp.where(lane < HD, zero, pair)], axis=0
    )


def attend_kernel(
    slope_ref, start_ref, q_ref, k_ref, v_ref, out_ref, log_ref, dist_ref, *, rows, scale
):
    pair = pl.program_id(1)
    length = k_ref.shape[0]

    @pl.when(pair == 0)
    def _():
        for r0 in range(0, length, rows):
            shape = (rows, r0 + rows)
            i = lax.broadcasted_iota(jnp.int32, shape, 0) + r0
            j = lax.broadcasted_iota(jnp.int32, shape, 1)
            allowed = (j <= i) & (j >= start_ref[0, r0 : r0 + rows, :])
            dist_ref[r0 : r0 + rows, 0 : r0 + rows] = jnp.where(allowed, (j - i).astype(f32), far)

    slope_a, slope_b = slope_ref[2 * pair] * scale, slope_ref[2 * pair + 1] * scale
    for r0 in range(0, length, rows):
        r1 = r0 + rows
        q = pick_heads(q_ref[r0:r1, :] * jnp.asarray(scale, bf16))
        s = lax.dot_general(q, k_ref[0:r1, :], NT, preferred_element_type=f32)
        d = dist_ref[r0:r1, 0:r1]
        s = jnp.concatenate([s[:rows] + d * slope_a, s[rows:] + d * slope_b], axis=0)
        row_max = jnp.max(s, axis=1, keepdims=True)
        weights = jnp.exp(s - row_max)
        row_total = jnp.sum(weights, axis=1, keepdims=True)
        probs = (weights * (1.0 / row_total)).astype(bf16)
        o = jnp.dot(probs, v_ref[0:r1, :], preferred_element_type=f32)
        lane = lax.broadcasted_iota(jnp.int32, (rows, 2 * HD), 1)
        out_ref[r0:r1, :] = jnp.where(lane < HD, o[:rows], o[rows:]).astype(bf16)
        logs = row_max + jnp.log(row_total)
        logs = jnp.where(
            lane < HD,
            jnp.broadcast_to(logs[:rows], (rows, 2 * HD)),
            jnp.broadcast_to(logs[rows:], (rows, 2 * HD)),
        ).T
        log_ref[0, 0:1, r0:r1] = logs[0:1]
        log_ref[0, 1:2, r0:r1] = logs[HD : HD + 1]


def attend_forward(mixed, starts, slopes, seqs, rows=256):
    length, pairs = mixed.shape[0] // seqs, mixed.shape[1] // (6 * HD)

    def part(i):
        return pl.BlockSpec((length, 2 * HD), lambda s, p, *_: (s, i * pairs + p))

    return pl.pallas_call(
        partial(attend_kernel, rows=rows, scale=HD**-0.5),
        grid_spec=pltpu.PrefetchScalarGridSpec(
            num_scalar_prefetch=1,
            grid=(seqs, pairs),
            in_specs=[
                pl.BlockSpec((1, length, 1), lambda s, p, *_: (s, 0, 0)),
                part(0),
                part(1),
                part(2),
            ],
            out_specs=[part(0), pl.BlockSpec((1, 2, length), lambda s, p, *_: (s * pairs + p, 0, 0))],
            scratch_shapes=[pltpu.VMEM((length, length), f32)],
        ),
        out_shape=[
            jax.ShapeDtypeStruct((mixed.shape[0], 2 * HD * pairs), bf16),
            jax.ShapeDtypeStruct((seqs * pairs, 2, length), f32),
        ],
        compiler_params=pltpu.CompilerParams(vmem_limit_bytes=VMEM_LIMIT),
        cost_estimate=pl.CostEstimate(
            flops=16 * seqs * pairs * length * length * HD // CHEAP,
            bytes_accessed=4 * mixed.size // CHEAP,
            transcendentals=seqs * pairs * length * length // CHEAP,
        ),
        name="attend_forward",
    )(slopes, starts[:, :, None], mixed, mixed, mixed)


def attend_back_kernel(
    slope_ref,
    start_ref,
    log_ref,
    q_ref,
    k_ref,
    v_ref,
    g_ref,
    dq_ref,
    dk_ref,
    dv_ref,
    qs_ref,
    vs_ref,
    dist_ref,
    ka_ref,
    va_ref,
    *,
    rows,
    scale,
):
    pair = pl.program_id(1)
    length = k_ref.shape[0]

    @pl.when(pair == 0)
    def _():
        for r0 in range(0, length, rows):
            shape = (r0 + rows, rows)
            i = lax.broadcasted_iota(jnp.int32, shape, 1) + r0
            j = lax.broadcasted_iota(jnp.int32, shape, 0)
            allowed = (j <= i) & (j >= start_ref[0, :, r0 : r0 + rows])
            dist_ref[0 : r0 + rows, r0 : r0 + rows] = jnp.where(allowed, (j - i).astype(f32), far)

    slope_a, slope_b = slope_ref[2 * pair] * scale, slope_ref[2 * pair + 1] * scale
    query_sum = jnp.zeros((1, 2 * HD), f32)
    for r0 in reversed(range(0, length, rows)):
        r1 = r0 + rows
        q = pick_heads(q_ref[r0:r1, :] * jnp.asarray(scale, bf16))
        g = pick_heads(g_ref[r0:r1, :])
        k, v = k_ref[0:r1, :], v_ref[0:r1, :]
        s = lax.dot_general(k, q, NT, preferred_element_type=f32)
        d = dist_ref[0:r1, r0:r1]
        logs = jnp.concatenate([log_ref[0, 0:1, r0:r1], log_ref[0, 1:2, r0:r1]], axis=1)
        s = jnp.concatenate([s[:, :rows] + d * slope_a, s[:, rows:] + d * slope_b], axis=1)
        probs = jnp.exp(s - logs)
        t = lax.dot_general(v, g, NT, preferred_element_type=f32)
        centre = jnp.sum(probs * t, axis=0, keepdims=True)
        score_grad = (probs * (t - centre)).astype(bf16)
        value_part = jnp.dot(probs.astype(bf16), g, preferred_element_type=f32)
        key_part = jnp.dot(score_grad, q, preferred_element_type=f32)
        if r1 == length:
            va_ref[...] = value_part
            ka_ref[...] = key_part
        else:
            va_ref[0:r1, :] += value_part
            ka_ref[0:r1, :] += key_part
        dq = lax.dot_general(score_grad, k, TN, preferred_element_type=f32)
        lane = lax.broadcasted_iota(jnp.int32, (rows, 2 * HD), 1)
        dq = (jnp.where(lane < HD, dq[:rows], dq[rows:]) * scale).astype(bf16)
        dq_ref[r0:r1, :] = dq
        query_sum = query_sum + jnp.sum(dq.astype(f32), axis=0, keepdims=True)
    qs_ref[0] = query_sum
    dk_ref[...] = ka_ref[...].astype(bf16)
    dv = va_ref[...].astype(bf16)
    dv_ref[...] = dv
    vs_ref[0] = jnp.sum(dv.astype(f32), axis=0, keepdims=True)


def attend_backward(mixed, grads, starts, logs, slopes, seqs, rows=256):
    length, pairs = mixed.shape[0] // seqs, mixed.shape[1] // (6 * HD)

    def part(i):
        return pl.BlockSpec((length, 2 * HD), lambda s, p, *_: (s, i * pairs + p))

    out = jax.ShapeDtypeStruct(grads.shape, bf16)
    sums = jax.ShapeDtypeStruct((seqs, 1, grads.shape[1]), f32)
    sum_spec = pl.BlockSpec((1, 1, 2 * HD), lambda s, p, *_: (s, 0, p))
    return pl.pallas_call(
        partial(attend_back_kernel, rows=rows, scale=HD**-0.5),
        grid_spec=pltpu.PrefetchScalarGridSpec(
            num_scalar_prefetch=1,
            grid=(seqs, pairs),
            in_specs=[
                pl.BlockSpec((1, 1, length), lambda s, p, *_: (s, 0, 0)),
                pl.BlockSpec((1, 2, length), lambda s, p, *_: (s * pairs + p, 0, 0)),
                part(0),
                part(1),
                part(2),
                part(0),
            ],
            out_specs=[part(0), part(0), part(0), sum_spec, sum_spec],
            scratch_shapes=[
                pltpu.VMEM((length, length), f32),
                pltpu.VMEM((length, 2 * HD), f32),
                pltpu.VMEM((length, 2 * HD), f32),
            ],
        ),
        out_shape=[out, out, out, sums, sums],
        compiler_params=pltpu.CompilerParams(vmem_limit_bytes=VMEM_LIMIT),
        cost_estimate=pl.CostEstimate(
            flops=40 * seqs * pairs * length * length * HD // CHEAP,
            bytes_accessed=14 * grads.size // CHEAP,
            transcendentals=seqs * pairs * length * length // CHEAP,
        ),
        name="attend_backward",
    )(slopes, starts[:, None, :], logs, mixed, mixed, mixed, grads)


def resident(shape):
    return pl.BlockSpec(shape, lambda *_: (0,) * len(shape), pipeline_mode=pl.Buffered(1))


def kept_out(shape):
    return pl.BlockSpec(shape, lambda *_: (0,) * len(shape))


def flat_rows(ws):
    return jnp.concatenate([w[...] for w in ws], axis=0)


def matmul_call(kernel, grid, ins, outs, scratch, flops, name, prefetch=()):
    moved = sum(a.size * a.dtype.itemsize for a, _ in ins)
    moved += sum(jnp.dtype(t).itemsize * math.prod(s) for s, t, _ in outs)
    return pl.pallas_call(
        kernel,
        grid_spec=pltpu.PrefetchScalarGridSpec(
            num_scalar_prefetch=len(prefetch),
            grid=grid,
            in_specs=[s for _, s in ins],
            out_specs=[s for _, _, s in outs],
            scratch_shapes=scratch,
        ),
        out_shape=[jax.ShapeDtypeStruct(s, t) for s, t, _ in outs],
        compiler_params=pltpu.CompilerParams(vmem_limit_bytes=VMEM_LIMIT),
        cost_estimate=pl.CostEstimate(
            flops=flops // CHEAP, bytes_accessed=moved // CHEAP, transcendentals=0
        ),
        name=name,
    )(*prefetch, *[a for a, _ in ins])


def times_rows(x, ws, extras, outs, finish, name, tn, window=None, joins=()):
    tokens, depth = x.shape
    first, width = window or (0, ws[0].shape[1])
    first, tiles = first // tn, width // tn
    n_ws, n_ex, n_out = len(ws), len(extras), len(outs)
    steps = ws[0].shape[1] // tn if joins else tiles

    def kernel(*refs):
        x_ref, w_refs = refs[0], refs[1 : 1 + n_ws]
        extra, out = refs[1 + n_ws : 1 + n_ws + n_ex], refs[1 + n_ws + n_ex :]
        for places, joined in zip(joins, out[n_out:]):
            at = 0
            for i in places:
                joined[at : at + ws[i].shape[0], :] = w_refs[i][...]
                at += ws[i].shape[0]

        def multiply():
            acc = jnp.dot(x_ref[...], flat_rows(w_refs), preferred_element_type=f32)
            finish(acc, extra, out[:n_out])

        if steps == tiles:
            multiply()
        else:
            pl.when(pl.program_id(0) < tiles)(multiply)

    def spec(rows):
        return pl.BlockSpec((rows, tn), lambda n: (0, jnp.minimum(n, tiles - 1)))

    def tile(rows):
        return pl.BlockSpec((rows, tn), lambda n: (0, n + first))

    ins = [(x, resident(x.shape))] + [(w, tile(w.shape[0])) for w in ws]
    ins += [(e, spec(e.shape[0])) for e in extras]
    results = [(s, t, spec(s[0])) for s, t in outs]
    for places in joins:
        rows = sum(ws[i].shape[0] for i in places)
        results.append(((rows, ws[0].shape[1]), bf16, tile(rows)))
    return matmul_call(kernel, (steps,), ins, results, [], 2 * tokens * depth * width, name)


def times_columns(xs, ws, order, side, dtype, name, first=0, added=(), block=0, chunks=None):
    tokens = xs[0].shape[0]
    count = order.shape[1]
    n_xs = len(xs)
    width = sum(x.shape[1] for x in xs)
    chunks = chunks or [tokens]

    def kernel(order_ref, side_ref, *refs):
        x_refs, w_refs = refs[:n_xs], refs[n_xs : n_xs + 2]
        added_refs, out_refs = refs[n_xs + 2 : n_xs + 2 + len(added)], refs[-len(chunks) :]
        x = jnp.concatenate([r[...] for r in x_refs], axis=1)
        for i, w_ref in enumerate(w_refs):
            acc = lax.dot_general(x, w_ref[...], NT, preferred_element_type=f32)
            place = side_ref[0] if i == 0 else 1 - side_ref[0]
            place = pl.ds(pl.multiple_of(place * BLOCK, BLOCK), BLOCK)
            if added:
                acc = acc + jnp.concatenate([r[:, place] for r in added_refs]).astype(f32)
            at = 0
            for out_ref, height in zip(out_refs, chunks):
                out_ref[:, place] = acc[at : at + height].astype(dtype)
                at += height

    def w_spec(i):
        return pl.BlockSpec((BLOCK, width), lambda n, order_ref, _: (order_ref[i, n], first // width))

    def pair(height, start):
        return pl.BlockSpec((height, 2 * BLOCK), lambda n, *_: (0, start + n))

    ins = [(x, resident(x.shape)) for x in xs]
    ins += [(w, w_spec(i)) for i, w in enumerate(ws)]
    ins += [(b, pair(b.shape[0], block)) for b in added]
    done = matmul_call(
        kernel,
        (count,),
        ins,
        [((height, 2 * BLOCK * count), dtype, pair(height, 0)) for height in chunks],
        [],
        4 * tokens * BLOCK * count * width,
        name,
        prefetch=(order, side),
    )
    return done if len(chunks) > 1 else done[0]


def weight_rows(a, order, gs, name, groups=None, dtype=bf16):
    tokens = a.shape[0]
    width = sum(g.shape[1] for g in gs)
    count = order.shape[0]
    n_gs = len(gs)

    def kernel(order_ref, a_ref, *refs):
        g_refs, out_refs = refs[:n_gs], refs[n_gs:]
        g = jnp.concatenate([r[...] for r in g_refs], axis=1)
        acc = lax.dot_general(a_ref[...], g, TN, preferred_element_type=f32).astype(dtype)
        if groups is None:
            out_refs[0][...] = acc
            return
        for out_ref, group in zip(out_refs, groups):
            for j, i in enumerate(group):

                @pl.when(pl.program_id(0) == i)
                def _(out_ref=out_ref, rows=slice(j * BLOCK, (j + 1) * BLOCK)):
                    out_ref[rows, :] = acc

    ins = [(a, pl.BlockSpec((tokens, BLOCK), lambda i, order_ref: (0, order_ref[i])))]
    ins += [(g, resident(g.shape)) for g in gs]
    if groups is None:
        outs = [((count * BLOCK, width), dtype, pl.BlockSpec((BLOCK, width), lambda i, *_: (i, 0)))]
    else:
        shapes = [(len(group) * BLOCK, width) for group in groups]
        outs = [(shape, dtype, kept_out(shape)) for shape in shapes]
    done = matmul_call(
        kernel, (count,), ins, outs, [], 2 * tokens * BLOCK * count * width, name, prefetch=(order,)
    )
    return done[0] if groups is None else done


def place_blocks(values, place_ref, out_ref):
    at = 0
    for value in values:
        for c0 in range(0, value.shape[1], BLOCK):
            place = pl.ds(pl.multiple_of(place_ref[at] * BLOCK, BLOCK), BLOCK)
            out_ref[:, place] = value[:, c0 : c0 + BLOCK]
            at += 1


def lay_out(parts, places, name, tm=256):
    tokens, width = parts[0].shape
    full = width * len(parts)

    def kernel(place_ref, *refs):
        place_blocks([r[...] for r in refs[:-1]], place_ref, refs[-1])

    return matmul_call(
        kernel,
        (tokens // tm,),
        [(p, pl.BlockSpec((tm, width), lambda m, *_: (m, 0))) for p in parts],
        [((tokens, full), bf16, pl.BlockSpec((tm, full), lambda m, *_: (m, 0)))],
        [],
        tokens * full,
        name,
        prefetch=(places,),
    )[0]


def normalize(parts, gain, shift, places, name, tm=256):
    tokens, width = parts[0].shape
    n = len(parts)
    full = width * n

    def kernel(place_ref, *refs):
        gain_ref, shift_ref, out_ref, mean_ref, scale_ref = refs[n:]
        rows = [r[...].astype(f32) for r in refs[:n]]
        mean = sum(jnp.sum(v, axis=1, keepdims=True) for v in rows) / full
        square = sum(jnp.sum(v * v, axis=1, keepdims=True) for v in rows) / full
        scale = lax.rsqrt(square - mean * mean + norm_eps)
        mean_ref[...] = mean
        scale_ref[...] = scale
        done = []
        for i, v in enumerate(rows):
            cols = slice(i * width, (i + 1) * width)
            done.append(((v - mean) * scale * gain_ref[:, cols] + shift_ref[:, cols]).astype(bf16))
        place_blocks(done, place_ref, out_ref)

    ins = [(p, pl.BlockSpec((tm, width), lambda m, *_: (m, 0))) for p in parts]
    ins += [(gain, resident(gain.shape)), (shift, resident(shift.shape))]
    column = pl.BlockSpec((tm, 1), lambda m, *_: (m, 0))
    return matmul_call(
        kernel,
        (tokens // tm,),
        ins,
        [
            ((tokens, full), bf16, pl.BlockSpec((tm, full), lambda m, *_: (m, 0))),
            ((tokens, 1), f32, column),
            ((tokens, 1), f32, column),
        ],
        [],
        8 * tokens * full,
        name,
        prefetch=(places,),
    )


def swap(x, axis, bit):
    return lax.ppermute(x, axis, [(i, i ^ bit) for i in range(lax.axis_size(axis))])


def turn(x, steps):
    count = lax.axis_size("row")
    return lax.ppermute(x, "row", [(i, (i + 2 * steps) % count) for i in range(count)])


def sum_col_stats(stats):
    stats = stats + swap(stats, "col", 1)
    return stats + swap(stats, "col", 2)


def sum_rows(x):
    bit = 1
    while bit < lax.axis_size("row"):
        x = x + swap(x, "row", bit)
        bit *= 2
    return x


def after(x, *first):
    return lax.optimization_barrier((x,) + first)[0] if first else x


def outer_groups():
    outer = lax.axis_size("row") // 2
    return [[2 * i + inner for i in range(outer)] for inner in range(2)]


def find(ids, wanted):
    at = jnp.arange(ids.shape[0])
    return jnp.sum(jnp.where(ids[None, :] == wanted[:, None], at[None, :], 0), axis=1).astype(
        jnp.int32
    )


def gather_whole(w):
    return [lax.all_gather(w, "row", axis=0, tiled=True)]


def gather_outer(w):
    return lax.all_gather(w, "row", axis=0, tiled=True, axis_index_groups=outer_groups())


class Clock:
    def __init__(self):
        self.now, self.new = [], []

    def at(self, x):
        return after(x, *self.now)

    def put(self, *xs):
        self.new += xs

    def tick(self):
        self.now, self.new = self.new, []


def on_device(
    tokens,
    segments,
    gains,
    shifts,
    biases,
    mixing,
    projection,
    expand,
    thresholds,
    contract,
    cotangent,
):
    seqs = segments.shape[0]
    rows, cols = lax.axis_size("row"), lax.axis_size("col")
    row, col = lax.axis_index("row"), lax.axis_index("col")
    tokens_here, width = tokens.shape
    full = width * cols
    heads = width // HD
    stepped = full // rows == BLOCK and rows == 2 * cols
    blocks, per_col = full // BLOCK, width // BLOCK
    at = jnp.arange(blocks)
    ours = per_col * ((at // per_col) ^ col) + at % per_col
    place, side = row // 2, row % 2
    steps = jnp.arange(max(rows // 2, 1))
    back = (place - steps) % (rows // 2)
    if stepped:
        ids_attend = ids_expand = jnp.concatenate([2 * back + side, 2 * back + 1 - side])
        ids_contract = jnp.stack([2 * steps + side, 2 * steps + 1 - side], axis=1).reshape(-1)
    else:
        ids_attend = ids_expand = ids_contract = at
        side = 0 * side
    sides = jnp.reshape(side, (1,)).astype(jnp.int32)
    away = jnp.array([1, 3, 0, 2]) ^ col
    clock = Clock()
    at_now, put, tick = clock.at, clock.put, clock.tick

    def columns_order(ids, ws):
        want = jnp.stack([2 * away + side, 2 * away + 1 - side]).reshape(-1)
        order = find(ids, want).reshape(2, -1)
        return order if len(ws) == 1 else order % (blocks // 2)

    def two(ws):
        return ws if len(ws) == 2 else [ws[0], ws[0]]

    def columns_sent(xs, ws, ids, name, first=0):
        order = columns_order(ids, ws)[:, :2]
        xs = [at_now(xs[0])] + xs[1:]
        chunks = [3 * tokens_here // 8, 3 * tokens_here // 8, tokens_here // 4]
        sent = times_columns(
            xs, two(ws), order, sides, bf16, name + "_sent", first, chunks=chunks
        )
        return [swap(v, "col", 1) for v in sent]

    def columns_part(xs, ws, ids, got, name, first=0):
        order = columns_order(ids, ws)[:, 3:]
        return times_columns(xs, two(ws), order, sides, bf16, name + "_part", first, got, 1)

    def columns_base(xs, ws, ids, got, name, first=0):
        order = columns_order(ids, ws)[:, 2:3]
        xs = [at_now(xs[0])] + xs[1:]
        return times_columns(xs, two(ws), order, sides, f32, name + "_base", first, got, 0)

    class WeightSum:
        def __init__(self, a, ids, gs, name, groups=None):
            self.a, self.ids, self.gs, self.name = a, ids, gs, name
            self.left = rows // 2
            self.groups = groups or [[k] for k in reversed(range(self.left))]
            self.got, self.kept, self.carry, self.result = {}, [], None, None

        def cut(self):
            if stepped:
                other = find(self.ids, 2 * back + 1 - side)
                self.sent = list(
                    weight_rows(at_now(self.a), other, self.gs, self.name + "_other", self.groups)
                )
            else:
                self.sent = [
                    weight_rows(at_now(self.a), find(self.ids, at), self.gs, self.name, dtype=f32)
                ]
            put(*self.sent)

        def keep(self, *first):
            if stepped:
                mine = find(self.ids, 2 * back + side)
                a = after(at_now(self.a), *first)
                single = [[k] for k in range(rows // 2)]
                self.kept = weight_rows(a, mine, self.gs, self.name + "_mine", single)
                put(*self.kept)

        def move(self, late=False):
            if stepped:
                group = self.groups.pop(0)
                got = swap(at_now(self.sent.pop(0)), "row", 1)
                if not late:
                    put(got)
                for j, k in enumerate(group):
                    self.got[k] = (got, j * BLOCK)

        def add(self, *first):
            if not stepped:
                if self.result is None:
                    self.result = lax.psum_scatter(
                        self.sent[0], "row", scatter_dimension=0, tiled=True
                    )
                return
            self.left -= 1
            got, start = self.got[self.left]
            got = after(at_now(got), *first)[start : start + BLOCK]
            total = self.kept[self.left].astype(f32) + got.astype(f32)
            if self.carry is not None:
                total = total + self.carry.astype(f32)
            if self.left == 0:
                self.result = total
            else:
                self.carry = turn(total.astype(bf16), -1)
                put(self.carry)

    head_ids = (col * heads + jnp.arange(heads)).astype(f32)
    slopes = jnp.exp2(-8.0 * (head_ids + 1.0) / (heads * cols))
    starts = jnp.sum(segments[:, None, :] < segments[:, :, None], axis=2).astype(jnp.int32)
    places_attend, places_expand = find(ids_attend, ours), find(ids_expand, ours)
    places_contract = find(ids_contract, ours)
    mix_width = 3 * width
    mixed_bias = jnp.concatenate([biases[0:1], jnp.zeros((1, width), f32), biases[1:2]], axis=1)

    attend_rows = jnp.concatenate([mixing.reshape(mixing.shape[0], -1), projection], axis=1)
    small = jnp.concatenate([gains, shifts], axis=0)
    put(attend_rows)
    tick()
    if stepped:
        own, near = [attend_rows], []
    else:
        whole = gather_whole(attend_rows)[0]
        own, near = [whole[: full // 2]], [whole[full // 2 :]]
        full_expand = gather_whole(expand)
        full_contract = gather_whole(contract)

    def weight_step(k):
        if stepped:
            ready = at_now(own[k])
            near.append(swap(ready, "row", 1))
            put(near[k])
            if k + 1 < rows // 2:
                own.append(turn(ready, 1))
                put(own[k + 1])

    weight_step(0)
    tokens_now = at_now(tokens)
    token_parts = [tokens, swap(tokens_now, "col", 1), swap(tokens_now, "col", 2)]
    put(*token_parts[1:])
    tick()

    weight_step(1)
    cot_now = at_now(cotangent)
    cot_parts = [cotangent, swap(cot_now, "col", 1), swap(cot_now, "col", 2)]
    token_parts.append(swap(at_now(token_parts[2]), "col", 1))
    put(*cot_parts[1:], token_parts[3])
    tick()

    weight_step(2)
    small_now = at_now(small)
    norms = [small, swap(small_now, "col", 1), swap(small_now, "col", 2)]
    cot_parts.append(swap(at_now(cot_parts[2]), "col", 1))
    put(*norms[1:], cot_parts[3])
    tick()

    weight_step(3)
    norms.append(swap(at_now(norms[2]), "col", 1))
    norms = jnp.concatenate(norms, axis=1)
    first_full, first_mean, first_scale = normalize(
        token_parts, norms[0:1], norms[2:3], places_attend, "first_norm"
    )
    cot_full = lay_out([at_now(cot_parts[0])] + cot_parts[1:], places_contract, "cotangent_rows")
    put(first_full, cot_full)
    expand_own, expand_near = [expand], []

    def expand_turn(start=None):
        if stepped:
            block = at_now(expand_own[2 if start is not None else -1])
            if start is not None:
                block = block[start : start + BLOCK // 2]
            expand_own.append(turn(block, 1))
            put(expand_own[-1])

    def expand_step(*ks):
        if stepped:
            for k in ks:
                expand_near.append(swap(at_now(expand_own[k]), "row", 1))
                put(expand_near[k])

    expand_turn()
    expand_turn()
    if stepped:
        contract_pair = jnp.concatenate([contract, swap(at_now(contract), "row", 1)], axis=0)
        put(contract_pair)
    tick()

    def add_bias(acc, extra, out):
        out[0][...] = (acc + extra[0][...]).astype(bf16)

    expand_turn(0)
    expand_step(0)
    if stepped:
        full_contract = [gather_outer(at_now(contract_pair))]
    mixed, *full_attend = times_rows(
        at_now(first_full),
        own + near,
        [mixed_bias],
        [((tokens_here, mix_width), bf16)],
        add_bias,
        "mix",
        tn=width,
        window=(0, mix_width),
        joins=[range(len(own)), range(len(own), len(own) + len(near))],
    )
    attended, logs = attend_forward(mixed, starts, slopes, seqs)
    put(attended)
    tick()

    expand_step(1)
    got = columns_sent([attended], full_attend, ids_attend, "project", mix_width)
    part = columns_part([attended], full_attend, ids_attend, got, "project", mix_width)
    put(part)
    tick()

    expand_step(2)
    expand_turn(BLOCK // 2)
    across = swap(at_now(part), "col", 2)
    base = columns_base([attended], full_attend, ids_attend, got, "project", mix_width)
    resid = tokens.astype(f32)
    middle = resid + (base + across.astype(f32) + biases[2])
    middle_low = middle.astype(bf16)
    first_mean, first_scale = first_mean[:, 0], first_scale[:, 0]
    put(middle_low, first_mean, first_scale)
    tick()

    expand_step(3, 4)
    middle_now = at_now(middle_low)
    middle_parts = [middle_low, swap(middle_now, "col", 1), swap(middle_now, "col", 2)]
    put(*middle_parts[1:])
    tick()

    middle_parts.append(swap(at_now(middle_parts[2]), "col", 1))
    second_full, second_mean, second_scale = normalize(
        middle_parts, norms[1:2], norms[3:4], places_expand, "second_norm"
    )
    put(second_full)
    tick()

    def activate(acc, extra, out):
        hidden = acc + extra[0][...]
        bell = 0.5 * (1.0 + lax.erf(hidden * sqrt_half))
        out[0][...] = (hidden * bell).astype(bf16)
        out[1][...] = bell + hidden * (jnp.exp(-0.5 * hidden * hidden) * inverse_root)

    hidden_shape = (tokens_here, expand.shape[1])
    active, slope, *joined = times_rows(
        at_now(second_full),
        expand_own + expand_near if stepped else full_expand,
        [thresholds[None]],
        [(hidden_shape, bf16), (hidden_shape, f32)],
        activate,
        "expand",
        tn=512,
        joins=[range(len(expand_own)), range(len(expand_own), 2 * len(expand_own))] if stepped else [],
    )
    if stepped:
        full_expand = joined
    contract_sum = WeightSum(
        cot_full, ids_contract, [active], "contract_grad", [[3, 2], [1], [0]]
    )
    contract_sum.cut()
    put(active)
    tick()

    def back_activate(acc, extra, out):
        grad = (acc * extra[0][...]).astype(bf16)
        out[0][...] = grad
        out[1][...] = jnp.sum(grad.astype(f32), axis=0, keepdims=True)

    second_mean, second_scale = at_now(second_mean)[:, 0], at_now(second_scale)[:, 0]
    put(second_mean, second_scale)
    contract_sum.move(late=True)
    contract_sum.keep()
    hidden_grad, thresholds_part = times_rows(
        after(at_now(cot_full), *contract_sum.kept[:1]),
        full_contract,
        [slope],
        [(hidden_shape, bf16), ((1, hidden_shape[1]), f32)],
        back_activate,
        "contract_back",
        tn=512,
    )
    got = columns_sent([hidden_grad], full_expand, ids_expand, "expand_back")
    part = columns_part([hidden_grad], full_expand, ids_expand, got, "expand_back")
    put(part)
    tick()

    contract_sum.add()
    contract_sum.move()
    across = swap(at_now(part), "col", 2)
    base = columns_base([hidden_grad], full_expand, ids_expand, got, "expand_back")
    expand_sum = WeightSum(second_full, ids_expand, [hidden_grad], "expand_grad")
    expand_sum.cut()
    second_back = base + across.astype(f32)
    put(second_back)
    tick()

    def norm_back(upstream, centred, scale, gain):
        scaled = upstream * gain
        sums = sum_col_stats(
            jnp.stack([jnp.sum(scaled, axis=1), jnp.sum(scaled * centred, axis=1)])
        )
        result = scale[:, None] * (
            scaled - sums[0][:, None] / full - centred * (sums[1][:, None] / full)
        )
        return result, jnp.sum(upstream * centred, axis=0), jnp.sum(upstream, axis=0)

    contract_sum.move()
    second_centred = (middle - second_mean[:, None]) * second_scale[:, None]
    second_input, second_gain, second_shift = norm_back(
        at_now(second_back), second_centred, second_scale, gains[1]
    )
    cot_float = cotangent.astype(f32)
    middle_grad = cot_float + second_input
    branch_grad = middle_grad.astype(bf16)
    branch_parts = [branch_grad, swap(branch_grad, "col", 1), swap(branch_grad, "col", 2)]
    contract_sum.add(branch_grad)
    expand_sum.keep(branch_grad)
    put(*branch_parts[1:])
    tick()

    def store(acc, extra, out):
        out[0][...] = acc.astype(bf16)

    contract_sum.add()
    expand_sum.move()
    branch_parts.append(swap(at_now(branch_parts[2]), "col", 1))
    branch_full = lay_out(branch_parts, places_attend, "branch_rows")
    (attended_grad,) = times_rows(
        branch_full,
        full_attend,
        [],
        [((tokens_here, width), bf16)],
        store,
        "project_back",
        tn=width,
        window=(mix_width, width),
    )
    project_sum = WeightSum(branch_full, ids_attend, [attended], "projection_grad", [[3, 2, 1, 0]])
    project_sum.cut()
    put(attended_grad)
    tick()

    expand_sum.add()
    expand_sum.move()
    query_back, key_back, value_back, query_sum, value_sum = attend_backward(
        mixed, at_now(attended_grad), starts, logs, slopes, seqs
    )
    mixed_grads = [query_back, key_back, value_back]
    put(query_back)
    tick()

    contract_sum.add()
    expand_sum.add()
    expand_sum.move()
    got = columns_sent(mixed_grads, full_attend, ids_attend, "mix_back")
    mixing_sum = WeightSum(first_full, ids_attend, mixed_grads, "mixing_grad")
    mixing_sum.cut()
    part = columns_part(mixed_grads, full_attend, ids_attend, got, "mix_back")
    put(part)
    tick()

    expand_sum.add()
    project_sum.move()
    project_sum.keep()
    across = swap(at_now(part), "col", 2)
    base = columns_base(mixed_grads, full_attend, ids_attend, got, "mix_back")
    first_back = base + across.astype(f32)
    put(first_back)
    tick()

    expand_sum.move()
    for _ in range(rows // 2 - 1):
        project_sum.add()
    out_got = columns_sent([active], full_contract, ids_contract, "contract")
    first_centred = (resid - first_mean[:, None]) * first_scale[:, None]
    first_input, first_gain, first_shift = norm_back(
        at_now(first_back), first_centred, first_scale, gains[0]
    )
    tokens_grad = middle_grad + first_input
    small = jnp.stack(
        [
            first_gain,
            second_gain,
            first_shift,
            second_shift,
            jnp.sum(query_sum, axis=(0, 1)),
            jnp.sum(value_sum, axis=(0, 1)),
            jnp.sum(branch_grad.astype(f32), axis=0),
            jnp.sum(cot_float, axis=0),
        ]
    )
    small = jnp.concatenate([small, thresholds_part.reshape(-1, width)], axis=0)
    put(small, *out_got)
    tick()

    def small_step(bit):
        return small + swap(at_now(small), "row", bit) if bit < rows else small

    expand_sum.add()
    project_sum.add()
    mixing_sum.move()
    mixing_sum.keep()
    out_part = columns_part([at_now(active)], full_contract, ids_contract, out_got, "contract")
    small = small_step(1)
    put(small, out_part)
    tick()

    mixing_sum.add()
    mixing_sum.move()
    out_across = swap(at_now(out_part), "col", 2)
    out_base = columns_base([active], full_contract, ids_contract, out_got, "contract")
    layer_out = (middle + (out_base + out_across.astype(f32) + biases[3])).astype(bf16)
    small = small_step(2)
    put(small)
    tick()

    bit = 4
    while bit < rows or mixing_sum.groups:
        mixing_sum.add()
        mixing_sum.groups and mixing_sum.move()
        small = small_step(bit)
        put(small)
        tick()
        bit *= 2
        if not stepped and bit >= rows:
            break
    mixing_sum.add()
    contract_grad, expand_grad = contract_sum.result, expand_sum.result
    projection_grad, mixing_grad = project_sum.result, mixing_sum.result
    mixing_grad = jnp.stack(
        [mixing_grad[:, i * width : (i + 1) * width] for i in range(3)], axis=1
    )
    return (
        layer_out,
        tokens_grad,
        small[0:2],
        small[2:4],
        small[4:8],
        mixing_grad,
        projection_grad,
        expand_grad,
        small[8:].reshape(thresholds.shape),
        contract_grad,
    )


def solution(mesh):
    return jax.shard_map(
        on_device,
        mesh=mesh,
        in_specs=(
            P("row", "col"),
            P("row", None),
            P(None, "col"),
            P(None, "col"),
            P(None, "col"),
            P("row", None, "col"),
            P("row", "col"),
            P("row", "col"),
            P("col"),
            P("row", "col"),
            P("row", "col"),
        ),
        out_specs=(
            P("row", "col"),
            P("row", "col"),
            P(None, "col"),
            P(None, "col"),
            P(None, "col"),
            P("row", None, "col"),
            P("row", "col"),
            P("row", "col"),
            P("col"),
            P("row", "col"),
        ),
        check_vma=False,
    )
```

```python
import math
from functools import partial

import jax
import jax.numpy as jnp
from jax import lax
from jax.experimental import pallas as pl
from jax.experimental.pallas import tpu as pltpu
from jax.sharding import PartitionSpec as P

HD = 64
BLOCK = 256

norm_eps = 1e-05
sqrt_half = 0.7071067811865476
inverse_root = 0.3989422804014327
far = -1e33
NT = (((1,), (1,)), ((), ()))
TN = (((0,), (0,)), ((), ()))
VMEM_LIMIT = 56 << 20
CHEAP = 64
f32 = jnp.float32
bf16 = jnp.bfloat16


def pick_heads(pair):
    lane = lax.broadcasted_iota(jnp.int32, pair.shape, 1)
    zero = jnp.zeros_like(pair)
    return jnp.concatenate(
        [jnp.where(lane < HD, pair, zero), jnp.where(lane < HD, zero, pair)], axis=0
    )


def attend_kernel(
    slope_ref, start_ref, q_ref, k_ref, v_ref, out_ref, log_ref, dist_ref, *, rows, scale
):
    pair = pl.program_id(1)
    length = k_ref.shape[0]

    @pl.when(pair == 0)
    def _():
        for r0 in range(0, length, rows):
            shape = (rows, r0 + rows)
            i = lax.broadcasted_iota(jnp.int32, shape, 0) + r0
            j = lax.broadcasted_iota(jnp.int32, shape, 1)
            allowed = (j <= i) & (j >= start_ref[0, r0 : r0 + rows, :])
            dist_ref[r0 : r0 + rows, 0 : r0 + rows] = jnp.where(allowed, (j - i).astype(f32), far)

    slope_a, slope_b = slope_ref[2 * pair] * scale, slope_ref[2 * pair + 1] * scale
    for r0 in range(0, length, rows):
        r1 = r0 + rows
        q = pick_heads(q_ref[r0:r1, :] * jnp.asarray(scale, bf16))
        s = lax.dot_general(q, k_ref[0:r1, :], NT, preferred_element_type=f32)
        d = dist_ref[r0:r1, 0:r1]
        s = jnp.concatenate([s[:rows] + d * slope_a, s[rows:] + d * slope_b], axis=0)
        row_max = jnp.max(s, axis=1, keepdims=True)
        weights = jnp.exp(s - row_max)
        row_total = jnp.sum(weights, axis=1, keepdims=True)
        probs = (weights * (1.0 / row_total)).astype(bf16)
        o = jnp.dot(probs, v_ref[0:r1, :], preferred_element_type=f32)
        lane = lax.broadcasted_iota(jnp.int32, (rows, 2 * HD), 1)
        out_ref[r0:r1, :] = jnp.where(lane < HD, o[:rows], o[rows:]).astype(bf16)
        logs = row_max + jnp.log(row_total)
        logs = jnp.where(
            lane < HD,
            jnp.broadcast_to(logs[:rows], (rows, 2 * HD)),
            jnp.broadcast_to(logs[rows:], (rows, 2 * HD)),
        ).T
        log_ref[0, 0:1, r0:r1] = logs[0:1]
        log_ref[0, 1:2, r0:r1] = logs[HD : HD + 1]


def attend_forward(mixed, starts, slopes, seqs, rows=256):
    length, pairs = mixed.shape[0] // seqs, mixed.shape[1] // (6 * HD)

    def part(i):
        return pl.BlockSpec((length, 2 * HD), lambda s, p, *_: (s, i * pairs + p))

    return pl.pallas_call(
        partial(attend_kernel, rows=rows, scale=HD**-0.5),
        grid_spec=pltpu.PrefetchScalarGridSpec(
            num_scalar_prefetch=1,
            grid=(seqs, pairs),
            in_specs=[
                pl.BlockSpec((1, length, 1), lambda s, p, *_: (s, 0, 0)),
                part(0),
                part(1),
                part(2),
            ],
            out_specs=[part(0), pl.BlockSpec((1, 2, length), lambda s, p, *_: (s * pairs + p, 0, 0))],
            scratch_shapes=[pltpu.VMEM((length, length), f32)],
        ),
        out_shape=[
            jax.ShapeDtypeStruct((mixed.shape[0], 2 * HD * pairs), bf16),
            jax.ShapeDtypeStruct((seqs * pairs, 2, length), f32),
        ],
        compiler_params=pltpu.CompilerParams(vmem_limit_bytes=VMEM_LIMIT),
        cost_estimate=pl.CostEstimate(
            flops=16 * seqs * pairs * length * length * HD // CHEAP,
            bytes_accessed=4 * mixed.size // CHEAP,
            transcendentals=seqs * pairs * length * length // CHEAP,
        ),
        name="attend_forward",
    )(slopes, starts, mixed, mixed, mixed)


def attend_back_kernel(
    slope_ref,
    start_ref,
    log_ref,
    q_ref,
    k_ref,
    v_ref,
    g_ref,
    dq_ref,
    dk_ref,
    dv_ref,
    qs_ref,
    vs_ref,
    dist_ref,
    ka_ref,
    va_ref,
    *,
    rows,
    scale,
):
    pair = pl.program_id(1)
    length = k_ref.shape[0]

    @pl.when(pair == 0)
    def _():
        for r0 in range(0, length, rows):
            shape = (r0 + rows, rows)
            i = lax.broadcasted_iota(jnp.int32, shape, 1) + r0
            j = lax.broadcasted_iota(jnp.int32, shape, 0)
            allowed = (j <= i) & (j >= start_ref[0, :, r0 : r0 + rows])
            dist_ref[0 : r0 + rows, r0 : r0 + rows] = jnp.where(allowed, (j - i).astype(f32), far)

    slope_a, slope_b = slope_ref[2 * pair] * scale, slope_ref[2 * pair + 1] * scale
    query_sum = jnp.zeros((1, 2 * HD), f32)
    for r0 in reversed(range(0, length, rows)):
        r1 = r0 + rows
        q = pick_heads(q_ref[r0:r1, :] * jnp.asarray(scale, bf16))
        g = pick_heads(g_ref[r0:r1, :])
        k, v = k_ref[0:r1, :], v_ref[0:r1, :]
        s = lax.dot_general(k, q, NT, preferred_element_type=f32)
        d = dist_ref[0:r1, r0:r1]
        logs = jnp.concatenate([log_ref[0, 0:1, r0:r1], log_ref[0, 1:2, r0:r1]], axis=1)
        s = jnp.concatenate([s[:, :rows] + d * slope_a, s[:, rows:] + d * slope_b], axis=1)
        probs = jnp.exp(s - logs)
        t = lax.dot_general(v, g, NT, preferred_element_type=f32)
        centre = jnp.sum(probs * t, axis=0, keepdims=True)
        score_grad = (probs * (t - centre)).astype(bf16)
        value_part = jnp.dot(probs.astype(bf16), g, preferred_element_type=f32)
        key_part = jnp.dot(score_grad, q, preferred_element_type=f32)
        if r1 == length:
            va_ref[...] = value_part
            ka_ref[...] = key_part
        else:
            va_ref[0:r1, :] += value_part
            ka_ref[0:r1, :] += key_part
        dq = lax.dot_general(score_grad, k, TN, preferred_element_type=f32)
        lane = lax.broadcasted_iota(jnp.int32, (rows, 2 * HD), 1)
        dq = (jnp.where(lane < HD, dq[:rows], dq[rows:]) * scale).astype(bf16)
        dq_ref[r0:r1, :] = dq
        query_sum = query_sum + jnp.sum(dq.astype(f32), axis=0, keepdims=True)
    qs_ref[0] = query_sum
    dk_ref[...] = ka_ref[...].astype(bf16)
    dv = va_ref[...].astype(bf16)
    dv_ref[...] = dv
    vs_ref[0] = jnp.sum(dv.astype(f32), axis=0, keepdims=True)


def attend_backward(mixed, grads, starts, logs, slopes, seqs, rows=256):
    length, pairs = mixed.shape[0] // seqs, mixed.shape[1] // (6 * HD)

    def part(i):
        return pl.BlockSpec((length, 2 * HD), lambda s, p, *_: (s, i * pairs + p))

    out = jax.ShapeDtypeStruct(grads.shape, bf16)
    sums = jax.ShapeDtypeStruct((seqs, 1, grads.shape[1]), f32)
    sum_spec = pl.BlockSpec((1, 1, 2 * HD), lambda s, p, *_: (s, 0, p))
    return pl.pallas_call(
        partial(attend_back_kernel, rows=rows, scale=HD**-0.5),
        grid_spec=pltpu.PrefetchScalarGridSpec(
            num_scalar_prefetch=1,
            grid=(seqs, pairs),
            in_specs=[
                pl.BlockSpec((1, 1, length), lambda s, p, *_: (s, 0, 0)),
                pl.BlockSpec((1, 2, length), lambda s, p, *_: (s * pairs + p, 0, 0)),
                part(0),
                part(1),
                part(2),
                part(0),
            ],
            out_specs=[part(0), part(0), part(0), sum_spec, sum_spec],
            scratch_shapes=[
                pltpu.VMEM((length, length), f32),
                pltpu.VMEM((length, 2 * HD), f32),
                pltpu.VMEM((length, 2 * HD), f32),
            ],
        ),
        out_shape=[out, out, out, sums, sums],
        compiler_params=pltpu.CompilerParams(vmem_limit_bytes=VMEM_LIMIT),
        cost_estimate=pl.CostEstimate(
            flops=40 * seqs * pairs * length * length * HD // CHEAP,
            bytes_accessed=14 * grads.size // CHEAP,
            transcendentals=seqs * pairs * length * length // CHEAP,
        ),
        name="attend_backward",
    )(slopes, starts, logs, mixed, mixed, mixed, grads)


def resident(shape):
    return pl.BlockSpec(shape, lambda *_: (0,) * len(shape), pipeline_mode=pl.Buffered(1))


def kept_out(shape):
    return pl.BlockSpec(shape, lambda *_: (0,) * len(shape))


def flat_rows(ws):
    return jnp.concatenate([w[...] for w in ws], axis=0)


def matmul_call(kernel, grid, ins, outs, scratch, flops, name, prefetch=()):
    moved = sum(a.size * a.dtype.itemsize for a, _ in ins)
    moved += sum(jnp.dtype(t).itemsize * math.prod(s) for s, t, _ in outs)
    return pl.pallas_call(
        kernel,
        grid_spec=pltpu.PrefetchScalarGridSpec(
            num_scalar_prefetch=len(prefetch),
            grid=grid,
            in_specs=[s for _, s in ins],
            out_specs=[s for _, _, s in outs],
            scratch_shapes=scratch,
        ),
        out_shape=[jax.ShapeDtypeStruct(s, t) for s, t, _ in outs],
        compiler_params=pltpu.CompilerParams(vmem_limit_bytes=VMEM_LIMIT),
        cost_estimate=pl.CostEstimate(
            flops=flops // CHEAP, bytes_accessed=moved // CHEAP, transcendentals=0
        ),
        name=name,
    )(*prefetch, *[a for a, _ in ins])


def times_rows(x, ws, extras, outs, finish, name, tn, window=None, joins=()):
    tokens, depth = x.shape
    first, width = window or (0, ws[0].shape[1])
    first, tiles = first // tn, width // tn
    n_ws, n_ex, n_out = len(ws), len(extras), len(outs)
    steps = ws[0].shape[1] // tn if joins else tiles

    def kernel(*refs):
        x_ref, w_refs = refs[0], refs[1 : 1 + n_ws]
        extra, out = refs[1 + n_ws : 1 + n_ws + n_ex], refs[1 + n_ws + n_ex :]
        for places, joined in zip(joins, out[n_out:]):
            at = 0
            for i in places:
                joined[at : at + ws[i].shape[0], :] = w_refs[i][...]
                at += ws[i].shape[0]

        def multiply():
            acc = jnp.dot(x_ref[...], flat_rows(w_refs), preferred_element_type=f32)
            finish(acc, extra, out[:n_out])

        if steps == tiles:
            multiply()
        else:
            pl.when(pl.program_id(0) < tiles)(multiply)

    def spec(rows):
        return pl.BlockSpec((rows, tn), lambda n: (0, jnp.minimum(n, tiles - 1)))

    def tile(rows):
        return pl.BlockSpec((rows, tn), lambda n: (0, n + first))

    ins = [(x, resident(x.shape))] + [(w, tile(w.shape[0])) for w in ws]
    ins += [(e, spec(e.shape[0])) for e in extras]
    results = [(s, t, spec(s[0])) for s, t in outs]
    for places in joins:
        rows = sum(ws[i].shape[0] for i in places)
        results.append(((rows, ws[0].shape[1]), bf16, tile(rows)))
    return matmul_call(kernel, (steps,), ins, results, [], 2 * tokens * depth * width, name)


def times_columns(xs, ws, order, side, dtype, name, first=0, added=(), block=0, chunks=None):
    tokens = xs[0].shape[0]
    count = order.shape[1]
    n_xs = len(xs)
    width = sum(x.shape[1] for x in xs)
    chunks = chunks or [tokens]

    def kernel(order_ref, side_ref, *refs):
        x_refs, w_refs = refs[:n_xs], refs[n_xs : n_xs + 2]
        added_refs, out_refs = refs[n_xs + 2 : n_xs + 2 + len(added)], refs[-len(chunks) :]
        x = jnp.concatenate([r[...] for r in x_refs], axis=1)
        for i, w_ref in enumerate(w_refs):
            acc = lax.dot_general(x, w_ref[...], NT, preferred_element_type=f32)
            place = side_ref[0] if i == 0 else 1 - side_ref[0]
            place = pl.ds(pl.multiple_of(place * BLOCK, BLOCK), BLOCK)
            if added:
                acc = acc + jnp.concatenate([r[:, place] for r in added_refs]).astype(f32)
            at = 0
            for out_ref, height in zip(out_refs, chunks):
                out_ref[:, place] = acc[at : at + height].astype(dtype)
                at += height

    def w_spec(i):
        return pl.BlockSpec((BLOCK, width), lambda n, order_ref, _: (order_ref[i, n], first // width))

    def pair(height, start):
        return pl.BlockSpec((height, 2 * BLOCK), lambda n, *_: (0, start + n))

    ins = [(x, resident(x.shape)) for x in xs]
    ins += [(w, w_spec(i)) for i, w in enumerate(ws)]
    ins += [(b, pair(b.shape[0], block)) for b in added]
    done = matmul_call(
        kernel,
        (count,),
        ins,
        [((height, 2 * BLOCK * count), dtype, pair(height, 0)) for height in chunks],
        [],
        4 * tokens * BLOCK * count * width,
        name,
        prefetch=(order, side),
    )
    return done if len(chunks) > 1 else done[0]


def weight_rows(a, order, gs, name, groups=None, dtype=bf16):
    tokens = a.shape[0]
    width = sum(g.shape[1] for g in gs)
    count = order.shape[0]
    n_gs = len(gs)

    def kernel(order_ref, a_ref, *refs):
        g_refs, out_refs = refs[:n_gs], refs[n_gs:]
        g = jnp.concatenate([r[...] for r in g_refs], axis=1)
        acc = lax.dot_general(a_ref[...], g, TN, preferred_element_type=f32).astype(dtype)
        if groups is None:
            out_refs[0][...] = acc
            return
        for out_ref, group in zip(out_refs, groups):
            for j, i in enumerate(group):

                @pl.when(pl.program_id(0) == i)
                def _(out_ref=out_ref, rows=slice(j * BLOCK, (j + 1) * BLOCK)):
                    out_ref[rows, :] = acc

    ins = [(a, pl.BlockSpec((tokens, BLOCK), lambda i, order_ref: (0, order_ref[i])))]
    ins += [(g, resident(g.shape)) for g in gs]
    if groups is None:
        outs = [((count * BLOCK, width), dtype, pl.BlockSpec((BLOCK, width), lambda i, *_: (i, 0)))]
    else:
        shapes = [(len(group) * BLOCK, width) for group in groups]
        outs = [(shape, dtype, kept_out(shape)) for shape in shapes]
    done = matmul_call(
        kernel, (count,), ins, outs, [], 2 * tokens * BLOCK * count * width, name, prefetch=(order,)
    )
    return done[0] if groups is None else done


def place_blocks(values, place_ref, out_ref):
    at = 0
    for value in values:
        for c0 in range(0, value.shape[1], BLOCK):
            place = pl.ds(pl.multiple_of(place_ref[at] * BLOCK, BLOCK), BLOCK)
            out_ref[:, place] = value[:, c0 : c0 + BLOCK]
            at += 1


def lay_out(parts, places, name, tm=256):
    tokens, width = parts[0].shape
    full = width * len(parts)

    def kernel(place_ref, *refs):
        place_blocks([r[...] for r in refs[:-1]], place_ref, refs[-1])

    return matmul_call(
        kernel,
        (tokens // tm,),
        [(p, pl.BlockSpec((tm, width), lambda m, *_: (m, 0))) for p in parts],
        [((tokens, full), bf16, pl.BlockSpec((tm, full), lambda m, *_: (m, 0)))],
        [],
        tokens * full,
        name,
        prefetch=(places,),
    )[0]


def normalize(parts, gain, shift, places, name, tm=256):
    tokens, width = parts[0].shape
    n = len(parts)
    full = width * n

    def kernel(place_ref, *refs):
        gain_ref, shift_ref, out_ref, mean_ref, scale_ref = refs[n:]
        rows = [r[...].astype(f32) for r in refs[:n]]
        mean = sum(jnp.sum(v, axis=1, keepdims=True) for v in rows) / full
        square = sum(jnp.sum(v * v, axis=1, keepdims=True) for v in rows) / full
        scale = lax.rsqrt(square - mean * mean + norm_eps)
        mean_ref[...] = mean
        scale_ref[...] = scale
        done = []
        for i, v in enumerate(rows):
            cols = slice(i * width, (i + 1) * width)
            done.append(((v - mean) * scale * gain_ref[:, cols] + shift_ref[:, cols]).astype(bf16))
        place_blocks(done, place_ref, out_ref)

    ins = [(p, pl.BlockSpec((tm, width), lambda m, *_: (m, 0))) for p in parts]
    ins += [(gain, resident(gain.shape)), (shift, resident(shift.shape))]
    column = pl.BlockSpec((tm, 1), lambda m, *_: (m, 0))
    return matmul_call(
        kernel,
        (tokens // tm,),
        ins,
        [
            ((tokens, full), bf16, pl.BlockSpec((tm, full), lambda m, *_: (m, 0))),
            ((tokens, 1), f32, column),
            ((tokens, 1), f32, column),
        ],
        [],
        8 * tokens * full,
        name,
        prefetch=(places,),
    )


def swap(x, axis, bit):
    return lax.ppermute(x, axis, [(i, i ^ bit) for i in range(lax.axis_size(axis))])


def turn(x, steps):
    count = lax.axis_size("row")
    return lax.ppermute(x, "row", [(i, (i + 2 * steps) % count) for i in range(count)])


def sum_col_stats(stats):
    stats = stats + swap(stats, "col", 1)
    return stats + swap(stats, "col", 2)


def sum_rows(x):
    bit = 1
    while bit < lax.axis_size("row"):
        x = x + swap(x, "row", bit)
        bit *= 2
    return x


def after(x, *first):
    return lax.optimization_barrier((x,) + first)[0] if first else x


def outer_groups():
    outer = lax.axis_size("row") // 2
    return [[2 * i + inner for i in range(outer)] for inner in range(2)]


def find(ids, wanted):
    at = jnp.arange(ids.shape[0])
    return jnp.sum(jnp.where(ids[None, :] == wanted[:, None], at[None, :], 0), axis=1).astype(
        jnp.int32
    )


def gather_whole(w):
    return [lax.all_gather(w, "row", axis=0, tiled=True)]


def gather_outer(w):
    return lax.all_gather(w, "row", axis=0, tiled=True, axis_index_groups=outer_groups())


class Clock:
    def __init__(self):
        self.now, self.new = [], []

    def at(self, x):
        return after(x, *self.now)

    def put(self, *xs):
        self.new += xs

    def tick(self):
        self.now, self.new = self.new, []


def on_device(
    tokens,
    segments,
    gains,
    shifts,
    biases,
    mixing,
    projection,
    expand,
    thresholds,
    contract,
    cotangent,
):
    seqs = segments.shape[0]
    rows, cols = lax.axis_size("row"), lax.axis_size("col")
    row, col = lax.axis_index("row"), lax.axis_index("col")
    tokens_here, width = tokens.shape
    full = width * cols
    heads = width // HD
    stepped = full // rows == BLOCK and rows == 2 * cols
    blocks, per_col = full // BLOCK, width // BLOCK
    at = jnp.arange(blocks)
    ours = per_col * ((at // per_col) ^ col) + at % per_col
    place, side = row // 2, row % 2
    steps = jnp.arange(max(rows // 2, 1))
    back = (place - steps) % (rows // 2)
    if stepped:
        ids_attend = ids_expand = jnp.concatenate([2 * back + side, 2 * back + 1 - side])
        ids_contract = jnp.stack([2 * steps + side, 2 * steps + 1 - side], axis=1).reshape(-1)
    else:
        ids_attend = ids_expand = ids_contract = at
        side = 0 * side
    sides = jnp.reshape(side, (1,)).astype(jnp.int32)
    away = jnp.array([1, 3, 0, 2]) ^ col
    clock = Clock()
    at_now, put, tick = clock.at, clock.put, clock.tick

    def columns_order(ids, ws):
        want = jnp.stack([2 * away + side, 2 * away + 1 - side]).reshape(-1)
        order = find(ids, want).reshape(2, -1)
        return order if len(ws) == 1 else order % (blocks // 2)

    def two(ws):
        return ws if len(ws) == 2 else [ws[0], ws[0]]

    def columns_sent(xs, ws, ids, name, first=0, whole=False):
        order = columns_order(ids, ws)[:, :2]
        xs = [at_now(xs[0])] + xs[1:]
        chunks = [3 * tokens_here // 8, 3 * tokens_here // 8, tokens_here // 4]
        if whole:
            chunks = [tokens_here]
        sent = times_columns(
            xs, two(ws), order, sides, bf16, name + "_sent", first, chunks=chunks
        )
        if whole:
            put(sent)
        return [swap(v, "col", 1) for v in ([sent] if whole else sent)]

    def columns_part(xs, ws, ids, got, name, first=0):
        order = columns_order(ids, ws)[:, 3:]
        return times_columns(xs, two(ws), order, sides, bf16, name + "_part", first, got, 1)

    def columns_base(xs, ws, ids, got, name, first=0):
        order = columns_order(ids, ws)[:, 2:3]
        xs = [at_now(xs[0])] + xs[1:]
        return times_columns(xs, two(ws), order, sides, f32, name + "_base", first, got, 0)

    class WeightSum:
        def __init__(self, a, ids, gs, name, groups=None):
            self.a, self.ids, self.gs, self.name = a, ids, gs, name
            self.left = rows // 2
            self.groups = groups or [[k] for k in reversed(range(self.left))]
            self.got, self.kept, self.carry, self.result = {}, [], None, None
            self.last = []

        def cut(self):
            if stepped:
                other = find(self.ids, 2 * back + 1 - side)
                self.sent = list(
                    weight_rows(at_now(self.a), other, self.gs, self.name + "_other", self.groups)
                )
            else:
                self.sent = [
                    weight_rows(at_now(self.a), find(self.ids, at), self.gs, self.name, dtype=f32)
                ]
            put(*self.sent)

        def keep(self, *first):
            if stepped:
                mine = find(self.ids, 2 * back + side)
                a = after(at_now(self.a), *first)
                single = [[k] for k in range(rows // 2)]
                self.kept = weight_rows(a, mine, self.gs, self.name + "_mine", single)
                put(*self.kept)

        def move(self, *first, late=False):
            if stepped:
                if not self.groups:
                    return
                group = self.groups.pop(0)
                got = swap(after(at_now(self.sent.pop(0)), *first), "row", 1)
                self.last = [got]
                if not late:
                    put(got)
                for j, k in enumerate(group):
                    self.got[k] = (got, j * BLOCK)

        def add(self, *first):
            if not stepped:
                if self.result is None:
                    self.result = lax.psum_scatter(
                        self.sent[0], "row", scatter_dimension=0, tiled=True
                    )
                return
            self.left -= 1
            got, start = self.got[self.left]
            got = after(at_now(got), *first)[start : start + BLOCK]
            total = self.kept[self.left].astype(f32) + got.astype(f32)
            if self.carry is not None:
                total = total + self.carry.astype(f32)
            if self.left == 0:
                self.result = total
            else:
                self.carry = turn(total.astype(bf16), -1)
                put(self.carry)

    head_ids = (col * heads + jnp.arange(heads)).astype(f32)
    slopes = jnp.exp2(-8.0 * (head_ids + 1.0) / (heads * cols))
    starts = jnp.sum(segments[:, None, :] < segments[:, :, None], axis=2).astype(jnp.int32)
    start_column, start_row = starts[:, :, None], starts[:, None, :]
    places_attend, places_expand = find(ids_attend, ours), find(ids_expand, ours)
    places_contract = find(ids_contract, ours)
    mix_width = 3 * width
    mixed_bias = jnp.concatenate([biases[0:1], jnp.zeros((1, width), f32), biases[1:2]], axis=1)

    attend_rows = jnp.concatenate([mixing.reshape(mixing.shape[0], -1), projection], axis=1)
    small = jnp.concatenate([gains, shifts], axis=0)
    put(attend_rows)
    tick()
    if stepped:
        own, near = [attend_rows], []
    else:
        whole = gather_whole(attend_rows)[0]
        own, near = [whole[: full // 2]], [whole[full // 2 :]]
        full_expand = gather_whole(expand)
        full_contract = gather_whole(contract)

    def weight_step(k):
        if stepped:
            ready = at_now(own[k])
            near.append(swap(ready, "row", 1))
            put(near[k])
            if k + 1 < rows // 2:
                own.append(turn(ready, 1))
                put(own[k + 1])

    weight_step(0)
    tokens_now = at_now(tokens)
    token_parts = [tokens, swap(tokens_now, "col", 1), swap(tokens_now, "col", 2)]
    put(*token_parts[1:])
    tick()

    weight_step(1)
    cot_now = at_now(cotangent)
    cot_parts = [cotangent, swap(cot_now, "col", 1), swap(cot_now, "col", 2)]
    token_parts.append(swap(at_now(token_parts[2]), "col", 1))
    put(*cot_parts[1:], token_parts[3])
    tick()

    weight_step(2)
    small_now = at_now(small)
    norms = [small, swap(small_now, "col", 1), swap(small_now, "col", 2)]
    cot_parts.append(swap(at_now(cot_parts[2]), "col", 1))
    put(*norms[1:], cot_parts[3], start_column)
    tick()

    weight_step(3)
    norms.append(swap(at_now(norms[2]), "col", 1))
    norms = jnp.concatenate(norms, axis=1)
    first_full, first_mean, first_scale = normalize(
        token_parts, norms[0:1], norms[2:3], places_attend, "first_norm"
    )
    cot_full = lay_out([at_now(cot_parts[0])] + cot_parts[1:], places_contract, "cotangent_rows")
    put(first_full, cot_full)
    expand_own, expand_near = [expand], []

    def expand_turn(*first):
        if stepped:
            expand_own.append(turn(after(at_now(expand_own[-1]), *first), 1))
            put(expand_own[-1])

    def expand_step(k):
        if stepped:
            expand_near.append(swap(at_now(expand_own[k]), "row", 1))
            put(expand_near[k])

    expand_turn()
    tick()

    def add_bias(acc, extra, out):
        out[0][...] = (acc + extra[0][...]).astype(bf16)

    expand_step(0)
    if stepped:
        contract_pair = jnp.concatenate([contract, swap(at_now(contract), "row", 1)], axis=0)
        put(contract_pair)
    expand_turn()
    mixed, *full_attend = times_rows(
        at_now(first_full),
        own + near,
        [mixed_bias],
        [((tokens_here, mix_width), bf16)],
        add_bias,
        "mix",
        tn=width,
        window=(0, mix_width),
        joins=[range(len(own)), range(len(own), len(own) + len(near))],
    )
    expand_turn(mixed)
    attended, logs = attend_forward(mixed, start_column, slopes, seqs)
    put(attended)
    tick()

    if stepped:
        full_contract = [gather_outer(at_now(contract_pair))]
    expand_step(1)
    got = columns_sent([attended], full_attend, ids_attend, "project", mix_width)
    part = columns_part([attended], full_attend, ids_attend, got, "project", mix_width)
    put(part)
    tick()

    expand_step(2)
    across = swap(at_now(part), "col", 2)
    base = columns_base([attended], full_attend, ids_attend, got, "project", mix_width)
    resid = tokens.astype(f32)
    middle = resid + (base + across.astype(f32) + biases[2])
    middle_low = middle.astype(bf16)
    first_mean, first_scale = first_mean[:, 0], first_scale[:, 0]
    put(middle_low, first_mean, first_scale)
    tick()

    expand_step(3)
    middle_now = at_now(middle_low)
    middle_parts = [middle_low, swap(middle_now, "col", 1), swap(middle_now, "col", 2)]
    put(*middle_parts[1:])
    tick()

    middle_parts.append(swap(at_now(middle_parts[2]), "col", 1))
    second_full, second_mean, second_scale = normalize(
        middle_parts, norms[1:2], norms[3:4], places_expand, "second_norm"
    )
    put(second_full)
    tick()

    def activate(acc, extra, out):
        hidden = acc + extra[0][...]
        bell = 0.5 * (1.0 + lax.erf(hidden * sqrt_half))
        out[0][...] = (hidden * bell).astype(bf16)
        out[1][...] = bell + hidden * (jnp.exp(-0.5 * hidden * hidden) * inverse_root)

    hidden_shape = (tokens_here, expand.shape[1])
    active, slope, *joined = times_rows(
        at_now(second_full),
        expand_own + expand_near if stepped else full_expand,
        [thresholds[None]],
        [(hidden_shape, bf16), (hidden_shape, f32)],
        activate,
        "expand",
        tn=512,
        joins=[range(len(expand_own)), range(len(expand_own), 2 * len(expand_own))] if stepped else [],
    )
    if stepped:
        full_expand = joined
    contract_sum = WeightSum(
        cot_full, ids_contract, [active], "contract_grad", [[3], [2, 1], [0]]
    )
    contract_sum.cut()
    put(active)
    tick()

    def back_activate(acc, extra, out):
        grad = (acc * extra[0][...]).astype(bf16)
        out[0][...] = grad
        out[1][...] = jnp.sum(grad.astype(f32), axis=0, keepdims=True)

    second_mean, second_scale = at_now(second_mean)[:, 0], at_now(second_scale)[:, 0]
    put(second_mean, second_scale)
    contract_sum.move()
    contract_sum.keep()
    tick()

    contract_sum.add()
    contract_sum.move()
    hidden_grad, thresholds_part = times_rows(
        at_now(cot_full),
        full_contract,
        [slope],
        [(hidden_shape, bf16), ((1, hidden_shape[1]), f32)],
        back_activate,
        "contract_back",
        tn=512,
    )
    got = columns_sent([hidden_grad], full_expand, ids_expand, "expand_back")
    part = columns_part([hidden_grad], full_expand, ids_expand, got, "expand_back")
    across = swap(part, "col", 2)
    put(part)
    tick()

    contract_sum.add()
    contract_sum.move()
    base = columns_base([hidden_grad], full_expand, ids_expand, got, "expand_back")
    expand_sum = WeightSum(second_full, ids_expand, [hidden_grad], "expand_grad", [[3], [2, 1], [0]])
    expand_sum.cut()
    second_back = base + across.astype(f32)
    put(second_back)
    tick()

    def norm_back(upstream, centred, scale, gain):
        scaled = upstream * gain
        sums = sum_col_stats(
            jnp.stack([jnp.sum(scaled, axis=1), jnp.sum(scaled * centred, axis=1)])
        )
        result = scale[:, None] * (
            scaled - sums[0][:, None] / full - centred * (sums[1][:, None] / full)
        )
        return result, jnp.sum(upstream * centred, axis=0), jnp.sum(upstream, axis=0)

    expand_sum.move()
    second_centred = (middle - second_mean[:, None]) * second_scale[:, None]
    second_input, second_gain, second_shift = norm_back(
        at_now(second_back), second_centred, second_scale, gains[1]
    )
    cot_float = cotangent.astype(f32)
    middle_grad = cot_float + second_input
    branch_grad = middle_grad.astype(bf16)
    branch_parts = [branch_grad, swap(branch_grad, "col", 1), swap(branch_grad, "col", 2)]
    contract_sum.add(branch_grad)
    expand_sum.keep(branch_grad)
    out_got = columns_sent(
        [after(active, branch_grad)], full_contract, ids_contract, "contract", whole=True
    )
    put(*branch_parts[1:])
    tick()

    def store(acc, extra, out):
        out[0][...] = acc.astype(bf16)

    contract_sum.add()
    expand_sum.move()
    expand_sum.add()
    branch_parts.append(swap(at_now(branch_parts[2]), "col", 1))
    branch_full = lay_out(branch_parts, places_attend, "branch_rows")
    (attended_grad,) = times_rows(
        branch_full,
        full_attend,
        [],
        [((tokens_here, width), bf16)],
        store,
        "project_back",
        tn=width,
        window=(mix_width, width),
    )
    if stepped:
        project_other = weight_rows(
            branch_full,
            find(ids_attend, 2 * steps + 1 - side),
            [attended],
            "projection_grad_other",
        )
        put(project_other)
    else:
        project_sum = WeightSum(branch_full, ids_attend, [attended], "projection_grad", None)
        project_sum.cut()
    query_back, key_back, value_back, query_sum, value_sum = attend_backward(
        mixed, attended_grad, start_row, logs, slopes, seqs
    )
    mixed_grads = [query_back, key_back, value_back]
    put(query_back)
    tick()

    expand_sum.move()
    if stepped:
        project_got = swap(at_now(project_other), "row", 1)
        put(project_got)
    expand_sum.add()
    got = columns_sent(mixed_grads, full_attend, ids_attend, "mix_back")
    mixing_sum = WeightSum(
        first_full, ids_attend, mixed_grads, "mixing_grad", [[3], [2], [1], [0]]
    )
    mixing_sum.cut()
    part = columns_part(mixed_grads, full_attend, ids_attend, got, "mix_back")
    across = swap(part, "col", 2)
    expand_sum.add()
    base = columns_base(mixed_grads, full_attend, ids_attend, got, "mix_back")
    if stepped:
        project_mine = weight_rows(
            after(branch_full, part),
            find(ids_attend, 2 * steps + side),
            [attended],
            "projection_grad_mine",
        )
        put(project_mine)
    first_back = base + across.astype(f32)
    put(first_back)
    tick()

    if stepped:
        total = at_now(project_mine).astype(f32) + project_got.astype(f32)
        projection_grad = lax.psum_scatter(
            total.astype(bf16),
            "row",
            scatter_dimension=0,
            tiled=True,
            axis_index_groups=outer_groups(),
        ).astype(f32)
    else:
        project_sum.add()
        projection_grad = project_sum.result
    expand_sum.add()
    mixing_sum.move()
    mixing_sum.keep()
    first_centred = (resid - first_mean[:, None]) * first_scale[:, None]
    first_input, first_gain, first_shift = norm_back(
        at_now(first_back), first_centred, first_scale, gains[0]
    )
    tokens_grad = middle_grad + first_input
    small = jnp.stack(
        [
            first_gain,
            second_gain,
            first_shift,
            second_shift,
            jnp.sum(query_sum, axis=(0, 1)),
            jnp.sum(value_sum, axis=(0, 1)),
            jnp.sum(branch_grad.astype(f32), axis=0),
            jnp.sum(cot_float, axis=0),
        ]
    )
    small = jnp.concatenate([small, thresholds_part.reshape(-1, width)], axis=0)
    def small_step(bit):
        return small + swap(at_now(small), "row", bit) if bit < rows else small

    put(small)
    tick()

    mixing_sum.add()
    mixing_sum.move()
    out_part = columns_part([at_now(active)], full_contract, ids_contract, out_got, "contract")
    small = small_step(2)
    put(out_part, small)
    tick()

    mixing_sum.add()
    mixing_sum.move()
    out_across = swap(at_now(out_part), "col", 2)
    out_base = columns_base([active], full_contract, ids_contract, out_got, "contract")
    layer_out = (middle + (out_base + out_across.astype(f32) + biases[3])).astype(bf16)
    small = small_step(4)
    put(small, projection_grad, out_base)
    tick()

    mixing_sum.add()
    mixing_sum.move()
    bit = 8
    while bit < rows:
        small = small_step(bit)
        put(small)
        tick()
        bit *= 2
    small = small_step(1)
    put(small)
    tick()
    mixing_sum.add()
    contract_grad, expand_grad = contract_sum.result, expand_sum.result
    mixing_grad = mixing_sum.result
    mixing_grad = jnp.stack(
        [mixing_grad[:, i * width : (i + 1) * width] for i in range(3)], axis=1
    )
    return (
        layer_out,
        tokens_grad,
        small[0:2],
        small[2:4],
        small[4:8],
        mixing_grad,
        projection_grad,
        expand_grad,
        small[8:].reshape(thresholds.shape),
        contract_grad,
    )


def solution(mesh):
    return jax.shard_map(
        on_device,
        mesh=mesh,
        in_specs=(
            P("row", "col"),
            P("row", None),
            P(None, "col"),
            P(None, "col"),
            P(None, "col"),
            P("row", None, "col"),
            P("row", "col"),
            P("row", "col"),
            P("col"),
            P("row", "col"),
            P("row", "col"),
        ),
        out_specs=(
            P("row", "col"),
            P("row", "col"),
            P(None, "col"),
            P(None, "col"),
            P(None, "col"),
            P("row", None, "col"),
            P("row", "col"),
            P("row", "col"),
            P("col"),
            P("row", "col"),
        ),
        check_vma=False,
    )
```

```python
import math
from functools import partial

import jax
import jax.numpy as jnp
from jax import lax
from jax.experimental import pallas as pl
from jax.experimental.pallas import tpu as pltpu
from jax.sharding import PartitionSpec as P

HD = 64
BLOCK = 256

norm_eps = 1e-05
sqrt_half = 0.7071067811865476
inverse_root = 0.3989422804014327
far = -1e33
NT = (((1,), (1,)), ((), ()))
TN = (((0,), (0,)), ((), ()))
VMEM_LIMIT = 40 << 20
CHEAP = 64
f32 = jnp.float32
bf16 = jnp.bfloat16


def pick_heads(pair):
    lane = lax.broadcasted_iota(jnp.int32, pair.shape, 1)
    zero = jnp.zeros_like(pair)
    return jnp.concatenate(
        [jnp.where(lane < HD, pair, zero), jnp.where(lane < HD, zero, pair)], axis=0
    )


def attend_kernel(
    slope_ref, start_ref, q_ref, k_ref, v_ref, out_ref, log_ref, dist_ref, *, rows, scale
):
    pair = pl.program_id(1)
    length = k_ref.shape[0]

    @pl.when(pair == 0)
    def _():
        for r0 in range(0, length, rows):
            shape = (rows, r0 + rows)
            i = lax.broadcasted_iota(jnp.int32, shape, 0) + r0
            j = lax.broadcasted_iota(jnp.int32, shape, 1)
            allowed = (j <= i) & (j >= start_ref[0, r0 : r0 + rows, :])
            dist_ref[r0 : r0 + rows, 0 : r0 + rows] = jnp.where(allowed, (j - i).astype(f32), far)

    slope_a, slope_b = slope_ref[2 * pair] * scale, slope_ref[2 * pair + 1] * scale
    for r0 in range(0, length, rows):
        r1 = r0 + rows
        q = pick_heads(q_ref[r0:r1, :] * jnp.asarray(scale, bf16))
        s = lax.dot_general(q, k_ref[0:r1, :], NT, preferred_element_type=f32)
        d = dist_ref[r0:r1, 0:r1]
        s = jnp.concatenate([s[:rows] + d * slope_a, s[rows:] + d * slope_b], axis=0)
        row_max = jnp.max(s, axis=1, keepdims=True)
        weights = jnp.exp(s - row_max)
        row_total = jnp.sum(weights, axis=1, keepdims=True)
        probs = (weights * (1.0 / row_total)).astype(bf16)
        o = jnp.dot(probs, v_ref[0:r1, :], preferred_element_type=f32)
        lane = lax.broadcasted_iota(jnp.int32, (rows, 2 * HD), 1)
        out_ref[r0:r1, :] = jnp.where(lane < HD, o[:rows], o[rows:]).astype(bf16)
        logs = row_max + jnp.log(row_total)
        logs = jnp.where(
            lane < HD,
            jnp.broadcast_to(logs[:rows], (rows, 2 * HD)),
            jnp.broadcast_to(logs[rows:], (rows, 2 * HD)),
        ).T
        log_ref[0, 0:1, r0:r1] = logs[0:1]
        log_ref[0, 1:2, r0:r1] = logs[HD : HD + 1]


def attend_forward(mixed, starts, slopes, seqs, rows=256):
    length, pairs = mixed.shape[0] // seqs, mixed.shape[1] // (6 * HD)

    def part(i):
        return pl.BlockSpec((length, 2 * HD), lambda s, p, *_: (s, i * pairs + p))

    return pl.pallas_call(
        partial(attend_kernel, rows=rows, scale=HD**-0.5),
        grid_spec=pltpu.PrefetchScalarGridSpec(
            num_scalar_prefetch=1,
            grid=(seqs, pairs),
            in_specs=[
                pl.BlockSpec((1, length, 1), lambda s, p, *_: (s, 0, 0)),
                part(0),
                part(1),
                part(2),
            ],
            out_specs=[part(0), pl.BlockSpec((1, 2, length), lambda s, p, *_: (s * pairs + p, 0, 0))],
            scratch_shapes=[pltpu.VMEM((length, length), f32)],
        ),
        out_shape=[
            jax.ShapeDtypeStruct((mixed.shape[0], 2 * HD * pairs), bf16),
            jax.ShapeDtypeStruct((seqs * pairs, 2, length), f32),
        ],
        compiler_params=pltpu.CompilerParams(vmem_limit_bytes=VMEM_LIMIT),
        cost_estimate=pl.CostEstimate(
            flops=16 * seqs * pairs * length * length * HD // CHEAP,
            bytes_accessed=4 * mixed.size // CHEAP,
            transcendentals=seqs * pairs * length * length // CHEAP,
        ),
        name="attend_forward",
    )(slopes, starts, mixed, mixed, mixed)


def attend_back_kernel(
    slope_ref,
    start_ref,
    log_ref,
    q_ref,
    k_ref,
    v_ref,
    g_ref,
    dq_ref,
    dk_ref,
    dv_ref,
    qs_ref,
    vs_ref,
    dist_ref,
    ka_ref,
    va_ref,
    *,
    rows,
    scale,
):
    pair = pl.program_id(1)
    length = k_ref.shape[0]

    @pl.when(pair == 0)
    def _():
        for r0 in range(0, length, rows):
            shape = (r0 + rows, rows)
            i = lax.broadcasted_iota(jnp.int32, shape, 1) + r0
            j = lax.broadcasted_iota(jnp.int32, shape, 0)
            allowed = (j <= i) & (j >= start_ref[0, :, r0 : r0 + rows])
            dist_ref[0 : r0 + rows, r0 : r0 + rows] = jnp.where(allowed, (j - i).astype(f32), far)

    slope_a, slope_b = slope_ref[2 * pair] * scale, slope_ref[2 * pair + 1] * scale
    query_sum = jnp.zeros((1, 2 * HD), f32)
    for r0 in reversed(range(0, length, rows)):
        r1 = r0 + rows
        q = pick_heads(q_ref[r0:r1, :] * jnp.asarray(scale, bf16))
        g = pick_heads(g_ref[r0:r1, :])
        k, v = k_ref[0:r1, :], v_ref[0:r1, :]
        s = lax.dot_general(k, q, NT, preferred_element_type=f32)
        d = dist_ref[0:r1, r0:r1]
        logs = jnp.concatenate([log_ref[0, 0:1, r0:r1], log_ref[0, 1:2, r0:r1]], axis=1)
        s = jnp.concatenate([s[:, :rows] + d * slope_a, s[:, rows:] + d * slope_b], axis=1)
        probs = jnp.exp(s - logs)
        t = lax.dot_general(v, g, NT, preferred_element_type=f32)
        centre = jnp.sum(probs * t, axis=0, keepdims=True)
        score_grad = (probs * (t - centre)).astype(bf16)
        value_part = jnp.dot(probs.astype(bf16), g, preferred_element_type=f32)
        key_part = jnp.dot(score_grad, q, preferred_element_type=f32)
        if r1 == length:
            va_ref[...] = value_part
            ka_ref[...] = key_part
        else:
            va_ref[0:r1, :] += value_part
            ka_ref[0:r1, :] += key_part
        dq = lax.dot_general(score_grad, k, TN, preferred_element_type=f32)
        lane = lax.broadcasted_iota(jnp.int32, (rows, 2 * HD), 1)
        dq = (jnp.where(lane < HD, dq[:rows], dq[rows:]) * scale).astype(bf16)
        dq_ref[r0:r1, :] = dq
        query_sum = query_sum + jnp.sum(dq.astype(f32), axis=0, keepdims=True)
    qs_ref[0] = query_sum
    dk_ref[...] = ka_ref[...].astype(bf16)
    dv = va_ref[...].astype(bf16)
    dv_ref[...] = dv
    vs_ref[0] = jnp.sum(dv.astype(f32), axis=0, keepdims=True)


def attend_backward(mixed, grads, starts, logs, slopes, seqs, rows=256):
    length, pairs = mixed.shape[0] // seqs, mixed.shape[1] // (6 * HD)

    def part(i):
        return pl.BlockSpec((length, 2 * HD), lambda s, p, *_: (s, i * pairs + p))

    out = jax.ShapeDtypeStruct(grads.shape, bf16)
    sums = jax.ShapeDtypeStruct((seqs, 1, grads.shape[1]), f32)
    sum_spec = pl.BlockSpec((1, 1, 2 * HD), lambda s, p, *_: (s, 0, p))
    return pl.pallas_call(
        partial(attend_back_kernel, rows=rows, scale=HD**-0.5),
        grid_spec=pltpu.PrefetchScalarGridSpec(
            num_scalar_prefetch=1,
            grid=(seqs, pairs),
            in_specs=[
                pl.BlockSpec((1, 1, length), lambda s, p, *_: (s, 0, 0)),
                pl.BlockSpec((1, 2, length), lambda s, p, *_: (s * pairs + p, 0, 0)),
                part(0),
                part(1),
                part(2),
                part(0),
            ],
            out_specs=[part(0), part(0), part(0), sum_spec, sum_spec],
            scratch_shapes=[
                pltpu.VMEM((length, length), f32),
                pltpu.VMEM((length, 2 * HD), f32),
                pltpu.VMEM((length, 2 * HD), f32),
            ],
        ),
        out_shape=[out, out, out, sums, sums],
        compiler_params=pltpu.CompilerParams(vmem_limit_bytes=VMEM_LIMIT),
        cost_estimate=pl.CostEstimate(
            flops=40 * seqs * pairs * length * length * HD // CHEAP,
            bytes_accessed=14 * grads.size // CHEAP,
            transcendentals=seqs * pairs * length * length // CHEAP,
        ),
        name="attend_backward",
    )(slopes, starts, logs, mixed, mixed, mixed, grads)


def resident(shape):
    return pl.BlockSpec(shape, lambda *_: (0,) * len(shape), pipeline_mode=pl.Buffered(1))


def kept_out(shape):
    return pl.BlockSpec(shape, lambda *_: (0,) * len(shape))


def flat_rows(ws):
    return jnp.concatenate([w[...] for w in ws], axis=0)


def matmul_call(kernel, grid, ins, outs, scratch, flops, name, prefetch=()):
    moved = sum(a.size * a.dtype.itemsize for a, _ in ins)
    moved += sum(jnp.dtype(t).itemsize * math.prod(s) for s, t, _ in outs)
    return pl.pallas_call(
        kernel,
        grid_spec=pltpu.PrefetchScalarGridSpec(
            num_scalar_prefetch=len(prefetch),
            grid=grid,
            in_specs=[s for _, s in ins],
            out_specs=[s for _, _, s in outs],
            scratch_shapes=scratch,
        ),
        out_shape=[jax.ShapeDtypeStruct(s, t) for s, t, _ in outs],
        compiler_params=pltpu.CompilerParams(vmem_limit_bytes=VMEM_LIMIT),
        cost_estimate=pl.CostEstimate(
            flops=flops // CHEAP, bytes_accessed=moved // CHEAP, transcendentals=0
        ),
        name=name,
    )(*prefetch, *[a for a, _ in ins])


def times_rows(x, ws, extras, outs, finish, name, tn, window=None, joins=(), skip=0):
    tokens, depth = x.shape
    picks = [w[1] if isinstance(w, tuple) else None for w in ws]
    ws = [w[0] if isinstance(w, tuple) else w for w in ws]
    first, width = window or (0, ws[0].shape[1])
    first, tiles = first // tn, width // tn
    n_ws, n_ex, n_out = len(ws), len(extras), len(outs)
    steps = ws[0].shape[1] // tn if joins else tiles

    def kernel(*refs):
        x_ref, w_refs = refs[0], refs[1 : 1 + n_ws]
        extra, out = refs[1 + n_ws : 1 + n_ws + n_ex], refs[1 + n_ws + n_ex :]
        for places, joined in zip(joins, out[n_out:]):
            at = 0
            for i in places:
                joined[at : at + ws[i].shape[0], :] = w_refs[i][...]
                at += ws[i].shape[0]

        def multiply():
            acc = jnp.dot(x_ref[...], flat_rows(w_refs), preferred_element_type=f32)
            finish(acc, extra, out[:n_out])

        if steps == tiles:
            multiply()
        else:
            pl.when(pl.program_id(0) < tiles)(multiply)

    def spec(rows, skipped=0):
        return pl.BlockSpec((rows, tn), lambda n: (0, jnp.minimum(n, tiles - 1) + skipped))

    def tile(rows, pick=None):
        if pick is not None:
            return pl.BlockSpec((BLOCK, tn), lambda n: (pick, n + first))
        return pl.BlockSpec((rows, tn), lambda n: (0, n + first))

    ins = [(x, resident(x.shape))]
    ins += [(w, tile(w.shape[0], pick)) for w, pick in zip(ws, picks)]
    ins += [(e, spec(e.shape[0], skip // tn)) for e in extras]
    results = [(s, t, spec(s[0])) for s, t in outs]
    for places in joins:
        rows = sum(ws[i].shape[0] for i in places)
        results.append(((rows, ws[0].shape[1]), bf16, tile(rows)))
    return matmul_call(kernel, (steps,), ins, results, [], 2 * tokens * depth * width, name)


def times_columns(xs, ws, order, side, dtype, name, added=(), block=0, chunks=None):
    tokens = xs[0].shape[0]
    count = order.shape[1]
    n_xs = len(xs)
    width = sum(x.shape[1] for x in xs)
    chunks = chunks or [tokens]
    n_ws = len(ws[0])

    def kernel(order_ref, side_ref, *refs):
        x_refs, w_refs = refs[:n_xs], refs[n_xs : n_xs + 2 * n_ws]
        after_ws = n_xs + 2 * n_ws
        added_refs, out_refs = refs[after_ws : after_ws + len(added)], refs[-len(chunks) :]
        x = jnp.concatenate([r[...] for r in x_refs], axis=1)
        for i in range(2):
            w = jnp.concatenate([r[...] for r in w_refs[i * n_ws : (i + 1) * n_ws]], axis=1)
            acc = lax.dot_general(x, w, NT, preferred_element_type=f32)
            place = side_ref[0] if i == 0 else 1 - side_ref[0]
            place = pl.ds(pl.multiple_of(place * BLOCK, BLOCK), BLOCK)
            if added:
                acc = acc + jnp.concatenate([r[:, place] for r in added_refs]).astype(f32)
            at = 0
            for out_ref, height in zip(out_refs, chunks):
                out_ref[:, place] = acc[at : at + height].astype(dtype)
                at += height

    def w_spec(i, over, start, columns):
        return pl.BlockSpec(
            (BLOCK, columns), lambda n, order_ref, _: (order_ref[i, n] // over, start // columns)
        )

    def pair(height, start):
        return pl.BlockSpec((height, 2 * BLOCK), lambda n, *_: (0, start + n))

    ins = [(x, resident(x.shape)) for x in xs]
    ins += [(w, w_spec(i, *rest)) for i, part in enumerate(ws) for w, *rest in part]
    ins += [(b, pair(b.shape[0], block)) for b in added]
    done = matmul_call(
        kernel,
        (count,),
        ins,
        [((height, 2 * BLOCK * count), dtype, pair(height, 0)) for height in chunks],
        [],
        4 * tokens * BLOCK * count * width,
        name,
        prefetch=(order, side),
    )
    return done if len(chunks) > 1 else done[0]


def weight_rows(a, order, gs, name, groups=None, dtype=bf16):
    tokens = a.shape[0]
    width = sum(g.shape[1] for g in gs)
    count = order.shape[0]
    n_gs = len(gs)

    def kernel(order_ref, a_ref, *refs):
        g_refs, out_refs = refs[:n_gs], refs[n_gs:]
        g = jnp.concatenate([r[...] for r in g_refs], axis=1)
        acc = lax.dot_general(a_ref[...], g, TN, preferred_element_type=f32).astype(dtype)
        if groups is None:
            out_refs[0][...] = acc
            return
        for out_ref, group in zip(out_refs, groups):
            for j, i in enumerate(group):

                @pl.when(pl.program_id(0) == i)
                def _(out_ref=out_ref, rows=slice(j * BLOCK, (j + 1) * BLOCK)):
                    out_ref[rows, :] = acc

    ins = [(a, pl.BlockSpec((tokens, BLOCK), lambda i, order_ref: (0, order_ref[i])))]
    ins += [(g, resident(g.shape)) for g in gs]
    if groups is None:
        outs = [((count * BLOCK, width), dtype, pl.BlockSpec((BLOCK, width), lambda i, *_: (i, 0)))]
    else:
        shapes = [(len(group) * BLOCK, width) for group in groups]
        outs = [(shape, dtype, kept_out(shape)) for shape in shapes]
    done = matmul_call(
        kernel, (count,), ins, outs, [], 2 * tokens * BLOCK * count * width, name, prefetch=(order,)
    )
    return done[0] if groups is None else done


def place_blocks(values, place_ref, out_ref):
    at = 0
    for value in values:
        for c0 in range(0, value.shape[1], BLOCK):
            place = pl.ds(pl.multiple_of(place_ref[at] * BLOCK, BLOCK), BLOCK)
            out_ref[:, place] = value[:, c0 : c0 + BLOCK]
            at += 1


def lay_out(parts, places, name, tm=256):
    tokens, width = parts[0].shape
    full = width * len(parts)

    def kernel(place_ref, *refs):
        place_blocks([r[...] for r in refs[:-1]], place_ref, refs[-1])

    return matmul_call(
        kernel,
        (tokens // tm,),
        [(p, pl.BlockSpec((tm, width), lambda m, *_: (m, 0))) for p in parts],
        [((tokens, full), bf16, pl.BlockSpec((tm, full), lambda m, *_: (m, 0)))],
        [],
        tokens * full,
        name,
        prefetch=(places,),
    )[0]


def normalize(parts, gain, shift, places, name, tm=256):
    tokens, width = parts[0].shape
    n = len(parts)
    full = width * n

    def kernel(place_ref, *refs):
        gain_ref, shift_ref, out_ref, mean_ref, scale_ref = refs[n:]
        rows = [r[...].astype(f32) for r in refs[:n]]
        mean = sum(jnp.sum(v, axis=1, keepdims=True) for v in rows) / full
        square = sum(jnp.sum(v * v, axis=1, keepdims=True) for v in rows) / full
        scale = lax.rsqrt(square - mean * mean + norm_eps)
        mean_ref[...] = mean
        scale_ref[...] = scale
        done = []
        for i, v in enumerate(rows):
            cols = slice(i * width, (i + 1) * width)
            done.append(((v - mean) * scale * gain_ref[:, cols] + shift_ref[:, cols]).astype(bf16))
        place_blocks(done, place_ref, out_ref)

    ins = [(p, pl.BlockSpec((tm, width), lambda m, *_: (m, 0))) for p in parts]
    ins += [(gain, resident(gain.shape)), (shift, resident(shift.shape))]
    column = pl.BlockSpec((tm, 1), lambda m, *_: (m, 0))
    return matmul_call(
        kernel,
        (tokens // tm,),
        ins,
        [
            ((tokens, full), bf16, pl.BlockSpec((tm, full), lambda m, *_: (m, 0))),
            ((tokens, 1), f32, column),
            ((tokens, 1), f32, column),
        ],
        [],
        8 * tokens * full,
        name,
        prefetch=(places,),
    )


def swap(x, axis, bit):
    return lax.ppermute(x, axis, [(i, i ^ bit) for i in range(lax.axis_size(axis))])


def turn(x, steps):
    count = lax.axis_size("row")
    return lax.ppermute(x, "row", [(i, (i + 2 * steps) % count) for i in range(count)])


def sum_col_stats(stats):
    stats = stats + swap(stats, "col", 1)
    return stats + swap(stats, "col", 2)


def sum_rows(x):
    bit = 1
    while bit < lax.axis_size("row"):
        x = x + swap(x, "row", bit)
        bit *= 2
    return x


def after(x, *first):
    return lax.optimization_barrier((x,) + first)[0] if first else x


def outer_groups():
    outer = lax.axis_size("row") // 2
    return [[2 * i + inner for i in range(outer)] for inner in range(2)]


def find(ids, wanted):
    at = jnp.arange(ids.shape[0])
    return jnp.sum(jnp.where(ids[None, :] == wanted[:, None], at[None, :], 0), axis=1).astype(
        jnp.int32
    )


def gather_whole(w):
    return [lax.all_gather(w, "row", axis=0, tiled=True)]


def gather_outer(w):
    return lax.all_gather(w, "row", axis=0, tiled=True, axis_index_groups=outer_groups())


class Clock:
    def __init__(self):
        self.now, self.new = [], []

    def at(self, x):
        return after(x, *self.now)

    def put(self, *xs):
        self.new += xs

    def tick(self):
        self.now, self.new = self.new, []


def on_device(
    tokens,
    segments,
    gains,
    shifts,
    biases,
    mixing,
    projection,
    expand,
    thresholds,
    contract,
    cotangent,
):
    seqs = segments.shape[0]
    rows, cols = lax.axis_size("row"), lax.axis_size("col")
    row, col = lax.axis_index("row"), lax.axis_index("col")
    tokens_here, width = tokens.shape
    full = width * cols
    heads = width // HD
    stepped = full // rows == BLOCK and rows == 2 * cols
    blocks, per_col = full // BLOCK, width // BLOCK
    at = jnp.arange(blocks)
    ours = per_col * ((at // per_col) ^ col) + at % per_col
    place, side = row // 2, row % 2
    steps = jnp.arange(max(rows // 2, 1))
    back = (place - steps) % (rows // 2)
    if stepped:
        ids_attend = ids_expand = jnp.concatenate([2 * back + side, 2 * back + 1 - side])
        ids_contract = jnp.stack([2 * steps + side, 2 * steps + 1 - side], axis=1).reshape(-1)
    else:
        ids_attend = ids_expand = ids_contract = at
        side = 0 * side
    sides = jnp.reshape(side, (1,)).astype(jnp.int32)
    away = jnp.array([1, 3, 0, 2]) ^ col
    clock = Clock()
    at_now, put, tick = clock.at, clock.put, clock.tick

    def columns_order(ids, ws):
        want = jnp.stack([2 * away + side, 2 * away + 1 - side]).reshape(-1)
        order = find(ids, want).reshape(2, -1)
        return order if len(ws) != 2 else order % (blocks // 2)

    def two(xs, ws, first):
        columns = sum(x.shape[1] for x in xs)
        if len(ws) <= 2:
            return [[(w, 1, first, columns)] for w in (ws if len(ws) == 2 else [ws[0], ws[0]])]
        half = columns // 2
        return [[(w, 2, 0, half), (ws[2], 1, 0, half)] for w in ws[:2]]

    def columns_sent(xs, ws, ids, name, first=0, whole=False):
        order = columns_order(ids, ws)[:, :2]
        xs = [at_now(xs[0])] + xs[1:]
        chunks = [3 * tokens_here // 8, 3 * tokens_here // 8, tokens_here // 4]
        if whole:
            chunks = [tokens_here]
        sent = times_columns(
            xs, two(xs, ws, first), order, sides, bf16, name + "_sent", chunks=chunks
        )
        if whole:
            put(sent)
        return [swap(v, "col", 1) for v in ([sent] if whole else sent)]

    def columns_part(xs, ws, ids, got, name, first=0):
        order = columns_order(ids, ws)[:, 3:]
        return times_columns(xs, two(xs, ws, first), order, sides, bf16, name + "_part", got, 1)

    def columns_base(xs, ws, ids, got, name, first=0):
        order = columns_order(ids, ws)[:, 2:3]
        xs = [at_now(xs[0])] + xs[1:]
        return times_columns(xs, two(xs, ws, first), order, sides, f32, name + "_base", got, 0)

    class WeightSum:
        def __init__(self, a, ids, gs, name, groups=None):
            self.a, self.ids, self.gs, self.name = a, ids, gs, name
            self.left = rows // 2
            self.groups = groups or [[k] for k in reversed(range(self.left))]
            self.got, self.kept, self.carry, self.result = {}, [], None, None
            self.last = []

        def cut(self):
            if stepped:
                other = find(self.ids, 2 * back + 1 - side)
                self.sent = list(
                    weight_rows(at_now(self.a), other, self.gs, self.name + "_other", self.groups)
                )
            else:
                self.sent = [
                    weight_rows(at_now(self.a), find(self.ids, at), self.gs, self.name, dtype=f32)
                ]
            put(*self.sent)

        def keep(self, *first):
            if stepped:
                mine = find(self.ids, 2 * back + side)
                a = after(at_now(self.a), *first)
                single = [[k] for k in range(rows // 2)]
                self.kept = weight_rows(a, mine, self.gs, self.name + "_mine", single)
                put(*self.kept)

        def move(self, *first, late=False):
            if stepped:
                if not self.groups:
                    return
                group = self.groups.pop(0)
                got = swap(after(at_now(self.sent.pop(0)), *first), "row", 1)
                self.last = [got]
                if not late:
                    put(got)
                for j, k in enumerate(group):
                    self.got[k] = (got, j * BLOCK)

        def add(self, *first):
            if not stepped:
                if self.result is None:
                    self.result = lax.psum_scatter(
                        self.sent[0], "row", scatter_dimension=0, tiled=True
                    )
                return
            self.left -= 1
            got, start = self.got[self.left]
            got = after(at_now(got), *first)[start : start + BLOCK]
            total = self.kept[self.left].astype(f32) + got.astype(f32)
            if self.carry is not None:
                total = total + self.carry.astype(f32)
            if self.left == 0:
                self.result = total
            else:
                self.carry = turn(total.astype(bf16), -1)
                put(self.carry)

    head_ids = (col * heads + jnp.arange(heads)).astype(f32)
    slopes = jnp.exp2(-8.0 * (head_ids + 1.0) / (heads * cols))
    starts = jnp.sum(segments[:, None, :] < segments[:, :, None], axis=2).astype(jnp.int32)
    start_column, start_row = starts[:, :, None], starts[:, None, :]
    places_attend, places_expand = find(ids_attend, ours), find(ids_expand, ours)
    places_contract = find(ids_contract, ours)
    mix_width = 3 * width
    mixed_bias = jnp.concatenate([biases[0:1], jnp.zeros((1, width), f32), biases[1:2]], axis=1)

    attend_rows = jnp.concatenate([mixing.reshape(mixing.shape[0], -1), projection], axis=1)
    small = jnp.concatenate([gains, shifts], axis=0)
    put(attend_rows)
    tick()
    if stepped:
        own, near = [attend_rows], []
    else:
        whole = gather_whole(attend_rows)[0]
        own, near = [whole[: full // 2]], [whole[full // 2 :]]
        full_expand = gather_whole(expand)
        full_contract = gather_whole(contract)

    def weight_step(k):
        if stepped:
            ready = at_now(own[k])
            near.append(swap(ready, "row", 1))
            put(near[k])
            if k + 1 < rows // 2:
                own.append(turn(ready, 1))
                put(own[k + 1])

    weight_step(0)
    tokens_now = at_now(tokens)
    token_parts = [tokens, swap(tokens_now, "col", 1), swap(tokens_now, "col", 2)]
    put(*token_parts[1:])
    tick()

    weight_step(1)
    cot_now = at_now(cotangent)
    cot_parts = [cotangent, swap(cot_now, "col", 1), swap(cot_now, "col", 2)]
    token_parts.append(swap(at_now(token_parts[2]), "col", 1))
    put(*cot_parts[1:], token_parts[3])
    tick()

    weight_step(2)
    small_now = at_now(small)
    norms = [small, swap(small_now, "col", 1), swap(small_now, "col", 2)]
    cot_parts.append(swap(at_now(cot_parts[2]), "col", 1))
    put(*norms[1:], cot_parts[3], start_column)
    tick()

    weight_step(3)
    norms.append(swap(at_now(norms[2]), "col", 1))
    norms = jnp.concatenate(norms, axis=1)
    first_full, first_mean, first_scale = normalize(
        token_parts, norms[0:1], norms[2:3], places_attend, "first_norm"
    )
    cot_full = lay_out([at_now(cot_parts[0])] + cot_parts[1:], places_contract, "cotangent_rows")
    put(first_full, cot_full)
    expand_own, expand_near = [expand], []

    def expand_turn(*first):
        if stepped:
            expand_own.append(turn(after(at_now(expand_own[-1]), *first), 1))
            put(expand_own[-1])

    def expand_step(k):
        if stepped:
            expand_near.append(swap(at_now(expand_own[k]), "row", 1))
            put(expand_near[k])

    expand_turn()
    tick()

    def add_bias(acc, extra, out):
        out[0][...] = (acc + extra[0][...]).astype(bf16)

    expand_step(0)
    if stepped:
        half = contract.shape[1] // 2
        contract_late = contract[:, half:]
        contract_pair = jnp.concatenate(
            [contract_late, swap(at_now(contract_late), "row", 1)], axis=0
        )
        put(contract_pair)
    expand_turn()
    mixed, *full_attend = times_rows(
        at_now(first_full),
        own + near,
        [mixed_bias],
        [((tokens_here, mix_width), bf16)],
        add_bias,
        "mix",
        tn=width,
        window=(0, mix_width),
        joins=[range(len(own)), range(len(own), len(own) + len(near))],
    )
    expand_turn(mixed)
    attended, logs = attend_forward(mixed, start_column, slopes, seqs)
    put(attended)
    tick()

    if stepped:
        contract_mine = gather_outer(at_now(contract[:, :half]))
        contract_rest = gather_outer(at_now(contract_pair))
    expand_step(1)
    got = columns_sent([attended], full_attend, ids_attend, "project", mix_width)
    part = columns_part([attended], full_attend, ids_attend, got, "project", mix_width)
    put(part)
    tick()

    expand_step(2)
    across = swap(at_now(part), "col", 2)
    base = columns_base([attended], full_attend, ids_attend, got, "project", mix_width)
    resid = tokens.astype(f32)
    middle = resid + (base + across.astype(f32) + biases[2])
    middle_low = middle.astype(bf16)
    first_mean, first_scale = first_mean[:, 0], first_scale[:, 0]
    put(middle_low, first_mean, first_scale)
    tick()

    expand_step(3)
    middle_now = at_now(middle_low)
    middle_parts = [middle_low, swap(middle_now, "col", 1), swap(middle_now, "col", 2)]
    put(*middle_parts[1:])
    if stepped:
        put(contract_mine)
    tick()

    if stepped:
        contract_near = swap(at_now(contract_mine), "row", 1)
        full_contract = [contract_mine, contract_near, contract_rest]

    middle_parts.append(swap(at_now(middle_parts[2]), "col", 1))
    second_full, second_mean, second_scale = normalize(
        middle_parts, norms[1:2], norms[3:4], places_expand, "second_norm"
    )

    def activate(acc, extra, out):
        hidden = acc + extra[0][...]
        bell = 0.5 * (1.0 + lax.erf(hidden * sqrt_half))
        out[0][...] = (hidden * bell).astype(bf16)
        out[1][...] = bell + hidden * (jnp.exp(-0.5 * hidden * hidden) * inverse_root)

    hidden_shape = (tokens_here, expand.shape[1])
    active, slope, *joined = times_rows(
        second_full,
        expand_own + expand_near if stepped else full_expand,
        [thresholds[None]],
        [(hidden_shape, bf16), (hidden_shape, f32)],
        activate,
        "expand",
        tn=512,
        joins=[range(len(expand_own)), range(len(expand_own), 2 * len(expand_own))] if stepped else [],
    )
    if stepped:
        full_expand = joined
    contract_sum = WeightSum(
        cot_full, ids_contract, [active], "contract_grad", [[3, 2], [1], [0]]
    )
    contract_sum.cut()
    contract_sum.keep(active)
    put(active)
    if stepped:
        put(contract_near)
    tick()

    def back_activate(acc, extra, out):
        grad = (acc * extra[0][...]).astype(bf16)
        out[0][...] = grad
        out[1][...] = jnp.sum(grad.astype(f32), axis=0, keepdims=True)

    second_mean, second_scale = at_now(second_mean)[:, 0], at_now(second_scale)[:, 0]
    put(second_mean, second_scale)
    contract_sum.move()

    def contract_back(rows_of, name, skip, width, *first):
        return times_rows(
            after(at_now(cot_full), *first),
            rows_of,
            [slope],
            [((tokens_here, width), bf16), ((1, width), f32)],
            back_activate,
            name,
            tn=512,
            skip=skip,
        )

    if stepped:
        pairs = [(w, k) for k in range(rows // 2) for w in full_contract[:2]]
        early, early_sum = contract_back(pairs, "contract_back_early", 0, half)
        late, late_sum = contract_back([contract_rest], "contract_back_late", half, half, early)
        hidden_grads, thresholds_part = [early, late], jnp.concatenate([early_sum, late_sum], axis=1)
    else:
        hidden_grad, thresholds_part = contract_back(
            full_contract, "contract_back", 0, hidden_shape[1]
        )
        hidden_grads = [hidden_grad]
    got = columns_sent(hidden_grads, full_expand, ids_expand, "expand_back")
    part = columns_part(hidden_grads, full_expand, ids_expand, got, "expand_back")
    across = swap(part, "col", 2)
    put(part)
    tick()

    contract_sum.add()
    contract_sum.move()
    base = columns_base(hidden_grads, full_expand, ids_expand, got, "expand_back")
    expand_sum = WeightSum(second_full, ids_expand, hidden_grads, "expand_grad", [[3], [2, 1], [0]])
    expand_sum.cut()
    second_back = base + across.astype(f32)
    put(second_back)
    tick()

    def norm_back(upstream, centred, scale, gain):
        scaled = upstream * gain
        sums = sum_col_stats(
            jnp.stack([jnp.sum(scaled, axis=1), jnp.sum(scaled * centred, axis=1)])
        )
        result = scale[:, None] * (
            scaled - sums[0][:, None] / full - centred * (sums[1][:, None] / full)
        )
        return result, jnp.sum(upstream * centred, axis=0), jnp.sum(upstream, axis=0)

    contract_sum.move()
    expand_sum.move()
    second_centred = (middle - second_mean[:, None]) * second_scale[:, None]
    second_input, second_gain, second_shift = norm_back(
        at_now(second_back), second_centred, second_scale, gains[1]
    )
    cot_float = cotangent.astype(f32)
    middle_grad = cot_float + second_input
    branch_grad = middle_grad.astype(bf16)
    branch_parts = [branch_grad, swap(branch_grad, "col", 1), swap(branch_grad, "col", 2)]
    contract_sum.add(branch_grad)
    expand_sum.keep(branch_grad)
    out_got = columns_sent(
        [after(active, branch_grad)], full_contract, ids_contract, "contract", whole=True
    )
    put(*branch_parts[1:])
    tick()

    def store(acc, extra, out):
        out[0][...] = acc.astype(bf16)

    contract_sum.add()
    expand_sum.move()
    branch_parts.append(swap(at_now(branch_parts[2]), "col", 1))
    branch_full = lay_out(branch_parts, places_attend, "branch_rows")
    (attended_grad,) = times_rows(
        branch_full,
        full_attend,
        [],
        [((tokens_here, width), bf16)],
        store,
        "project_back",
        tn=width,
        window=(mix_width, width),
    )
    project_sum = WeightSum(
        branch_full, ids_attend, [attended], "projection_grad", [[3, 2, 1, 0]]
    )
    project_sum.cut()
    expand_sum.add(attended_grad)
    query_back, key_back, value_back, query_sum, value_sum = attend_backward(
        mixed, attended_grad, start_row, logs, slopes, seqs
    )
    mixed_grads = [query_back, key_back, value_back]
    put(query_back)
    tick()

    contract_sum.add()
    project_sum.move()
    mixing_sum = WeightSum(
        first_full, ids_attend, mixed_grads, "mixing_grad", [[3, 2], [1, 0]]
    )
    mixing_sum.cut()
    mixed_grads = [after(query_back, mixing_sum.sent[0]), key_back, value_back]
    mixing_sum.move(*project_sum.last)
    expand_sum.add()
    got = columns_sent(mixed_grads, full_attend, ids_attend, "mix_back")
    part = columns_part(mixed_grads, full_attend, ids_attend, got, "mix_back")
    across = swap(part, "col", 2)
    expand_sum.add()
    base = columns_base(mixed_grads, full_attend, ids_attend, got, "mix_back")
    project_sum.keep(part)
    mixing_sum.keep(part)
    first_back = base + across.astype(f32)
    put(first_back)
    tick()

    project_sum.add()
    mixing_sum.move()
    mixing_sum.add()
    mixing_sum.add()
    out_part = columns_part([at_now(active)], full_contract, ids_contract, out_got, "contract")
    first_centred = (resid - first_mean[:, None]) * first_scale[:, None]
    first_input, first_gain, first_shift = norm_back(
        at_now(first_back), first_centred, first_scale, gains[0]
    )
    tokens_grad = middle_grad + first_input
    small = jnp.stack(
        [
            first_gain,
            second_gain,
            first_shift,
            second_shift,
            jnp.sum(query_sum, axis=(0, 1)),
            jnp.sum(value_sum, axis=(0, 1)),
            jnp.sum(branch_grad.astype(f32), axis=0),
            jnp.sum(cot_float, axis=0),
        ]
    )
    small = jnp.concatenate([small, thresholds_part.reshape(-1, width)], axis=0)
    bits = [1 << i for i in range(1, rows.bit_length() - 1)] + [1]
    put(small, out_part)
    tick()

    expand_sum.move()
    mixing_sum.add()
    project_sum.add()
    project_sum.add()
    small = at_now(small)
    for bit in bits[:-1]:
        small = small + swap(small, "row", bit)
    out_across = swap(at_now(out_part), "col", 2)
    out_base = columns_base([active], full_contract, ids_contract, out_got, "contract")
    layer_out = (middle + (out_base + out_across.astype(f32) + biases[3])).astype(bf16)
    put(small, out_base)
    tick()

    small = small + swap(at_now(small), "row", bits[-1])
    expand_sum.add()
    project_sum.add()
    mixing_sum.add()
    contract_grad, expand_grad = contract_sum.result, expand_sum.result
    projection_grad, mixing_grad = project_sum.result, mixing_sum.result
    mixing_grad = jnp.stack(
        [mixing_grad[:, i * width : (i + 1) * width] for i in range(3)], axis=1
    )
    return (
        layer_out,
        tokens_grad,
        small[0:2],
        small[2:4],
        small[4:8],
        mixing_grad,
        projection_grad,
        expand_grad,
        small[8:].reshape(thresholds.shape),
        contract_grad,
    )


def solution(mesh):
    return jax.shard_map(
        on_device,
        mesh=mesh,
        in_specs=(
            P("row", "col"),
            P("row", None),
            P(None, "col"),
            P(None, "col"),
            P(None, "col"),
            P("row", None, "col"),
            P("row", "col"),
            P("row", "col"),
            P("col"),
            P("row", "col"),
            P("row", "col"),
        ),
        out_specs=(
            P("row", "col"),
            P("row", "col"),
            P(None, "col"),
            P(None, "col"),
            P(None, "col"),
            P("row", None, "col"),
            P("row", "col"),
            P("row", "col"),
            P("col"),
            P("row", "col"),
        ),
        check_vma=False,
    )
```

```python
import math
from functools import partial

import jax
import jax.numpy as jnp
from jax import lax
from jax.experimental import pallas as pl
from jax.experimental.pallas import tpu as pltpu
from jax.sharding import PartitionSpec as P

HD = 64
BLOCK = 256

norm_eps = 1e-05
sqrt_half = 0.7071067811865476
inverse_root = 0.3989422804014327
far = -1e33
NT = (((1,), (1,)), ((), ()))
TN = (((0,), (0,)), ((), ()))
VMEM_LIMIT = 26 << 20
CHEAP = 64
f32 = jnp.float32
bf16 = jnp.bfloat16


def pick_heads(pair):
    lane = lax.broadcasted_iota(jnp.int32, pair.shape, 1)
    zero = jnp.zeros_like(pair)
    return jnp.concatenate(
        [jnp.where(lane < HD, pair, zero), jnp.where(lane < HD, zero, pair)], axis=0
    )


def attend_kernel(
    slope_ref, start_ref, q_ref, k_ref, v_ref, out_ref, log_ref, dist_ref, *, rows, scale
):
    pair = pl.program_id(1)
    length = k_ref.shape[0]

    @pl.when(pair == 0)
    def _():
        for r0 in range(0, length, rows):
            shape = (rows, r0 + rows)
            i = lax.broadcasted_iota(jnp.int32, shape, 0) + r0
            j = lax.broadcasted_iota(jnp.int32, shape, 1)
            allowed = (j <= i) & (j >= start_ref[0, r0 : r0 + rows, :])
            dist_ref[r0 : r0 + rows, 0 : r0 + rows] = jnp.where(allowed, (j - i).astype(f32), far)

    slope_a, slope_b = slope_ref[2 * pair] * scale, slope_ref[2 * pair + 1] * scale
    for r0 in range(0, length, rows):
        r1 = r0 + rows
        q = pick_heads(q_ref[r0:r1, :] * jnp.asarray(scale, bf16))
        s = lax.dot_general(q, k_ref[0:r1, :], NT, preferred_element_type=f32)
        d = dist_ref[r0:r1, 0:r1]
        s = jnp.concatenate([s[:rows] + d * slope_a, s[rows:] + d * slope_b], axis=0)
        row_max = jnp.max(s, axis=1, keepdims=True)
        weights = jnp.exp(s - row_max)
        row_total = jnp.sum(weights, axis=1, keepdims=True)
        probs = (weights * (1.0 / row_total)).astype(bf16)
        o = jnp.dot(probs, v_ref[0:r1, :], preferred_element_type=f32)
        lane = lax.broadcasted_iota(jnp.int32, (rows, 2 * HD), 1)
        out_ref[r0:r1, :] = jnp.where(lane < HD, o[:rows], o[rows:]).astype(bf16)
        logs = row_max + jnp.log(row_total)
        logs = jnp.where(
            lane < HD,
            jnp.broadcast_to(logs[:rows], (rows, 2 * HD)),
            jnp.broadcast_to(logs[rows:], (rows, 2 * HD)),
        ).T
        log_ref[0, 0:1, r0:r1] = logs[0:1]
        log_ref[0, 1:2, r0:r1] = logs[HD : HD + 1]


def attend_forward(mixed, starts, slopes, seqs, rows=256):
    length, pairs = mixed.shape[0] // seqs, mixed.shape[1] // (6 * HD)

    def part(i):
        return pl.BlockSpec((length, 2 * HD), lambda s, p, *_: (s, i * pairs + p))

    return pl.pallas_call(
        partial(attend_kernel, rows=rows, scale=HD**-0.5),
        grid_spec=pltpu.PrefetchScalarGridSpec(
            num_scalar_prefetch=1,
            grid=(seqs, pairs),
            in_specs=[
                pl.BlockSpec((1, length, 1), lambda s, p, *_: (s, 0, 0)),
                part(0),
                part(1),
                part(2),
            ],
            out_specs=[part(0), pl.BlockSpec((1, 2, length), lambda s, p, *_: (s * pairs + p, 0, 0))],
            scratch_shapes=[pltpu.VMEM((length, length), f32)],
        ),
        out_shape=[
            jax.ShapeDtypeStruct((mixed.shape[0], 2 * HD * pairs), bf16),
            jax.ShapeDtypeStruct((seqs * pairs, 2, length), f32),
        ],
        compiler_params=pltpu.CompilerParams(vmem_limit_bytes=VMEM_LIMIT),
        cost_estimate=pl.CostEstimate(
            flops=16 * seqs * pairs * length * length * HD // CHEAP,
            bytes_accessed=4 * mixed.size // CHEAP,
            transcendentals=seqs * pairs * length * length // CHEAP,
        ),
        name="attend_forward",
    )(slopes, starts, mixed, mixed, mixed)


def attend_back_kernel(
    slope_ref,
    start_ref,
    log_ref,
    q_ref,
    k_ref,
    v_ref,
    g_ref,
    dq_ref,
    dk_ref,
    dv_ref,
    qs_ref,
    vs_ref,
    dist_ref,
    ka_ref,
    va_ref,
    *,
    rows,
    scale,
):
    pair = pl.program_id(1)
    length = k_ref.shape[0]

    @pl.when(pair == 0)
    def _():
        for r0 in range(0, length, rows):
            shape = (r0 + rows, rows)
            i = lax.broadcasted_iota(jnp.int32, shape, 1) + r0
            j = lax.broadcasted_iota(jnp.int32, shape, 0)
            allowed = (j <= i) & (j >= start_ref[0, :, r0 : r0 + rows])
            dist_ref[0 : r0 + rows, r0 : r0 + rows] = jnp.where(allowed, (j - i).astype(f32), far)

    slope_a, slope_b = slope_ref[2 * pair] * scale, slope_ref[2 * pair + 1] * scale
    query_sum = jnp.zeros((1, 2 * HD), f32)
    for r0 in reversed(range(0, length, rows)):
        r1 = r0 + rows
        q = pick_heads(q_ref[r0:r1, :] * jnp.asarray(scale, bf16))
        g = pick_heads(g_ref[r0:r1, :])
        k, v = k_ref[0:r1, :], v_ref[0:r1, :]
        s = lax.dot_general(k, q, NT, preferred_element_type=f32)
        d = dist_ref[0:r1, r0:r1]
        logs = jnp.concatenate([log_ref[0, 0:1, r0:r1], log_ref[0, 1:2, r0:r1]], axis=1)
        s = jnp.concatenate([s[:, :rows] + d * slope_a, s[:, rows:] + d * slope_b], axis=1)
        probs = jnp.exp(s - logs)
        t = lax.dot_general(v, g, NT, preferred_element_type=f32)
        centre = jnp.sum(probs * t, axis=0, keepdims=True)
        score_grad = (probs * (t - centre)).astype(bf16)
        value_part = jnp.dot(probs.astype(bf16), g, preferred_element_type=f32)
        key_part = jnp.dot(score_grad, q, preferred_element_type=f32)
        if r1 == length:
            va_ref[...] = value_part
            ka_ref[...] = key_part
        else:
            va_ref[0:r1, :] += value_part
            ka_ref[0:r1, :] += key_part
        dq = lax.dot_general(score_grad, k, TN, preferred_element_type=f32)
        lane = lax.broadcasted_iota(jnp.int32, (rows, 2 * HD), 1)
        dq = (jnp.where(lane < HD, dq[:rows], dq[rows:]) * scale).astype(bf16)
        dq_ref[r0:r1, :] = dq
        query_sum = query_sum + jnp.sum(dq.astype(f32), axis=0, keepdims=True)
    qs_ref[0] = query_sum
    dk_ref[...] = ka_ref[...].astype(bf16)
    dv = va_ref[...].astype(bf16)
    dv_ref[...] = dv
    vs_ref[0] = jnp.sum(dv.astype(f32), axis=0, keepdims=True)


def attend_backward(mixed, grads, starts, logs, slopes, seqs, rows=256):
    length, pairs = mixed.shape[0] // seqs, mixed.shape[1] // (6 * HD)

    def part(i):
        return pl.BlockSpec((length, 2 * HD), lambda s, p, *_: (s, i * pairs + p))

    out = jax.ShapeDtypeStruct(grads.shape, bf16)
    sums = jax.ShapeDtypeStruct((seqs, 1, grads.shape[1]), f32)
    sum_spec = pl.BlockSpec((1, 1, 2 * HD), lambda s, p, *_: (s, 0, p))
    return pl.pallas_call(
        partial(attend_back_kernel, rows=rows, scale=HD**-0.5),
        grid_spec=pltpu.PrefetchScalarGridSpec(
            num_scalar_prefetch=1,
            grid=(seqs, pairs),
            in_specs=[
                pl.BlockSpec((1, 1, length), lambda s, p, *_: (s, 0, 0)),
                pl.BlockSpec((1, 2, length), lambda s, p, *_: (s * pairs + p, 0, 0)),
                part(0),
                part(1),
                part(2),
                part(0),
            ],
            out_specs=[part(0), part(0), part(0), sum_spec, sum_spec],
            scratch_shapes=[
                pltpu.VMEM((length, length), f32),
                pltpu.VMEM((length, 2 * HD), f32),
                pltpu.VMEM((length, 2 * HD), f32),
            ],
        ),
        out_shape=[out, out, out, sums, sums],
        compiler_params=pltpu.CompilerParams(vmem_limit_bytes=VMEM_LIMIT),
        cost_estimate=pl.CostEstimate(
            flops=40 * seqs * pairs * length * length * HD // CHEAP,
            bytes_accessed=14 * grads.size // CHEAP,
            transcendentals=seqs * pairs * length * length // CHEAP,
        ),
        name="attend_backward",
    )(slopes, starts, logs, mixed, mixed, mixed, grads)


def resident(shape):
    return pl.BlockSpec(shape, lambda *_: (0,) * len(shape), pipeline_mode=pl.Buffered(1))


def kept_out(shape):
    return pl.BlockSpec(shape, lambda *_: (0,) * len(shape))


def flat_rows(ws):
    return jnp.concatenate([w[...] for w in ws], axis=0)


def matmul_call(kernel, grid, ins, outs, scratch, flops, name, prefetch=()):
    moved = sum(a.size * a.dtype.itemsize for a, _ in ins)
    moved += sum(jnp.dtype(t).itemsize * math.prod(s) for s, t, _ in outs)
    return pl.pallas_call(
        kernel,
        grid_spec=pltpu.PrefetchScalarGridSpec(
            num_scalar_prefetch=len(prefetch),
            grid=grid,
            in_specs=[s for _, s in ins],
            out_specs=[s for _, _, s in outs],
            scratch_shapes=scratch,
        ),
        out_shape=[jax.ShapeDtypeStruct(s, t) for s, t, _ in outs],
        compiler_params=pltpu.CompilerParams(vmem_limit_bytes=VMEM_LIMIT),
        cost_estimate=pl.CostEstimate(
            flops=flops // CHEAP, bytes_accessed=moved // CHEAP, transcendentals=0
        ),
        name=name,
    )(*prefetch, *[a for a, _ in ins])


def times_rows(x, ws, extras, outs, finish, name, tn, window=None, joins=()):
    tokens, depth = x.shape
    first, width = window or (0, ws[0].shape[1])
    first, tiles = first // tn, width // tn
    n_ws, n_ex, n_out = len(ws), len(extras), len(outs)
    steps = ws[0].shape[1] // tn if joins else tiles

    def kernel(*refs):
        x_ref, w_refs = refs[0], refs[1 : 1 + n_ws]
        extra, out = refs[1 + n_ws : 1 + n_ws + n_ex], refs[1 + n_ws + n_ex :]
        for places, joined in zip(joins, out[n_out:]):
            at = 0
            for i in places:
                joined[at : at + ws[i].shape[0], :] = w_refs[i][...]
                at += ws[i].shape[0]

        def multiply():
            acc = jnp.dot(x_ref[...], flat_rows(w_refs), preferred_element_type=f32)
            finish(acc, extra, out[:n_out])

        if steps == tiles:
            multiply()
        else:
            pl.when(pl.program_id(0) < tiles)(multiply)

    def spec(rows):
        return pl.BlockSpec((rows, tn), lambda n: (0, jnp.minimum(n, tiles - 1)))

    def tile(rows):
        return pl.BlockSpec((rows, tn), lambda n: (0, n + first))

    ins = [(x, resident(x.shape))] + [(w, tile(w.shape[0])) for w in ws]
    ins += [(e, spec(e.shape[0])) for e in extras]
    results = [(s, t, spec(s[0])) for s, t in outs]
    for places in joins:
        rows = sum(ws[i].shape[0] for i in places)
        results.append(((rows, ws[0].shape[1]), bf16, tile(rows)))
    return matmul_call(kernel, (steps,), ins, results, [], 2 * tokens * depth * width, name)


def times_columns(xs, ws, order, side, dtype, name, first=0, added=(), block=0, chunks=None):
    tokens = xs[0].shape[0]
    count = order.shape[1]
    n_xs = len(xs)
    width = sum(x.shape[1] for x in xs)
    chunks = chunks or [tokens]

    def kernel(order_ref, side_ref, *refs):
        x_refs, w_refs = refs[:n_xs], refs[n_xs : n_xs + 2]
        added_refs, out_refs = refs[n_xs + 2 : n_xs + 2 + len(added)], refs[-len(chunks) :]
        x = jnp.concatenate([r[...] for r in x_refs], axis=1)
        for i, w_ref in enumerate(w_refs):
            acc = lax.dot_general(x, w_ref[...], NT, preferred_element_type=f32)
            place = side_ref[0] if i == 0 else 1 - side_ref[0]
            place = pl.ds(pl.multiple_of(place * BLOCK, BLOCK), BLOCK)
            if added:
                acc = acc + jnp.concatenate([r[:, place] for r in added_refs]).astype(f32)
            at = 0
            for out_ref, height in zip(out_refs, chunks):
                out_ref[:, place] = acc[at : at + height].astype(dtype)
                at += height

    def w_spec(i):
        return pl.BlockSpec((BLOCK, width), lambda n, order_ref, _: (order_ref[i, n], first // width))

    def pair(height, start):
        return pl.BlockSpec((height, 2 * BLOCK), lambda n, *_: (0, start + n))

    ins = [(x, resident(x.shape)) for x in xs]
    ins += [(w, w_spec(i)) for i, w in enumerate(ws)]
    ins += [(b, pair(b.shape[0], block)) for b in added]
    done = matmul_call(
        kernel,
        (count,),
        ins,
        [((height, 2 * BLOCK * count), dtype, pair(height, 0)) for height in chunks],
        [],
        4 * tokens * BLOCK * count * width,
        name,
        prefetch=(order, side),
    )
    return done if len(chunks) > 1 else done[0]


def weight_rows(a, order, gs, name, groups=None, dtype=bf16):
    tokens = a.shape[0]
    width = sum(g.shape[1] for g in gs)
    count = order.shape[0]
    n_gs = len(gs)

    def kernel(order_ref, a_ref, *refs):
        g_refs, out_refs = refs[:n_gs], refs[n_gs:]
        g = jnp.concatenate([r[...] for r in g_refs], axis=1)
        acc = lax.dot_general(a_ref[...], g, TN, preferred_element_type=f32).astype(dtype)
        if groups is None:
            out_refs[0][...] = acc
            return
        for out_ref, group in zip(out_refs, groups):
            for j, i in enumerate(group):

                @pl.when(pl.program_id(0) == i)
                def _(out_ref=out_ref, rows=slice(j * BLOCK, (j + 1) * BLOCK)):
                    out_ref[rows, :] = acc

    ins = [(a, pl.BlockSpec((tokens, BLOCK), lambda i, order_ref: (0, order_ref[i])))]
    ins += [(g, resident(g.shape)) for g in gs]
    if groups is None:
        outs = [((count * BLOCK, width), dtype, pl.BlockSpec((BLOCK, width), lambda i, *_: (i, 0)))]
    else:
        shapes = [(len(group) * BLOCK, width) for group in groups]
        outs = [(shape, dtype, kept_out(shape)) for shape in shapes]
    done = matmul_call(
        kernel, (count,), ins, outs, [], 2 * tokens * BLOCK * count * width, name, prefetch=(order,)
    )
    return done[0] if groups is None else done


def place_blocks(values, place_ref, out_ref):
    at = 0
    for value in values:
        for c0 in range(0, value.shape[1], BLOCK):
            place = pl.ds(pl.multiple_of(place_ref[at] * BLOCK, BLOCK), BLOCK)
            out_ref[:, place] = value[:, c0 : c0 + BLOCK]
            at += 1


def lay_out(parts, places, name, tm=256):
    tokens, width = parts[0].shape
    full = width * len(parts)

    def kernel(place_ref, *refs):
        place_blocks([r[...] for r in refs[:-1]], place_ref, refs[-1])

    return matmul_call(
        kernel,
        (tokens // tm,),
        [(p, pl.BlockSpec((tm, width), lambda m, *_: (m, 0))) for p in parts],
        [((tokens, full), bf16, pl.BlockSpec((tm, full), lambda m, *_: (m, 0)))],
        [],
        tokens * full,
        name,
        prefetch=(places,),
    )[0]


def normalize(parts, gain, shift, places, name, tm=256):
    tokens, width = parts[0].shape
    n = len(parts)
    full = width * n

    def kernel(place_ref, *refs):
        gain_ref, shift_ref, out_ref, mean_ref, scale_ref = refs[n:]
        rows = [r[...].astype(f32) for r in refs[:n]]
        mean = sum(jnp.sum(v, axis=1, keepdims=True) for v in rows) / full
        square = sum(jnp.sum(v * v, axis=1, keepdims=True) for v in rows) / full
        scale = lax.rsqrt(square - mean * mean + norm_eps)
        mean_ref[...] = mean
        scale_ref[...] = scale
        done = []
        for i, v in enumerate(rows):
            cols = slice(i * width, (i + 1) * width)
            done.append(((v - mean) * scale * gain_ref[:, cols] + shift_ref[:, cols]).astype(bf16))
        place_blocks(done, place_ref, out_ref)

    ins = [(p, pl.BlockSpec((tm, width), lambda m, *_: (m, 0))) for p in parts]
    ins += [(gain, resident(gain.shape)), (shift, resident(shift.shape))]
    column = pl.BlockSpec((tm, 1), lambda m, *_: (m, 0))
    return matmul_call(
        kernel,
        (tokens // tm,),
        ins,
        [
            ((tokens, full), bf16, pl.BlockSpec((tm, full), lambda m, *_: (m, 0))),
            ((tokens, 1), f32, column),
            ((tokens, 1), f32, column),
        ],
        [],
        8 * tokens * full,
        name,
        prefetch=(places,),
    )


def swap(x, axis, bit):
    return lax.ppermute(x, axis, [(i, i ^ bit) for i in range(lax.axis_size(axis))])


def turn(x, steps):
    count = lax.axis_size("row")
    return lax.ppermute(x, "row", [(i, (i + 2 * steps) % count) for i in range(count)])


def sum_col_stats(stats):
    stats = stats + swap(stats, "col", 1)
    return stats + swap(stats, "col", 2)


def sum_rows(x):
    bit = 1
    while bit < lax.axis_size("row"):
        x = x + swap(x, "row", bit)
        bit *= 2
    return x


def after(x, *first):
    return lax.optimization_barrier((x,) + first)[0] if first else x


def outer_groups():
    outer = lax.axis_size("row") // 2
    return [[2 * i + inner for i in range(outer)] for inner in range(2)]


def find(ids, wanted):
    at = jnp.arange(ids.shape[0])
    return jnp.sum(jnp.where(ids[None, :] == wanted[:, None], at[None, :], 0), axis=1).astype(
        jnp.int32
    )


def gather_whole(w):
    return [lax.all_gather(w, "row", axis=0, tiled=True)]


def gather_outer(w):
    return lax.all_gather(w, "row", axis=0, tiled=True, axis_index_groups=outer_groups())


class Clock:
    def __init__(self):
        self.now, self.new = [], []

    def at(self, x):
        return after(x, *self.now)

    def put(self, *xs):
        self.new += xs

    def tick(self):
        self.now, self.new = self.new, []


def on_device(
    tokens,
    segments,
    gains,
    shifts,
    biases,
    mixing,
    projection,
    expand,
    thresholds,
    contract,
    cotangent,
):
    seqs = segments.shape[0]
    rows, cols = lax.axis_size("row"), lax.axis_size("col")
    row, col = lax.axis_index("row"), lax.axis_index("col")
    tokens_here, width = tokens.shape
    full = width * cols
    heads = width // HD
    stepped = full // rows == BLOCK and rows == 2 * cols
    blocks, per_col = full // BLOCK, width // BLOCK
    at = jnp.arange(blocks)
    ours = per_col * ((at // per_col) ^ col) + at % per_col
    place, side = row // 2, row % 2
    steps = jnp.arange(max(rows // 2, 1))
    back = (place - steps) % (rows // 2)
    if stepped:
        ids_attend = ids_expand = jnp.concatenate([2 * back + side, 2 * back + 1 - side])
        ids_contract = jnp.stack([2 * steps + side, 2 * steps + 1 - side], axis=1).reshape(-1)
    else:
        ids_attend = ids_expand = ids_contract = at
        side = 0 * side
    sides = jnp.reshape(side, (1,)).astype(jnp.int32)
    away = jnp.array([1, 3, 0, 2]) ^ col
    clock = Clock()
    at_now, put, tick = clock.at, clock.put, clock.tick

    def columns_order(ids, ws):
        want = jnp.stack([2 * away + side, 2 * away + 1 - side]).reshape(-1)
        order = find(ids, want).reshape(2, -1)
        return order if len(ws) == 1 else order % (blocks // 2)

    def two(ws):
        return ws if len(ws) == 2 else [ws[0], ws[0]]

    def columns_sent(xs, ws, ids, name, first=0, whole=False):
        order = columns_order(ids, ws)[:, :2]
        xs = [at_now(xs[0])] + xs[1:]
        chunks = [3 * tokens_here // 8, 3 * tokens_here // 8, tokens_here // 4]
        if whole:
            chunks = [tokens_here]
        sent = times_columns(
            xs, two(ws), order, sides, bf16, name + "_sent", first, chunks=chunks
        )
        if whole:
            put(sent)
        return [swap(v, "col", 1) for v in ([sent] if whole else sent)]

    def columns_part(xs, ws, ids, got, name, first=0):
        order = columns_order(ids, ws)[:, 3:]
        return times_columns(xs, two(ws), order, sides, bf16, name + "_part", first, got, 1)

    def columns_base(xs, ws, ids, got, name, first=0):
        order = columns_order(ids, ws)[:, 2:3]
        xs = [at_now(xs[0])] + xs[1:]
        return times_columns(xs, two(ws), order, sides, f32, name + "_base", first, got, 0)

    class WeightSum:
        def __init__(self, a, ids, gs, name, groups=None):
            self.a, self.ids, self.gs, self.name = a, ids, gs, name
            self.left = rows // 2
            self.groups = groups or [[k] for k in reversed(range(self.left))]
            self.got, self.kept, self.carry, self.result = {}, [], None, None
            self.last = []

        def cut(self):
            if stepped:
                other = find(self.ids, 2 * back + 1 - side)
                self.sent = list(
                    weight_rows(at_now(self.a), other, self.gs, self.name + "_other", self.groups)
                )
            else:
                self.sent = [
                    weight_rows(at_now(self.a), find(self.ids, at), self.gs, self.name, dtype=f32)
                ]
            put(*self.sent)

        def keep(self, *first):
            if stepped:
                mine = find(self.ids, 2 * back + side)
                a = after(at_now(self.a), *first)
                single = [[k] for k in range(rows // 2)]
                self.kept = weight_rows(a, mine, self.gs, self.name + "_mine", single)
                put(*self.kept)

        def move(self, *first, late=False):
            if stepped:
                if not self.groups:
                    return
                group = self.groups.pop(0)
                got = swap(after(at_now(self.sent.pop(0)), *first), "row", 1)
                self.last = [got]
                if not late:
                    put(got)
                for j, k in enumerate(group):
                    self.got[k] = (got, j * BLOCK)

        def add(self, *first):
            if not stepped:
                if self.result is None:
                    self.result = lax.psum_scatter(
                        self.sent[0], "row", scatter_dimension=0, tiled=True
                    )
                return
            self.left -= 1
            got, start = self.got[self.left]
            got = after(at_now(got), *first)[start : start + BLOCK]
            total = self.kept[self.left].astype(f32) + got.astype(f32)
            if self.carry is not None:
                total = total + self.carry.astype(f32)
            if self.left == 0:
                self.result = total
            else:
                self.carry = turn(total.astype(bf16), -1)
                put(self.carry)

    head_ids = (col * heads + jnp.arange(heads)).astype(f32)
    slopes = jnp.exp2(-8.0 * (head_ids + 1.0) / (heads * cols))
    starts = jnp.sum(segments[:, None, :] < segments[:, :, None], axis=2).astype(jnp.int32)
    start_column, start_row = starts[:, :, None], starts[:, None, :]
    places_attend, places_expand = find(ids_attend, ours), find(ids_expand, ours)
    places_contract = find(ids_contract, ours)
    mix_width = 3 * width
    mixed_bias = jnp.concatenate([biases[0:1], jnp.zeros((1, width), f32), biases[1:2]], axis=1)

    attend_rows = jnp.concatenate([mixing.reshape(mixing.shape[0], -1), projection], axis=1)
    small = jnp.concatenate([gains, shifts], axis=0)
    put(attend_rows)
    tick()
    if stepped:
        own, near = [attend_rows], []
    else:
        whole = gather_whole(attend_rows)[0]
        own, near = [whole[: full // 2]], [whole[full // 2 :]]
        full_expand = gather_whole(expand)
        full_contract = gather_whole(contract)

    def weight_step(k):
        if stepped:
            ready = at_now(own[k])
            near.append(swap(ready, "row", 1))
            put(near[k])
            if k + 1 < rows // 2:
                own.append(turn(ready, 1))
                put(own[k + 1])

    weight_step(0)
    tokens_now = at_now(tokens)
    token_parts = [tokens, swap(tokens_now, "col", 1), swap(tokens_now, "col", 2)]
    put(*token_parts[1:])
    tick()

    weight_step(1)
    cot_now = at_now(cotangent)
    cot_parts = [cotangent, swap(cot_now, "col", 1), swap(cot_now, "col", 2)]
    token_parts.append(swap(at_now(token_parts[2]), "col", 1))
    put(*cot_parts[1:], token_parts[3])
    tick()

    weight_step(2)
    small_now = at_now(small)
    norms = [small, swap(small_now, "col", 1), swap(small_now, "col", 2)]
    cot_parts.append(swap(at_now(cot_parts[2]), "col", 1))
    put(*norms[1:], cot_parts[3], start_column)
    tick()

    weight_step(3)
    norms.append(swap(at_now(norms[2]), "col", 1))
    norms = jnp.concatenate(norms, axis=1)
    first_full, first_mean, first_scale = normalize(
        token_parts, norms[0:1], norms[2:3], places_attend, "first_norm"
    )
    cot_full = lay_out([at_now(cot_parts[0])] + cot_parts[1:], places_contract, "cotangent_rows")
    put(first_full, cot_full)
    expand_own, expand_near = [expand], []

    def expand_turn(*first):
        if stepped:
            expand_own.append(turn(after(at_now(expand_own[-1]), *first), 1))
            put(expand_own[-1])

    def expand_step(k):
        if stepped:
            expand_near.append(swap(at_now(expand_own[k]), "row", 1))
            put(expand_near[k])

    expand_turn()
    tick()

    def add_bias(acc, extra, out):
        out[0][...] = (acc + extra[0][...]).astype(bf16)

    expand_step(0)
    if stepped:
        contract_pair = jnp.concatenate([contract, swap(at_now(contract), "row", 1)], axis=0)
        put(contract_pair)
    expand_turn()
    mixed, *full_attend = times_rows(
        at_now(first_full),
        own + near,
        [mixed_bias],
        [((tokens_here, mix_width), bf16)],
        add_bias,
        "mix",
        tn=width,
        window=(0, mix_width),
        joins=[range(len(own)), range(len(own), len(own) + len(near))],
    )
    expand_turn(mixed)
    attended, logs = attend_forward(mixed, start_column, slopes, seqs)
    put(attended)
    tick()

    if stepped:
        full_contract = [gather_outer(at_now(contract_pair))]
    expand_step(1)
    got = columns_sent([attended], full_attend, ids_attend, "project", mix_width)
    part = columns_part([attended], full_attend, ids_attend, got, "project", mix_width)
    put(part)
    tick()

    expand_step(2)
    across = swap(at_now(part), "col", 2)
    base = columns_base([attended], full_attend, ids_attend, got, "project", mix_width)
    resid = tokens.astype(f32)
    middle = resid + (base + across.astype(f32) + biases[2])
    middle_low = middle.astype(bf16)
    first_mean, first_scale = first_mean[:, 0], first_scale[:, 0]
    put(middle_low, first_mean, first_scale)
    tick()

    expand_step(3)
    middle_now = at_now(middle_low)
    middle_parts = [middle_low, swap(middle_now, "col", 1), swap(middle_now, "col", 2)]
    put(*middle_parts[1:])
    tick()

    middle_parts.append(swap(at_now(middle_parts[2]), "col", 1))
    second_full, second_mean, second_scale = normalize(
        middle_parts, norms[1:2], norms[3:4], places_expand, "second_norm"
    )
    put(second_full)
    tick()

    def activate(acc, extra, out):
        hidden = acc + extra[0][...]
        bell = 0.5 * (1.0 + lax.erf(hidden * sqrt_half))
        out[0][...] = (hidden * bell).astype(bf16)
        out[1][...] = bell + hidden * (jnp.exp(-0.5 * hidden * hidden) * inverse_root)

    hidden_shape = (tokens_here, expand.shape[1])
    active, slope, *joined = times_rows(
        at_now(second_full),
        expand_own + expand_near if stepped else full_expand,
        [thresholds[None]],
        [(hidden_shape, bf16), (hidden_shape, f32)],
        activate,
        "expand",
        tn=512,
        joins=[range(len(expand_own)), range(len(expand_own), 2 * len(expand_own))] if stepped else [],
    )
    if stepped:
        full_expand = joined
    contract_sum = WeightSum(
        cot_full, ids_contract, [active], "contract_grad", [[3], [2, 1], [0]]
    )
    contract_sum.cut()
    put(active)
    tick()

    def back_activate(acc, extra, out):
        grad = (acc * extra[0][...]).astype(bf16)
        out[0][...] = grad
        out[1][...] = jnp.sum(grad.astype(f32), axis=0, keepdims=True)

    second_mean, second_scale = at_now(second_mean)[:, 0], at_now(second_scale)[:, 0]
    put(second_mean, second_scale)
    contract_sum.move()
    contract_sum.keep()
    tick()

    contract_sum.add()
    contract_sum.move()
    hidden_grad, thresholds_part = times_rows(
        at_now(cot_full),
        full_contract,
        [slope],
        [(hidden_shape, bf16), ((1, hidden_shape[1]), f32)],
        back_activate,
        "contract_back",
        tn=512,
    )
    got = columns_sent([hidden_grad], full_expand, ids_expand, "expand_back")
    part = columns_part([hidden_grad], full_expand, ids_expand, got, "expand_back")
    across = swap(part, "col", 2)
    put(part)
    tick()

    contract_sum.add()
    contract_sum.move()
    base = columns_base([hidden_grad], full_expand, ids_expand, got, "expand_back")
    expand_sum = WeightSum(second_full, ids_expand, [hidden_grad], "expand_grad", [[3], [2, 1], [0]])
    expand_sum.cut()
    second_back = base + across.astype(f32)
    put(second_back)
    tick()

    def norm_back(upstream, centred, scale, gain):
        scaled = upstream * gain
        sums = sum_col_stats(
            jnp.stack([jnp.sum(scaled, axis=1), jnp.sum(scaled * centred, axis=1)])
        )
        result = scale[:, None] * (
            scaled - sums[0][:, None] / full - centred * (sums[1][:, None] / full)
        )
        return result, jnp.sum(upstream * centred, axis=0), jnp.sum(upstream, axis=0)

    expand_sum.move()
    second_centred = (middle - second_mean[:, None]) * second_scale[:, None]
    second_input, second_gain, second_shift = norm_back(
        at_now(second_back), second_centred, second_scale, gains[1]
    )
    cot_float = cotangent.astype(f32)
    middle_grad = cot_float + second_input
    branch_grad = middle_grad.astype(bf16)
    branch_parts = [branch_grad, swap(branch_grad, "col", 1), swap(branch_grad, "col", 2)]
    contract_sum.add(branch_grad)
    expand_sum.keep(branch_grad)
    out_got = columns_sent(
        [after(active, branch_grad)], full_contract, ids_contract, "contract", whole=True
    )
    put(*branch_parts[1:])
    tick()

    def store(acc, extra, out):
        out[0][...] = acc.astype(bf16)

    contract_sum.add()
    expand_sum.move()
    expand_sum.add()
    branch_parts.append(swap(at_now(branch_parts[2]), "col", 1))
    branch_full = lay_out(branch_parts, places_attend, "branch_rows")
    (attended_grad,) = times_rows(
        branch_full,
        full_attend,
        [],
        [((tokens_here, width), bf16)],
        store,
        "project_back",
        tn=width,
        window=(mix_width, width),
    )
    if stepped:
        project_other = weight_rows(
            branch_full,
            find(ids_attend, 2 * steps + 1 - side),
            [attended],
            "projection_grad_other",
        )
        put(project_other)
    else:
        project_sum = WeightSum(branch_full, ids_attend, [attended], "projection_grad", None)
        project_sum.cut()
    query_back, key_back, value_back, query_sum, value_sum = attend_backward(
        mixed, attended_grad, start_row, logs, slopes, seqs
    )
    mixed_grads = [query_back, key_back, value_back]
    put(query_back)
    tick()

    expand_sum.move()
    if stepped:
        project_got = swap(at_now(project_other), "row", 1)
        put(project_got)
    expand_sum.add()
    got = columns_sent(mixed_grads, full_attend, ids_attend, "mix_back")
    mixing_sum = WeightSum(
        first_full, ids_attend, mixed_grads, "mixing_grad", [[3], [2], [1], [0]]
    )
    mixing_sum.cut()
    part = columns_part(mixed_grads, full_attend, ids_attend, got, "mix_back")
    across = swap(part, "col", 2)
    expand_sum.add()
    base = columns_base(mixed_grads, full_attend, ids_attend, got, "mix_back")
    if stepped:
        project_mine = weight_rows(
            after(branch_full, part),
            find(ids_attend, 2 * steps + side),
            [attended],
            "projection_grad_mine",
        )
        put(project_mine)
    first_back = base + across.astype(f32)
    put(first_back)
    tick()

    if stepped:
        total = at_now(project_mine).astype(f32) + project_got.astype(f32)
        projection_grad = lax.psum_scatter(
            total.astype(bf16),
            "row",
            scatter_dimension=0,
            tiled=True,
            axis_index_groups=outer_groups(),
        ).astype(f32)
    else:
        project_sum.add()
        projection_grad = project_sum.result
    expand_sum.add()
    mixing_sum.move()
    mixing_sum.keep()
    first_centred = (resid - first_mean[:, None]) * first_scale[:, None]
    first_input, first_gain, first_shift = norm_back(
        at_now(first_back), first_centred, first_scale, gains[0]
    )
    tokens_grad = middle_grad + first_input
    small = jnp.stack(
        [
            first_gain,
            second_gain,
            first_shift,
            second_shift,
            jnp.sum(query_sum, axis=(0, 1)),
            jnp.sum(value_sum, axis=(0, 1)),
            jnp.sum(branch_grad.astype(f32), axis=0),
            jnp.sum(cot_float, axis=0),
        ]
    )
    small = jnp.concatenate([small, thresholds_part.reshape(-1, width)], axis=0)
    def small_step(bit):
        return small + swap(at_now(small), "row", bit) if bit < rows else small

    put(small)
    tick()

    mixing_sum.add()
    mixing_sum.move()
    out_part = columns_part([at_now(active)], full_contract, ids_contract, out_got, "contract")
    small = small_step(2)
    put(out_part, small)
    tick()

    mixing_sum.add()
    mixing_sum.move()
    out_across = swap(at_now(out_part), "col", 2)
    out_base = columns_base([active], full_contract, ids_contract, out_got, "contract")
    layer_out = (middle + (out_base + out_across.astype(f32) + biases[3])).astype(bf16)
    small = small_step(4)
    put(small, projection_grad, out_base)
    tick()

    mixing_sum.add()
    mixing_sum.move()
    bit = 8
    while bit < rows:
        small = small_step(bit)
        put(small)
        tick()
        bit *= 2
    small = small_step(1)
    put(small)
    tick()
    mixing_sum.add()
    contract_grad, expand_grad = contract_sum.result, expand_sum.result
    mixing_grad = mixing_sum.result
    mixing_grad = jnp.stack(
        [mixing_grad[:, i * width : (i + 1) * width] for i in range(3)], axis=1
    )
    return (
        layer_out,
        tokens_grad,
        small[0:2],
        small[2:4],
        small[4:8],
        mixing_grad,
        projection_grad,
        expand_grad,
        small[8:].reshape(thresholds.shape),
        contract_grad,
    )


def solution(mesh):
    return jax.shard_map(
        on_device,
        mesh=mesh,
        in_specs=(
            P("row", "col"),
            P("row", None),
            P(None, "col"),
            P(None, "col"),
            P(None, "col"),
            P("row", None, "col"),
            P("row", "col"),
            P("row", "col"),
            P("col"),
            P("row", "col"),
            P("row", "col"),
        ),
        out_specs=(
            P("row", "col"),
            P("row", "col"),
            P(None, "col"),
            P(None, "col"),
            P(None, "col"),
            P("row", None, "col"),
            P("row", "col"),
            P("row", "col"),
            P("col"),
            P("row", "col"),
        ),
        check_vma=False,
    )
```

```python
import math
from functools import partial

import jax
import jax.numpy as jnp
from jax import lax
from jax.experimental import pallas as pl
from jax.experimental.pallas import tpu as pltpu
from jax.sharding import PartitionSpec as P

HD = 64
BLOCK = 256

norm_eps = 1e-05
sqrt_half = 0.7071067811865476
inverse_root = 0.3989422804014327
far = -1e33
NT = (((1,), (1,)), ((), ()))
TN = (((0,), (0,)), ((), ()))
VMEM_LIMIT = 26 << 20
CHEAP = 64
f32 = jnp.float32
bf16 = jnp.bfloat16


def pick_heads(pair):
    lane = lax.broadcasted_iota(jnp.int32, pair.shape, 1)
    zero = jnp.zeros_like(pair)
    return jnp.concatenate(
        [jnp.where(lane < HD, pair, zero), jnp.where(lane < HD, zero, pair)], axis=0
    )


def attend_kernel(
    slope_ref, start_ref, q_ref, k_ref, v_ref, out_ref, log_ref, dist_ref, *, rows, scale
):
    pair = pl.program_id(1)
    length = k_ref.shape[0]

    @pl.when(pair == 0)
    def _():
        for r0 in range(0, length, rows):
            shape = (rows, r0 + rows)
            i = lax.broadcasted_iota(jnp.int32, shape, 0) + r0
            j = lax.broadcasted_iota(jnp.int32, shape, 1)
            allowed = (j <= i) & (j >= start_ref[0, r0 : r0 + rows, :])
            dist_ref[r0 : r0 + rows, 0 : r0 + rows] = jnp.where(allowed, (j - i).astype(f32), far)

    slope_a, slope_b = slope_ref[2 * pair] * scale, slope_ref[2 * pair + 1] * scale
    for r0 in range(0, length, rows):
        r1 = r0 + rows
        q = pick_heads(q_ref[r0:r1, :] * jnp.asarray(scale, bf16))
        s = lax.dot_general(q, k_ref[0:r1, :], NT, preferred_element_type=f32)
        d = dist_ref[r0:r1, 0:r1]
        s = jnp.concatenate([s[:rows] + d * slope_a, s[rows:] + d * slope_b], axis=0)
        row_max = jnp.max(s, axis=1, keepdims=True)
        weights = jnp.exp(s - row_max)
        row_total = jnp.sum(weights, axis=1, keepdims=True)
        probs = (weights * (1.0 / row_total)).astype(bf16)
        o = jnp.dot(probs, v_ref[0:r1, :], preferred_element_type=f32)
        lane = lax.broadcasted_iota(jnp.int32, (rows, 2 * HD), 1)
        out_ref[r0:r1, :] = jnp.where(lane < HD, o[:rows], o[rows:]).astype(bf16)
        logs = row_max + jnp.log(row_total)
        logs = jnp.where(
            lane < HD,
            jnp.broadcast_to(logs[:rows], (rows, 2 * HD)),
            jnp.broadcast_to(logs[rows:], (rows, 2 * HD)),
        ).T
        log_ref[0, 0:1, r0:r1] = logs[0:1]
        log_ref[0, 1:2, r0:r1] = logs[HD : HD + 1]


def attend_forward(mixed, starts, slopes, seqs, rows=256):
    length, pairs = mixed.shape[0] // seqs, mixed.shape[1] // (6 * HD)

    def part(i):
        return pl.BlockSpec((length, 2 * HD), lambda s, p, *_: (s, i * pairs + p))

    return pl.pallas_call(
        partial(attend_kernel, rows=rows, scale=HD**-0.5),
        grid_spec=pltpu.PrefetchScalarGridSpec(
            num_scalar_prefetch=1,
            grid=(seqs, pairs),
            in_specs=[
                pl.BlockSpec((1, length, 1), lambda s, p, *_: (s, 0, 0)),
                part(0),
                part(1),
                part(2),
            ],
            out_specs=[part(0), pl.BlockSpec((1, 2, length), lambda s, p, *_: (s * pairs + p, 0, 0))],
            scratch_shapes=[pltpu.VMEM((length, length), f32)],
        ),
        out_shape=[
            jax.ShapeDtypeStruct((mixed.shape[0], 2 * HD * pairs), bf16),
            jax.ShapeDtypeStruct((seqs * pairs, 2, length), f32),
        ],
        compiler_params=pltpu.CompilerParams(vmem_limit_bytes=VMEM_LIMIT),
        cost_estimate=pl.CostEstimate(
            flops=16 * seqs * pairs * length * length * HD // CHEAP,
            bytes_accessed=4 * mixed.size // CHEAP,
            transcendentals=seqs * pairs * length * length // CHEAP,
        ),
        name="attend_forward",
    )(slopes, starts, mixed, mixed, mixed)


def attend_back_kernel(
    slope_ref,
    start_ref,
    log_ref,
    q_ref,
    k_ref,
    v_ref,
    g_ref,
    dq_ref,
    dk_ref,
    dv_ref,
    qs_ref,
    vs_ref,
    dist_ref,
    ka_ref,
    va_ref,
    *,
    rows,
    scale,
):
    pair = pl.program_id(1)
    length = k_ref.shape[0]

    @pl.when(pair == 0)
    def _():
        for r0 in range(0, length, rows):
            shape = (r0 + rows, rows)
            i = lax.broadcasted_iota(jnp.int32, shape, 1) + r0
            j = lax.broadcasted_iota(jnp.int32, shape, 0)
            allowed = (j <= i) & (j >= start_ref[0, :, r0 : r0 + rows])
            dist_ref[0 : r0 + rows, r0 : r0 + rows] = jnp.where(allowed, (j - i).astype(f32), far)

    slope_a, slope_b = slope_ref[2 * pair] * scale, slope_ref[2 * pair + 1] * scale
    query_sum = jnp.zeros((1, 2 * HD), f32)
    for r0 in reversed(range(0, length, rows)):
        r1 = r0 + rows
        q = pick_heads(q_ref[r0:r1, :] * jnp.asarray(scale, bf16))
        g = pick_heads(g_ref[r0:r1, :])
        k, v = k_ref[0:r1, :], v_ref[0:r1, :]
        s = lax.dot_general(k, q, NT, preferred_element_type=f32)
        d = dist_ref[0:r1, r0:r1]
        logs = jnp.concatenate([log_ref[0, 0:1, r0:r1], log_ref[0, 1:2, r0:r1]], axis=1)
        s = jnp.concatenate([s[:, :rows] + d * slope_a, s[:, rows:] + d * slope_b], axis=1)
        probs = jnp.exp(s - logs)
        t = lax.dot_general(v, g, NT, preferred_element_type=f32)
        centre = jnp.sum(probs * t, axis=0, keepdims=True)
        score_grad = (probs * (t - centre)).astype(bf16)
        value_part = jnp.dot(probs.astype(bf16), g, preferred_element_type=f32)
        key_part = jnp.dot(score_grad, q, preferred_element_type=f32)
        if r1 == length:
            va_ref[...] = value_part
            ka_ref[...] = key_part
        else:
            va_ref[0:r1, :] += value_part
            ka_ref[0:r1, :] += key_part
        dq = lax.dot_general(score_grad, k, TN, preferred_element_type=f32)
        lane = lax.broadcasted_iota(jnp.int32, (rows, 2 * HD), 1)
        dq = (jnp.where(lane < HD, dq[:rows], dq[rows:]) * scale).astype(bf16)
        dq_ref[r0:r1, :] = dq
        query_sum = query_sum + jnp.sum(dq.astype(f32), axis=0, keepdims=True)
    qs_ref[0] = query_sum
    dk_ref[...] = ka_ref[...].astype(bf16)
    dv = va_ref[...].astype(bf16)
    dv_ref[...] = dv
    vs_ref[0] = jnp.sum(dv.astype(f32), axis=0, keepdims=True)


def attend_backward(mixed, grads, starts, logs, slopes, seqs, rows=256):
    length, pairs = mixed.shape[0] // seqs, mixed.shape[1] // (6 * HD)

    def part(i):
        return pl.BlockSpec((length, 2 * HD), lambda s, p, *_: (s, i * pairs + p))

    out = jax.ShapeDtypeStruct(grads.shape, bf16)
    sums = jax.ShapeDtypeStruct((seqs, 1, grads.shape[1]), f32)
    sum_spec = pl.BlockSpec((1, 1, 2 * HD), lambda s, p, *_: (s, 0, p))
    return pl.pallas_call(
        partial(attend_back_kernel, rows=rows, scale=HD**-0.5),
        grid_spec=pltpu.PrefetchScalarGridSpec(
            num_scalar_prefetch=1,
            grid=(seqs, pairs),
            in_specs=[
                pl.BlockSpec((1, 1, length), lambda s, p, *_: (s, 0, 0)),
                pl.BlockSpec((1, 2, length), lambda s, p, *_: (s * pairs + p, 0, 0)),
                part(0),
                part(1),
                part(2),
                part(0),
            ],
            out_specs=[part(0), part(0), part(0), sum_spec, sum_spec],
            scratch_shapes=[
                pltpu.VMEM((length, length), f32),
                pltpu.VMEM((length, 2 * HD), f32),
                pltpu.VMEM((length, 2 * HD), f32),
            ],
        ),
        out_shape=[out, out, out, sums, sums],
        compiler_params=pltpu.CompilerParams(vmem_limit_bytes=VMEM_LIMIT),
        cost_estimate=pl.CostEstimate(
            flops=40 * seqs * pairs * length * length * HD // CHEAP,
            bytes_accessed=14 * grads.size // CHEAP,
            transcendentals=seqs * pairs * length * length // CHEAP,
        ),
        name="attend_backward",
    )(slopes, starts, logs, mixed, mixed, mixed, grads)


def resident(shape):
    return pl.BlockSpec(shape, lambda *_: (0,) * len(shape), pipeline_mode=pl.Buffered(1))


def kept_out(shape):
    return pl.BlockSpec(shape, lambda *_: (0,) * len(shape))


def flat_rows(ws):
    return jnp.concatenate([w[...] for w in ws], axis=0)


def matmul_call(kernel, grid, ins, outs, scratch, flops, name, prefetch=()):
    moved = sum(a.size * a.dtype.itemsize for a, _ in ins)
    moved += sum(jnp.dtype(t).itemsize * math.prod(s) for s, t, _ in outs)
    return pl.pallas_call(
        kernel,
        grid_spec=pltpu.PrefetchScalarGridSpec(
            num_scalar_prefetch=len(prefetch),
            grid=grid,
            in_specs=[s for _, s in ins],
            out_specs=[s for _, _, s in outs],
            scratch_shapes=scratch,
        ),
        out_shape=[jax.ShapeDtypeStruct(s, t) for s, t, _ in outs],
        compiler_params=pltpu.CompilerParams(vmem_limit_bytes=VMEM_LIMIT),
        cost_estimate=pl.CostEstimate(
            flops=flops // CHEAP, bytes_accessed=moved // CHEAP, transcendentals=0
        ),
        name=name,
    )(*prefetch, *[a for a, _ in ins])


def times_rows(x, ws, extras, outs, finish, name, tn, window=None, joins=()):
    tokens, depth = x.shape
    first, width = window or (0, ws[0].shape[1])
    first, tiles = first // tn, width // tn
    n_ws, n_ex, n_out = len(ws), len(extras), len(outs)
    steps = ws[0].shape[1] // tn if joins else tiles

    def kernel(*refs):
        x_ref, w_refs = refs[0], refs[1 : 1 + n_ws]
        extra, out = refs[1 + n_ws : 1 + n_ws + n_ex], refs[1 + n_ws + n_ex :]
        for places, joined in zip(joins, out[n_out:]):
            at = 0
            for i in places:
                joined[at : at + ws[i].shape[0], :] = w_refs[i][...]
                at += ws[i].shape[0]

        def multiply():
            acc = jnp.dot(x_ref[...], flat_rows(w_refs), preferred_element_type=f32)
            finish(acc, extra, out[:n_out])

        if steps == tiles:
            multiply()
        else:
            pl.when(pl.program_id(0) < tiles)(multiply)

    def spec(rows):
        return pl.BlockSpec((rows, tn), lambda n: (0, jnp.minimum(n, tiles - 1)))

    def tile(rows):
        return pl.BlockSpec((rows, tn), lambda n: (0, n + first))

    ins = [(x, resident(x.shape))] + [(w, tile(w.shape[0])) for w in ws]
    ins += [(e, spec(e.shape[0])) for e in extras]
    results = [(s, t, spec(s[0])) for s, t in outs]
    for places in joins:
        rows = sum(ws[i].shape[0] for i in places)
        results.append(((rows, ws[0].shape[1]), bf16, tile(rows)))
    return matmul_call(kernel, (steps,), ins, results, [], 2 * tokens * depth * width, name)


def times_columns(xs, ws, order, side, dtype, name, first=0, added=(), block=0, chunks=None):
    tokens = xs[0].shape[0]
    count = order.shape[1]
    n_xs = len(xs)
    width = sum(x.shape[1] for x in xs)
    chunks = chunks or [tokens]

    def kernel(order_ref, side_ref, *refs):
        x_refs, w_refs = refs[:n_xs], refs[n_xs : n_xs + 2]
        added_refs, out_refs = refs[n_xs + 2 : n_xs + 2 + len(added)], refs[-len(chunks) :]
        x = jnp.concatenate([r[...] for r in x_refs], axis=1)
        for i, w_ref in enumerate(w_refs):
            acc = lax.dot_general(x, w_ref[...], NT, preferred_element_type=f32)
            place = side_ref[0] if i == 0 else 1 - side_ref[0]
            place = pl.ds(pl.multiple_of(place * BLOCK, BLOCK), BLOCK)
            if added:
                acc = acc + jnp.concatenate([r[:, place] for r in added_refs]).astype(f32)
            at = 0
            for out_ref, height in zip(out_refs, chunks):
                out_ref[:, place] = acc[at : at + height].astype(dtype)
                at += height

    def w_spec(i):
        return pl.BlockSpec((BLOCK, width), lambda n, order_ref, _: (order_ref[i, n], first // width))

    def pair(height, start):
        return pl.BlockSpec((height, 2 * BLOCK), lambda n, *_: (0, start + n))

    ins = [(x, resident(x.shape)) for x in xs]
    ins += [(w, w_spec(i)) for i, w in enumerate(ws)]
    ins += [(b, pair(b.shape[0], block)) for b in added]
    done = matmul_call(
        kernel,
        (count,),
        ins,
        [((height, 2 * BLOCK * count), dtype, pair(height, 0)) for height in chunks],
        [],
        4 * tokens * BLOCK * count * width,
        name,
        prefetch=(order, side),
    )
    return done if len(chunks) > 1 else done[0]


def weight_rows(a, order, gs, name, groups=None, dtype=bf16):
    tokens = a.shape[0]
    width = sum(g.shape[1] for g in gs)
    count = order.shape[0]
    n_gs = len(gs)

    def kernel(order_ref, a_ref, *refs):
        g_refs, out_refs = refs[:n_gs], refs[n_gs:]
        g = jnp.concatenate([r[...] for r in g_refs], axis=1)
        acc = lax.dot_general(a_ref[...], g, TN, preferred_element_type=f32).astype(dtype)
        if groups is None:
            out_refs[0][...] = acc
            return
        for out_ref, group in zip(out_refs, groups):
            for j, i in enumerate(group):

                @pl.when(pl.program_id(0) == i)
                def _(out_ref=out_ref, rows=slice(j * BLOCK, (j + 1) * BLOCK)):
                    out_ref[rows, :] = acc

    ins = [(a, pl.BlockSpec((tokens, BLOCK), lambda i, order_ref: (0, order_ref[i])))]
    ins += [(g, resident(g.shape)) for g in gs]
    if groups is None:
        outs = [((count * BLOCK, width), dtype, pl.BlockSpec((BLOCK, width), lambda i, *_: (i, 0)))]
    else:
        shapes = [(len(group) * BLOCK, width) for group in groups]
        outs = [(shape, dtype, kept_out(shape)) for shape in shapes]
    done = matmul_call(
        kernel, (count,), ins, outs, [], 2 * tokens * BLOCK * count * width, name, prefetch=(order,)
    )
    return done[0] if groups is None else done


def place_blocks(values, place_ref, out_ref):
    at = 0
    for value in values:
        for c0 in range(0, value.shape[1], BLOCK):
            place = pl.ds(pl.multiple_of(place_ref[at] * BLOCK, BLOCK), BLOCK)
            out_ref[:, place] = value[:, c0 : c0 + BLOCK]
            at += 1


def lay_out(parts, places, name, tm=256):
    tokens, width = parts[0].shape
    full = width * len(parts)

    def kernel(place_ref, *refs):
        place_blocks([r[...] for r in refs[:-1]], place_ref, refs[-1])

    return matmul_call(
        kernel,
        (tokens // tm,),
        [(p, pl.BlockSpec((tm, width), lambda m, *_: (m, 0))) for p in parts],
        [((tokens, full), bf16, pl.BlockSpec((tm, full), lambda m, *_: (m, 0)))],
        [],
        tokens * full,
        name,
        prefetch=(places,),
    )[0]


def normalize(parts, gain, shift, places, name, tm=256):
    tokens, width = parts[0].shape
    n = len(parts)
    full = width * n

    def kernel(place_ref, *refs):
        gain_ref, shift_ref, out_ref, mean_ref, scale_ref = refs[n:]
        rows = [r[...].astype(f32) for r in refs[:n]]
        mean = sum(jnp.sum(v, axis=1, keepdims=True) for v in rows) / full
        square = sum(jnp.sum(v * v, axis=1, keepdims=True) for v in rows) / full
        scale = lax.rsqrt(square - mean * mean + norm_eps)
        mean_ref[...] = mean
        scale_ref[...] = scale
        done = []
        for i, v in enumerate(rows):
            cols = slice(i * width, (i + 1) * width)
            done.append(((v - mean) * scale * gain_ref[:, cols] + shift_ref[:, cols]).astype(bf16))
        place_blocks(done, place_ref, out_ref)

    ins = [(p, pl.BlockSpec((tm, width), lambda m, *_: (m, 0))) for p in parts]
    ins += [(gain, resident(gain.shape)), (shift, resident(shift.shape))]
    column = pl.BlockSpec((tm, 1), lambda m, *_: (m, 0))
    return matmul_call(
        kernel,
        (tokens // tm,),
        ins,
        [
            ((tokens, full), bf16, pl.BlockSpec((tm, full), lambda m, *_: (m, 0))),
            ((tokens, 1), f32, column),
            ((tokens, 1), f32, column),
        ],
        [],
        8 * tokens * full,
        name,
        prefetch=(places,),
    )


def swap(x, axis, bit):
    return lax.ppermute(x, axis, [(i, i ^ bit) for i in range(lax.axis_size(axis))])


def turn(x, steps):
    count = lax.axis_size("row")
    return lax.ppermute(x, "row", [(i, (i + 2 * steps) % count) for i in range(count)])


def sum_col_stats(stats):
    stats = stats + swap(stats, "col", 1)
    return stats + swap(stats, "col", 2)


def sum_rows(x):
    bit = 1
    while bit < lax.axis_size("row"):
        x = x + swap(x, "row", bit)
        bit *= 2
    return x


def after(x, *first):
    return lax.optimization_barrier((x,) + first)[0] if first else x


def outer_groups():
    outer = lax.axis_size("row") // 2
    return [[2 * i + inner for i in range(outer)] for inner in range(2)]


def find(ids, wanted):
    at = jnp.arange(ids.shape[0])
    return jnp.sum(jnp.where(ids[None, :] == wanted[:, None], at[None, :], 0), axis=1).astype(
        jnp.int32
    )


def gather_whole(w):
    return [lax.all_gather(w, "row", axis=0, tiled=True)]


def gather_outer(w):
    return lax.all_gather(w, "row", axis=0, tiled=True, axis_index_groups=outer_groups())


class Clock:
    def __init__(self):
        self.now, self.new = [], []

    def at(self, x):
        return after(x, *self.now)

    def put(self, *xs):
        self.new += xs

    def tick(self):
        self.now, self.new = self.new, []


def on_device(
    tokens,
    segments,
    gains,
    shifts,
    biases,
    mixing,
    projection,
    expand,
    thresholds,
    contract,
    cotangent,
):
    seqs = segments.shape[0]
    rows, cols = lax.axis_size("row"), lax.axis_size("col")
    row, col = lax.axis_index("row"), lax.axis_index("col")
    tokens_here, width = tokens.shape
    full = width * cols
    heads = width // HD
    stepped = full // rows == BLOCK and rows == 2 * cols
    blocks, per_col = full // BLOCK, width // BLOCK
    at = jnp.arange(blocks)
    ours = per_col * ((at // per_col) ^ col) + at % per_col
    place, side = row // 2, row % 2
    steps = jnp.arange(max(rows // 2, 1))
    back = (place - steps) % (rows // 2)
    if stepped:
        ids_attend = ids_expand = jnp.concatenate([2 * back + side, 2 * back + 1 - side])
        ids_contract = jnp.stack([2 * steps + side, 2 * steps + 1 - side], axis=1).reshape(-1)
    else:
        ids_attend = ids_expand = ids_contract = at
        side = 0 * side
    sides = jnp.reshape(side, (1,)).astype(jnp.int32)
    away = jnp.array([1, 3, 0, 2]) ^ col
    clock = Clock()
    at_now, put, tick = clock.at, clock.put, clock.tick

    def columns_order(ids, ws):
        want = jnp.stack([2 * away + side, 2 * away + 1 - side]).reshape(-1)
        order = find(ids, want).reshape(2, -1)
        return order if len(ws) == 1 else order % (blocks // 2)

    def two(ws):
        return ws if len(ws) == 2 else [ws[0], ws[0]]

    def columns_sent(xs, ws, ids, name, first=0, whole=False):
        order = columns_order(ids, ws)[:, :2]
        xs = [at_now(xs[0])] + xs[1:]
        chunks = [3 * tokens_here // 8, 3 * tokens_here // 8, tokens_here // 4]
        if whole:
            chunks = [tokens_here]
        sent = times_columns(
            xs, two(ws), order, sides, bf16, name + "_sent", first, chunks=chunks
        )
        if whole:
            put(sent)
        return [swap(v, "col", 1) for v in ([sent] if whole else sent)]

    def columns_part(xs, ws, ids, got, name, first=0):
        order = columns_order(ids, ws)[:, 3:]
        return times_columns(xs, two(ws), order, sides, bf16, name + "_part", first, got, 1)

    def columns_base(xs, ws, ids, got, name, first=0):
        order = columns_order(ids, ws)[:, 2:3]
        xs = [at_now(xs[0])] + xs[1:]
        return times_columns(xs, two(ws), order, sides, f32, name + "_base", first, got, 0)

    class WeightSum:
        def __init__(self, a, ids, gs, name, groups=None):
            self.a, self.ids, self.gs, self.name = a, ids, gs, name
            self.left = rows // 2
            self.groups = groups or [[k] for k in reversed(range(self.left))]
            self.got, self.kept, self.carry, self.result = {}, [], None, None
            self.last = []

        def cut(self):
            if stepped:
                other = find(self.ids, 2 * back + 1 - side)
                self.sent = list(
                    weight_rows(at_now(self.a), other, self.gs, self.name + "_other", self.groups)
                )
            else:
                self.sent = [
                    weight_rows(at_now(self.a), find(self.ids, at), self.gs, self.name, dtype=f32)
                ]
            put(*self.sent)

        def keep(self, *first):
            if stepped:
                mine = find(self.ids, 2 * back + side)
                a = after(at_now(self.a), *first)
                single = [[k] for k in range(rows // 2)]
                self.kept = weight_rows(a, mine, self.gs, self.name + "_mine", single)
                put(*self.kept)

        def move(self, *first, late=False):
            if stepped:
                if not self.groups:
                    return
                group = self.groups.pop(0)
                got = swap(after(at_now(self.sent.pop(0)), *first), "row", 1)
                self.last = [got]
                if not late:
                    put(got)
                for j, k in enumerate(group):
                    self.got[k] = (got, j * BLOCK)

        def add(self, *first):
            if not stepped:
                if self.result is None:
                    self.result = lax.psum_scatter(
                        self.sent[0], "row", scatter_dimension=0, tiled=True
                    )
                return
            self.left -= 1
            got, start = self.got[self.left]
            got = after(at_now(got), *first)[start : start + BLOCK]
            total = self.kept[self.left].astype(f32) + got.astype(f32)
            if self.carry is not None:
                total = total + self.carry.astype(f32)
            if self.left == 0:
                self.result = total
            else:
                self.carry = turn(total.astype(bf16), -1)
                put(self.carry)

    head_ids = (col * heads + jnp.arange(heads)).astype(f32)
    slopes = jnp.exp2(-8.0 * (head_ids + 1.0) / (heads * cols))
    starts = jnp.sum(segments[:, None, :] < segments[:, :, None], axis=2).astype(jnp.int32)
    start_column, start_row = starts[:, :, None], starts[:, None, :]
    places_attend, places_expand = find(ids_attend, ours), find(ids_expand, ours)
    places_contract = find(ids_contract, ours)
    mix_width = 3 * width
    mixed_bias = jnp.concatenate([biases[0:1], jnp.zeros((1, width), f32), biases[1:2]], axis=1)

    attend_rows = jnp.concatenate([mixing.reshape(mixing.shape[0], -1), projection], axis=1)
    small = jnp.concatenate([gains, shifts], axis=0)
    put(attend_rows)
    tick()
    if stepped:
        own, near = [attend_rows], []
    else:
        whole = gather_whole(attend_rows)[0]
        own, near = [whole[: full // 2]], [whole[full // 2 :]]
        full_expand = gather_whole(expand)
        full_contract = gather_whole(contract)

    def weight_step(k):
        if stepped:
            ready = at_now(own[k])
            near.append(swap(ready, "row", 1))
            put(near[k])
            if k + 1 < rows // 2:
                own.append(turn(ready, 1))
                put(own[k + 1])

    weight_step(0)
    tokens_now = tokens
    token_parts = [tokens, swap(tokens_now, "col", 1), swap(tokens_now, "col", 2)]
    put(*token_parts[1:])
    tick()

    weight_step(1)
    cot_now = at_now(cotangent)
    cot_parts = [cotangent, swap(cot_now, "col", 1), swap(cot_now, "col", 2)]
    token_parts.append(swap(at_now(token_parts[2]), "col", 1))
    put(*cot_parts[1:], token_parts[3])
    tick()

    weight_step(2)
    small_now = at_now(small)
    norms = [small, swap(small_now, "col", 1), swap(small_now, "col", 2)]
    cot_parts.append(swap(at_now(cot_parts[2]), "col", 1))
    put(*norms[1:], cot_parts[3], start_column)
    tick()

    weight_step(3)
    norms.append(swap(at_now(norms[2]), "col", 1))
    norms = jnp.concatenate(norms, axis=1)
    first_full, first_mean, first_scale = normalize(
        token_parts, norms[0:1], norms[2:3], places_attend, "first_norm"
    )
    cot_full = lay_out([at_now(cot_parts[0])] + cot_parts[1:], places_contract, "cotangent_rows")
    put(first_full, cot_full)
    expand_own, expand_near = [expand], []

    def expand_turn(*first):
        if stepped:
            expand_own.append(turn(after(at_now(expand_own[-1]), *first), 1))
            put(expand_own[-1])

    def expand_step(k):
        if stepped:
            expand_near.append(swap(at_now(expand_own[k]), "row", 1))
            put(expand_near[k])

    expand_turn()
    tick()

    def add_bias(acc, extra, out):
        out[0][...] = (acc + extra[0][...]).astype(bf16)

    expand_step(0)
    if stepped:
        contract_pair = jnp.concatenate([contract, swap(at_now(contract), "row", 1)], axis=0)
        put(contract_pair)
    expand_turn()
    mixed, *full_attend = times_rows(
        at_now(first_full),
        own + near,
        [mixed_bias],
        [((tokens_here, mix_width), bf16)],
        add_bias,
        "mix",
        tn=width,
        window=(0, mix_width),
        joins=[range(len(own)), range(len(own), len(own) + len(near))],
    )
    expand_turn(mixed)
    attended, logs = attend_forward(mixed, start_column, slopes, seqs)
    put(attended)
    tick()

    if stepped:
        full_contract = [gather_outer(at_now(contract_pair))]
    expand_step(1)
    got = columns_sent([attended], full_attend, ids_attend, "project", mix_width)
    part = columns_part([attended], full_attend, ids_attend, got, "project", mix_width)
    put(part)
    tick()

    expand_step(2)
    across = swap(at_now(part), "col", 2)
    base = columns_base([attended], full_attend, ids_attend, got, "project", mix_width)
    resid = tokens.astype(f32)
    middle = resid + (base + across.astype(f32) + biases[2])
    middle_low = middle.astype(bf16)
    first_mean, first_scale = first_mean[:, 0], first_scale[:, 0]
    put(middle_low, first_mean, first_scale)
    tick()

    expand_step(3)
    middle_now = at_now(middle_low)
    middle_parts = [middle_low, swap(middle_now, "col", 1), swap(middle_now, "col", 2)]
    put(*middle_parts[1:])
    tick()

    middle_parts.append(swap(at_now(middle_parts[2]), "col", 1))
    second_full, second_mean, second_scale = normalize(
        middle_parts, norms[1:2], norms[3:4], places_expand, "second_norm"
    )
    put(second_full)
    tick()

    def activate(acc, extra, out):
        hidden = acc + extra[0][...]
        bell = 0.5 * (1.0 + lax.erf(hidden * sqrt_half))
        out[0][...] = (hidden * bell).astype(bf16)
        out[1][...] = bell + hidden * (jnp.exp(-0.5 * hidden * hidden) * inverse_root)

    hidden_shape = (tokens_here, expand.shape[1])
    active, slope, *joined = times_rows(
        at_now(second_full),
        expand_own + expand_near if stepped else full_expand,
        [thresholds[None]],
        [(hidden_shape, bf16), (hidden_shape, f32)],
        activate,
        "expand",
        tn=512,
        joins=[range(len(expand_own)), range(len(expand_own), 2 * len(expand_own))] if stepped else [],
    )
    if stepped:
        full_expand = joined
    contract_sum = WeightSum(
        cot_full, ids_contract, [active], "contract_grad", [[3], [2, 1], [0]]
    )
    contract_sum.cut()
    put(active)
    tick()

    def back_activate(acc, extra, out):
        grad = (acc * extra[0][...]).astype(bf16)
        out[0][...] = grad
        out[1][...] = jnp.sum(grad.astype(f32), axis=0, keepdims=True)

    second_mean, second_scale = at_now(second_mean)[:, 0], at_now(second_scale)[:, 0]
    put(second_mean, second_scale)
    contract_sum.move()
    contract_sum.keep()
    tick()

    contract_sum.add()
    contract_sum.move()
    hidden_grad, thresholds_part = times_rows(
        at_now(cot_full),
        full_contract,
        [slope],
        [(hidden_shape, bf16), ((1, hidden_shape[1]), f32)],
        back_activate,
        "contract_back",
        tn=512,
    )
    got = columns_sent([hidden_grad], full_expand, ids_expand, "expand_back")
    part = columns_part([hidden_grad], full_expand, ids_expand, got, "expand_back")
    across = swap(part, "col", 2)
    put(part)
    tick()

    contract_sum.add()
    contract_sum.move()
    base = columns_base([hidden_grad], full_expand, ids_expand, got, "expand_back")
    expand_sum = WeightSum(second_full, ids_expand, [hidden_grad], "expand_grad", [[3], [2, 1], [0]])
    expand_sum.cut()
    second_back = base + across.astype(f32)
    put(second_back)
    tick()

    def norm_back(upstream, centred, scale, gain):
        scaled = upstream * gain
        sums = sum_col_stats(
            jnp.stack([jnp.sum(scaled, axis=1), jnp.sum(scaled * centred, axis=1)])
        )
        result = scale[:, None] * (
            scaled - sums[0][:, None] / full - centred * (sums[1][:, None] / full)
        )
        return result, jnp.sum(upstream * centred, axis=0), jnp.sum(upstream, axis=0)

    expand_sum.move()
    second_centred = (middle - second_mean[:, None]) * second_scale[:, None]
    second_input, second_gain, second_shift = norm_back(
        at_now(second_back), second_centred, second_scale, gains[1]
    )
    cot_float = cotangent.astype(f32)
    middle_grad = cot_float + second_input
    branch_grad = middle_grad.astype(bf16)
    branch_parts = [branch_grad, swap(branch_grad, "col", 1), swap(branch_grad, "col", 2)]
    contract_sum.add()
    expand_sum.keep(branch_grad)
    out_got = columns_sent(
        [after(active, branch_grad)], full_contract, ids_contract, "contract", whole=True
    )
    put(*branch_parts[1:])
    tick()

    def store(acc, extra, out):
        out[0][...] = acc.astype(bf16)

    contract_sum.add()
    expand_sum.move()
    expand_sum.add()
    branch_parts.append(swap(at_now(branch_parts[2]), "col", 1))
    branch_full = lay_out(branch_parts, places_attend, "branch_rows")
    (attended_grad,) = times_rows(
        branch_full,
        full_attend,
        [],
        [((tokens_here, width), bf16)],
        store,
        "project_back",
        tn=width,
        window=(mix_width, width),
    )
    if stepped:
        project_other = weight_rows(
            branch_full,
            find(ids_attend, 2 * steps + 1 - side),
            [attended],
            "projection_grad_other",
        )
        put(project_other)
    else:
        project_sum = WeightSum(branch_full, ids_attend, [attended], "projection_grad", None)
        project_sum.cut()
    query_back, key_back, value_back, query_sum, value_sum = attend_backward(
        mixed, attended_grad, start_row, logs, slopes, seqs
    )
    mixed_grads = [query_back, key_back, value_back]
    put(query_back)
    tick()

    expand_sum.move()
    if stepped:
        project_got = swap(at_now(project_other), "row", 1)
        put(project_got)
    expand_sum.add()
    got = columns_sent(mixed_grads, full_attend, ids_attend, "mix_back")
    mixing_sum = WeightSum(
        first_full, ids_attend, mixed_grads, "mixing_grad", [[3], [2], [1], [0]]
    )
    mixing_sum.cut()
    part = columns_part(mixed_grads, full_attend, ids_attend, got, "mix_back")
    across = swap(part, "col", 2)
    expand_sum.add()
    base = columns_base(mixed_grads, full_attend, ids_attend, got, "mix_back")
    if stepped:
        project_mine = weight_rows(
            after(branch_full, part),
            find(ids_attend, 2 * steps + side),
            [attended],
            "projection_grad_mine",
        )
        put(project_mine)
    first_back = base + across.astype(f32)
    put(first_back)
    tick()

    if stepped:
        total = at_now(project_mine).astype(f32) + project_got.astype(f32)
        projection_grad = lax.psum_scatter(
            total.astype(bf16),
            "row",
            scatter_dimension=0,
            tiled=True,
            axis_index_groups=outer_groups(),
        ).astype(f32)
    else:
        project_sum.add()
        projection_grad = project_sum.result
    expand_sum.add()
    mixing_sum.move()
    mixing_sum.keep()
    first_centred = (resid - first_mean[:, None]) * first_scale[:, None]
    first_input, first_gain, first_shift = norm_back(
        at_now(first_back), first_centred, first_scale, gains[0]
    )
    tokens_grad = middle_grad + first_input
    small = jnp.stack(
        [
            first_gain,
            second_gain,
            first_shift,
            second_shift,
            jnp.sum(query_sum, axis=(0, 1)),
            jnp.sum(value_sum, axis=(0, 1)),
            jnp.sum(branch_grad.astype(f32), axis=0),
            jnp.sum(cot_float, axis=0),
        ]
    )
    small = jnp.concatenate([small, thresholds_part.reshape(-1, width)], axis=0)
    def small_step(bit):
        return small + swap(at_now(small), "row", bit) if bit < rows else small

    put(small)
    tick()

    mixing_sum.add()
    mixing_sum.move()
    out_part = columns_part([at_now(active)], full_contract, ids_contract, out_got, "contract")
    small = small_step(2)
    put(out_part, small)
    tick()

    mixing_sum.add()
    mixing_sum.move()
    out_across = swap(at_now(out_part), "col", 2)
    out_base = columns_base([active], full_contract, ids_contract, out_got, "contract")
    layer_out = (middle + (out_base + out_across.astype(f32) + biases[3])).astype(bf16)
    small = small_step(4)
    put(small, projection_grad, out_base)
    tick()

    mixing_sum.add()
    mixing_sum.move()
    bit = 8
    while bit < rows:
        small = small_step(bit)
        put(small)
        tick()
        bit *= 2
    small = small_step(1)
    put(small)
    tick()
    mixing_sum.add()
    contract_grad, expand_grad = contract_sum.result, expand_sum.result
    mixing_grad = mixing_sum.result
    mixing_grad = jnp.stack(
        [mixing_grad[:, i * width : (i + 1) * width] for i in range(3)], axis=1
    )
    return (
        layer_out,
        tokens_grad,
        small[0:2],
        small[2:4],
        small[4:8],
        mixing_grad,
        projection_grad,
        expand_grad,
        small[8:].reshape(thresholds.shape),
        contract_grad,
    )


def solution(mesh):
    return jax.shard_map(
        on_device,
        mesh=mesh,
        in_specs=(
            P("row", "col"),
            P("row", None),
            P(None, "col"),
            P(None, "col"),
            P(None, "col"),
            P("row", None, "col"),
            P("row", "col"),
            P("row", "col"),
            P("col"),
            P("row", "col"),
            P("row", "col"),
        ),
        out_specs=(
            P("row", "col"),
            P("row", "col"),
            P(None, "col"),
            P(None, "col"),
            P(None, "col"),
            P("row", None, "col"),
            P("row", "col"),
            P("row", "col"),
            P("col"),
            P("row", "col"),
        ),
        check_vma=False,
    )
```
